32 devices in a mesh: head: 2 (over x), blk: 16 (over z, y, core).
Axes of the slice: x: 2, y: 2, z: 4, core: 2. Of those that a mesh axis runs over, the one named last changes fastest.
Arguments:
- layer_input: bfloat16 [2, 2048, 768], P(None, ('head', 'blk')), may hold values from -12 to 12
- segment_ids: int32 [2, 2048], P(None, ('head', 'blk')), may hold values from 0 to 3, never falling along the last dimension, each value on 1 to 1024 neighbouring positions
- token_live: int32 [2, 2048], P(None, ('head', 'blk')), may hold values 0 or 1
- w_query: bfloat16 [768, 768], P(('head', 'blk')), may hold values from -0.21875 to 0.21875
- b_query: bfloat16 [768], P(('head', 'blk')), may hold values from -1.75 to 1.75
- w_key: bfloat16 [768, 768], P(('head', 'blk')), may hold values from -0.21875 to 0.21875
- w_value: bfloat16 [768, 768], P(('head', 'blk')), may hold values from -0.21875 to 0.21875
- b_value: bfloat16 [768], P(('head', 'blk')), may hold values from -0.625 to 0.625
- w_output: bfloat16 [768, 768], P(('head', 'blk')), may hold values from -0.875 to 0.875
- b_output: bfloat16 [768], P(('head', 'blk')), may hold values from -1.25 to 1.25
- first_gain: bfloat16 [768], P(('head', 'blk')), may hold values from 0.5 to 1.5
- first_shift: bfloat16 [768], P(('head', 'blk')), may hold values from -1.25 to 1.25
- w_gate: bfloat16 [768, 3072], P(('head', 'blk')), may hold values from -0.21875 to 0.21875
- w_up: bfloat16 [768, 3072], P(('head', 'blk')), may hold values from -0.21875 to 0.21875
- w_down: bfloat16 [3072, 768], P(('head', 'blk')), may hold values from -0.109375 to 0.109375
- b_down: bfloat16 [768], P(('head', 'blk')), may hold values from -1.25 to 1.25
- second_gain: bfloat16 [768], P(('head', 'blk')), may hold values from 0.5 to 1.5
- second_shift: bfloat16 [768], P(('head', 'blk')), may hold values from -1.25 to 1.25
- output_grad: bfloat16 [2, 2048, 768], P(None, ('head', 'blk')), may hold values from -12 to 12
Outputs:
- layer_output: bfloat16 [2, 2048, 768], P(None, ('head', 'blk'))
- input_grad: bfloat16 [2, 2048, 768], P(None, ('head', 'blk'))
- grad_query: float32 [768, 768], P(('head', 'blk'))
- grad_query_bias: float32 [768], P(('head', 'blk'))
- grad_key: float32 [768, 768], P(('head', 'blk'))
- grad_value: float32 [768, 768], P(('head', 'blk'))
- grad_value_bias: float32 [768], P(('head', 'blk'))
- grad_output: float32 [768, 768], P(('head', 'blk'))
- grad_output_bias: float32 [768], P(('head', 'blk'))
- grad_first_gain: float32 [768], P(('head', 'blk'))
- grad_first_shift: float32 [768], P(('head', 'blk'))
- grad_gate: float32 [768, 3072], P(('head', 'blk'))
- grad_up: float32 [768, 3072], P(('head', 'blk'))
- grad_down: float32 [3072, 768], P(('head', 'blk'))
- grad_down_bias: float32 [768], P(('head', 'blk'))
- grad_second_gain: float32 [768], P(('head', 'blk'))
- grad_second_shift: float32 [768], P(('head', 'blk'))
The draws below stay inside these ranges and needn't reach their ends.
Inputs may be any that keep to these rules, and one draw needn't show every extreme that they name: `segment_ids`: along each sequence the numbers never fall; each document covers 1 to 1024 tokens, and in each sequence one covers exactly 1024.
All inputs are finite; a program needn't handle non-finite values. No bound on the sum of `token_live` on one device may be relied on, other than what follows from the above.
Results may differ from the reference program's by a relative error of at most 0.039.
Values may be sent and summed in bfloat16 or wider, within the bound.
No kernel may reach another device: no remote copies, remote signals or barrier semaphores. Data moves between devices by JAX's collectives and lax.ppermute only.
A program may use at most 192 MiB of HBM per device.

```python
import math
import jax
import jax.numpy as jnp
import numpy as np
from jax import lax

D = 768
HEADS = 12
HEAD_DIM = 64
FF = 3072
SEQS = 2
SEQ_LEN = 2048
DOCS = 4
DOC_MOST = 1024


def place_ends(values, own_key, smallest, largest):
    longest = values.shape.index(max(values.shape))
    spots = []
    for shift in (0, 1):
        where = [jax.random.randint(jax.random.fold_in(own_key, axis), (), 0, length) for axis, length in enumerate(values.shape)]
        where[longest] = (where[longest] + shift) % values.shape[longest]
        spots.append(tuple(where))
    return values.at[spots[0]].set(smallest).at[spots[1]].set(largest)


def with_spikes(result, rng, source, target, blocks, factor):
    def block_of(dim):
        return (jnp.arange(result.shape[dim]) // (result.shape[dim] // blocks)).reshape((-1,) + (1,) * (result.ndim - 1 - dim))

    near = jax.random.permutation(rng, blocks)[block_of(target)]
    far = (block_of(target) + blocks // 2) % blocks
    return jnp.where((block_of(source) == near) | (block_of(source) == far), factor * result, result)


def level_of(rng, extent, pieces, least, high):
    level, own = 1.0, jax.random.fold_in(rng, 6)
    for position, shards_of in pieces:
        heights = jnp.exp(jax.random.uniform(jax.random.fold_in(own, position), (shards_of,), jnp.float32, least / len(pieces), high / len(pieces)))
        level = level * jnp.repeat(heights, extent[position] // shards_of).reshape([-1 if axis == position else 1 for axis in range(len(extent))])
    return level


def length_profile(amount, total, limit, slope):
    portions = [(1 << 20) // math.isqrt(rank ** slope) + 1 for rank in range(2, amount + 1)]
    rest, holding = total - limit - (amount - 1), [1] * (amount - 1)
    while rest > 0:
        candidates = [i for i in range(amount - 1) if holding[i] < limit]
        whole, budget = sum([portions[i] for i in candidates]), rest
        for i in candidates:
            more = min(limit - holding[i], max(1, budget * portions[i] // whole), rest)
            holding[i] = holding[i] + more
            rest = rest - more
    return np.array([limit] + holding)


def ragged_sizes(key, number_of, total, limit, lean):
    if number_of == 2:
        one = jax.random.randint(key, (), max(1, total - limit), min(limit, total - 1) + 1)
        return jnp.stack([one, total - one])
    lengths = jnp.asarray(length_profile(number_of, total, limit, lean), jnp.int32)
    couples = (number_of - 1) // 2
    giver, sink = lengths[1:1 + 2 * couples:2], lengths[2:2 + 2 * couples:2]
    room = jnp.minimum(giver - 1, limit - sink)
    shifted = jax.random.randint(jax.random.fold_in(key, 1), (couples,), 0, 1 << 20) % (room + 1)
    lengths = lengths.at[1:1 + 2 * couples:2].set(giver - shifted).at[2:2 + 2 * couples:2].set(sink + shifted)
    return lengths[jax.random.permutation(jax.random.fold_in(key, 2), number_of)]


def gaussian(key, extent, deviation, limit, shards=(), kind=jnp.bfloat16):
    drawn = deviation * jax.random.normal(key, extent, jnp.float32)
    if shards:
        drawn = drawn * level_of(key, extent, shards, -0.22, 0.18)
    return jnp.clip(drawn, -limit, limit).astype(kind)


def gaussian_with(own_key, extent, width, most, split, heavy, held_as=jnp.bfloat16):
    result = width * jax.random.normal(own_key, extent, jnp.float32)
    if split:
        result = result * level_of(own_key, extent, split, -0.22, 0.18)
    return jnp.clip(with_spikes(result, jax.random.fold_in(own_key, 3), *heavy), -most, most).astype(held_as)


def setup_inputs(seed: int = 0) -> dict:
    key_of = jax.random.split(jax.random.key(seed), 20)
    layer_input = gaussian_with(key_of[0], (SEQS, SEQ_LEN, D), 1.0, 12.0, ((1, 32),), (1, 2, 32, 2.75))
    segment_ids = jax.vmap(lambda own: jnp.searchsorted(jnp.cumsum(ragged_sizes(own, DOCS, SEQ_LEN, DOC_MOST, 2)), jnp.arange(SEQ_LEN), side="right"))(jax.random.split(key_of[1], SEQS)).reshape((SEQS, SEQ_LEN)).astype(jnp.int32)
    token_live = place_ends((jax.random.randint(key_of[2], (SEQS, SEQ_LEN), 0, 8) < 7).astype(jnp.int32), jax.random.fold_in(key_of[2], 1), 0, 1)
    w_query = gaussian(key_of[3], (D, D), D ** -0.5, 0.21875, ((0, 32),))
    b_query = gaussian(key_of[4], (D,), 0.3, 1.75, ((0, 32),))
    w_key = gaussian(key_of[5], (D, D), D ** -0.5, 0.21875, ((0, 32),))
    w_value = gaussian(key_of[6], (D, D), D ** -0.5, 0.21875, ((0, 32),))
    b_value = gaussian(key_of[7], (D,), 0.1, 0.625, ((0, 32),))
    w_output = gaussian(key_of[8], (D, D), (D // 16) ** -0.5, 0.875, ((0, 32),))
    b_output = gaussian(key_of[9], (D,), 0.2, 1.25, ((0, 32),))
    first_gain = jnp.clip(1.0 + 0.1 * jax.random.normal(key_of[10], (D,), jnp.float32), 0.5, 1.5).astype(jnp.bfloat16)
    first_shift = gaussian(key_of[11], (D,), 0.2, 1.25, ((0, 32),))
    w_gate = gaussian(key_of[12], (D, FF), D ** -0.5, 0.21875, ((0, 32),))
    w_up = gaussian(key_of[13], (D, FF), D ** -0.5, 0.21875, ((0, 32),))
    w_down = gaussian(key_of[14], (FF, D), FF ** -0.5, 0.109375, ((0, 32),))
    b_down = gaussian(key_of[15], (D,), 0.2, 1.25, ((0, 32),))
    second_gain = jnp.clip(1.0 + 0.1 * jax.random.normal(key_of[16], (D,), jnp.float32), 0.5, 1.5).astype(jnp.bfloat16)
    second_shift = gaussian(key_of[17], (D,), 0.2, 1.25, ((0, 32),))
    output_grad = gaussian_with(key_of[18], (SEQS, SEQ_LEN, D), 1.0, 12.0, ((1, 32),), (1, 2, 32, 2.75))
    return dict(layer_input=layer_input, segment_ids=segment_ids, token_live=token_live, w_query=w_query, b_query=b_query, w_key=w_key, w_value=w_value, b_value=b_value, w_output=w_output, b_output=b_output, first_gain=first_gain, first_shift=first_shift, w_gate=w_gate, w_up=w_up, w_down=w_down, b_down=b_down, second_gain=second_gain, second_shift=second_shift, output_grad=output_grad)


@jax.custom_vjp
def low(v):
    return lax.optimization_barrier(v.astype(jnp.bfloat16)).astype(jnp.float32)

@jax.custom_vjp
def low_back(v):
    return v

def low_keep(v):
    return (low(v), None)

def low_pass(kept, grad):
    return (grad,)

def back_keep(v):
    return (v, None)

def back_low(kept, grad):
    return (low(grad),)
low.defvjp(low_keep, low_pass)
low_back.defvjp(back_keep, back_low)
highest = lax.Precision.HIGHEST
norm_epsilon = 1e-12

def alibi_slopes(head_total):
    nearest = 2 ** int(math.floor(math.log2(head_total)))
    slopes = [2.0 ** (-8.0 * (head_index + 1) / nearest) for head_index in range(nearest)]
    if nearest < head_total:
        extra_slopes = [2.0 ** (-8.0 * (head_index + 1) / (2 * nearest)) for head_index in range(2 * nearest)]
        slopes = slopes + extra_slopes[0::2][:head_total - nearest]
    return np.array(slopes, dtype=np.float32)

def product(left_side, right_side):
    return jnp.dot(left_side, right_side, precision=highest, preferred_element_type=jnp.float32)

def layer_norm(values, norm_gain, norm_shift):
    centred = values - lax.optimization_barrier(jnp.mean(values, axis=-1, keepdims=True))
    scaled = centred * lax.rsqrt(lax.optimization_barrier(jnp.mean(centred * centred, axis=-1, keepdims=True)) + norm_epsilon)
    return scaled * norm_gain + norm_shift

def attend_block(query_block, segment_block, place_block, key_heads, value_heads, code_row, slopes):
    key_place = jnp.arange(key_heads.shape[1], dtype=jnp.int32)
    raw_scores = jnp.einsum('hqd,hkd->hqk', query_block, key_heads, precision=highest)
    distance = jnp.abs(place_block[:, None] - key_place[None, :]).astype(jnp.float32)
    scores = low_back(raw_scores * HEAD_DIM ** (-0.5) - slopes[:, None, None] * distance[None])
    allowed = (segment_block[:, None] == code_row[None, :]) | (place_block[:, None] == key_place[None, :])
    masked = jnp.where(allowed[None], scores, -jnp.inf)
    log_total = jax.nn.logsumexp(masked, axis=-1, keepdims=True)
    soft_probs = jnp.exp(masked - log_total)
    return jnp.einsum('hqk,hkd->hqd', low(soft_probs), value_heads, precision=highest)

def attend_sequence(query_row, key_row, value_row, segment_row, code_row, slopes):
    length_rows = query_row.shape[0]
    block_rows = math.gcd(length_rows, 512)
    block_total = length_rows // block_rows
    key_heads = jnp.transpose(key_row.reshape(length_rows, HEADS, HEAD_DIM), (1, 0, 2))
    value_heads = jnp.transpose(value_row.reshape(length_rows, HEADS, HEAD_DIM), (1, 0, 2))
    query_blocks = jnp.transpose(query_row.reshape(block_total, block_rows, HEADS, HEAD_DIM), (0, 2, 1, 3))
    segment_blocks = segment_row.reshape(block_total, block_rows)
    place_blocks = jnp.arange(length_rows, dtype=jnp.int32).reshape(block_total, block_rows)
    checked = jax.checkpoint(attend_block)
    blocks_out = lax.map(lambda packed: checked(packed[0], packed[1], packed[2], key_heads, value_heads, code_row, slopes), (query_blocks, segment_blocks, place_blocks))
    return jnp.transpose(blocks_out, (0, 2, 1, 3)).reshape(length_rows, HEADS * HEAD_DIM)

def forward(inputs, w_query, b_query, w_key, w_value, b_value, w_output, b_output, first_gain, first_shift, w_gate, w_up, w_down, b_down, second_gain, second_shift, segment_ids, codes):
    sequences, length_rows, model_width = inputs.shape
    tokens = inputs.reshape(sequences * length_rows, model_width)
    query_rows = low_back(low(product(tokens, w_query) + b_query)).reshape(inputs.shape)
    key_rows = low_back(low(product(tokens, w_key))).reshape(inputs.shape)
    value_rows = low_back(low(product(tokens, w_value) + b_value)).reshape(inputs.shape)
    slopes = jnp.asarray(alibi_slopes(HEADS))
    attended = lax.map(lambda packed: attend_sequence(packed[0], packed[1], packed[2], packed[3], packed[4], slopes), (query_rows, key_rows, value_rows, segment_ids, codes))
    attended = low_back(low(attended.reshape(sequences * length_rows, model_width)))
    branch = low_back(product(attended, w_output) + b_output)
    first_norm = layer_norm(tokens + branch, first_gain, first_shift)
    first_low = low(first_norm)
    gate_rows = low_back(product(first_low, w_gate))
    up_rows = low_back(product(first_low, w_up))
    hidden = low(jax.nn.gelu(gate_rows, approximate=False) * up_rows)
    mixed_rows = low_back(product(hidden, w_down) + b_down)
    return layer_norm(first_norm + mixed_rows, second_gain, second_shift).reshape(inputs.shape)

def reference(layer_input, segment_ids, token_live, w_query, b_query, w_key, w_value, b_value, w_output, b_output, first_gain, first_shift, w_gate, w_up, w_down, b_down, second_gain, second_shift, output_grad):
    float_inputs = [member.astype(jnp.float32) for member in (layer_input, w_query, b_query, w_key, w_value, b_value, w_output, b_output, first_gain, first_shift, w_gate, w_up, w_down, b_down, second_gain, second_shift)]
    codes = jnp.where(token_live == 1, segment_ids, -1).astype(jnp.int32)
    layer_wide, pullback = jax.vjp(lambda *parameters: forward(*parameters, segment_ids, codes), *float_inputs)
    gradients = pullback(output_grad.astype(jnp.float32))
    return (layer_wide.astype(jnp.bfloat16), gradients[0].astype(jnp.bfloat16), gradients[1].astype(jnp.float32), gradients[2].astype(jnp.float32), gradients[3].astype(jnp.float32), gradients[4].astype(jnp.float32), gradients[5].astype(jnp.float32), gradients[6].astype(jnp.float32), gradients[7].astype(jnp.float32), gradients[8].astype(jnp.float32), gradients[9].astype(jnp.float32), gradients[10].astype(jnp.float32), gradients[11].astype(jnp.float32), gradients[12].astype(jnp.float32), gradients[13].astype(jnp.float32), gradients[14].astype(jnp.float32), gradients[15].astype(jnp.float32))
```

```python
import functools
import math

import jax
import jax.numpy as jnp
import numpy as np
from jax import lax
from jax.experimental import pallas as pl
from jax.experimental.pallas import tpu as pltpu
from jax.sharding import Mesh
from jax.sharding import PartitionSpec as P

HEADS = 12
HEAD_DIM = 64
FEATS = 4
SLOTS = 4
PACK = 4 * HEAD_DIM
BLOCK = 256

norm_epsilon = 1e-12
masked_value = -1e30
f32 = jnp.float32
bf16 = jnp.bfloat16


def alibi_slopes(head_total):
    nearest = 2 ** int(math.floor(math.log2(head_total)))
    slopes = [2.0 ** (-8.0 * (index + 1) / nearest) for index in range(nearest)]
    extra = [2.0 ** (-8.0 * (index + 1) / (2 * nearest)) for index in range(2 * nearest)]
    slopes = slopes + extra[0::2][: head_total - nearest]
    return np.array(slopes, dtype=np.float32)


def dot(left, right, left_dim=1, right_dim=0):
    return lax.dot_general(
        left, right, (((left_dim,), (right_dim,)), ((), ())), preferred_element_type=f32
    )


def swap(values, axis, step=1):
    size = lax.axis_size(axis)
    return lax.ppermute(values, axis, [(i, i ^ step) for i in range(size)])


def in_order(parts, me):
    if len(parts) == 2:
        mine, other = parts
        return jnp.stack([jnp.where(me == 0, mine, other), jnp.where(me == 0, other, mine)])
    return jnp.take(jnp.stack(parts), jnp.arange(len(parts)) ^ me, axis=0)


def gather_axis(values, axis):
    size = lax.axis_size(axis)
    parts = [values] + [swap(values, axis, k) for k in range(1, size)]
    return in_order(parts, lax.axis_index(axis))


def scatter_axis(values, axis):
    size = lax.axis_size(axis)
    me = lax.axis_index(axis)

    def pick(k):
        if size == 2:
            return jnp.where((me ^ k) == 0, values[0], values[1])
        return lax.dynamic_index_in_dim(values, me ^ k, 0, keepdims=False)

    total = pick(0)
    for k in range(1, size):
        total = total + swap(pick(k).astype(bf16), axis, k).astype(f32)
    return total


def gather_feats(values):
    return [values] + [swap(values, "f", k) for k in range(1, FEATS)]


def scatter_feats(values):
    rows = values.shape[0] // FEATS
    total = values[:rows]
    for k in range(1, FEATS):
        total = total + swap(values[k * rows : (k + 1) * rows].astype(bf16), "f", k).astype(f32)
    return total


def all_to_all(values, axes):
    return lax.all_to_all(values, axes, split_axis=0, concat_axis=0, tiled=True)


def place(unit, side, feat, core, rows):
    return (((unit * 2 + side) * FEATS + feat) * 2 + core) * rows


def unpack_qkv(qkv_ref, q_s, k_s, v_s, feat):
    slots, feats, sides, rows, _ = qkv_ref.shape
    for slot in range(slots):
        for k in range(feats):
            for side in range(sides):
                start = pl.multiple_of(place(slot // 2, side, feat ^ k, slot % 2, rows), rows)
                here = pl.ds(start, rows)
                piece = qkv_ref[slot, k, side]
                q_s[here, :] = piece[:, :HEAD_DIM] * (HEAD_DIM**-0.5)
                k_s[here, :] = piece[:, HEAD_DIM : 2 * HEAD_DIM]
                v_s[here, :] = piece[:, 2 * HEAD_DIM : 3 * HEAD_DIM]


def spread_codes(code_ref, code_s):
    for start in range(0, code_ref.shape[1], 128):
        row = code_ref[:, start : start + 128]
        code_s[start : start + 128, :] = jnp.transpose(jnp.broadcast_to(row, (128, 128)))


def distance_tile():
    rows = lax.broadcasted_iota(jnp.int32, (BLOCK, BLOCK), 0)
    cols = lax.broadcasted_iota(jnp.int32, (BLOCK, BLOCK), 1)
    return (cols - rows).astype(f32)


def score_tile(q_part, k_part, code_part, seg_part, tile, offset, slope):
    distance = tile + offset
    scores = dot(k_part, q_part, 1, 1) - slope * jnp.abs(distance)
    codes = jnp.concatenate([code_part] * (BLOCK // 128), axis=1)
    allowed = (codes == seg_part) | (distance == 0.0)
    return scores, allowed


def attend_kernel(
    table_ref, slope_ref, qkv_ref, seg_ref, code_ref, out_ref, lse_ref, ot_ref,
    q_s, k_s, v_s, o_s, code_s,
):
    slope = slope_ref[0, 0]
    unpack_qkv(qkv_ref, q_s, k_s, v_s, table_ref[2, 0])
    spread_codes(code_ref, code_s)
    tile = distance_tile()
    units = qkv_ref.shape[0] // 2
    rows = qkv_ref.shape[3]
    if qkv_ref.shape[0] > SLOTS:
        o_s[...] = jnp.zeros_like(o_s)
        ot_ref[...] = jnp.zeros_like(ot_ref)
        lse_ref[...] = jnp.zeros_like(lse_ref)

    def query_step(i, carry):
        here = pl.ds(pl.multiple_of(i * BLOCK, BLOCK), BLOCK)
        q_part = q_s[here, :]
        seg_part = seg_ref[:, here]

        def key_step(j, state):
            top, total, mixed = state
            there = pl.ds(pl.multiple_of(j * BLOCK, BLOCK), BLOCK)
            offset = ((i - j) * BLOCK).astype(f32)
            scores, allowed = score_tile(
                q_part, k_s[there, :], code_s[there, :], seg_part, tile, offset, slope
            )
            scores = jnp.where(allowed, scores, masked_value)
            top_new = jnp.maximum(top, jnp.max(scores, axis=0, keepdims=True))
            probs = jnp.exp(scores - top_new)
            factor = jnp.exp(top - top_new)
            total = total * factor + jnp.sum(probs, axis=0, keepdims=True)
            mixed = mixed * factor + dot(v_s[there, :], probs.astype(bf16), 0, 0)
            return top_new, total, mixed

        top, total, mixed = lax.fori_loop(
            table_ref[0, i],
            table_ref[1, i],
            key_step,
            (
                jnp.full((1, BLOCK), masked_value, f32),
                jnp.zeros((1, BLOCK), f32),
                jnp.zeros((HEAD_DIM, BLOCK), f32),
            ),
        )
        mixed = mixed / total
        ot_ref[:, here] = mixed
        lse_ref[:, here] = top + jnp.log(total)
        o_s[here, :] = jnp.transpose(mixed)
        return carry

    lax.fori_loop(table_ref[2, 1], table_ref[2, 2], query_step, 0)
    for unit in range(units):
        for feat in range(FEATS):
            for core in range(2):
                starts = [place(unit, side, feat, core, rows) for side in range(2)]
                sides = [o_s[start : start + rows, :] for start in starts]
                out_ref[(unit * FEATS + feat) * 2 + core] = jnp.concatenate(sides, axis=1).astype(bf16)


def attend_back_kernel(
    table_ref, slope_ref, qkv_ref, dout_ref, ot_ref, lse_ref, seg_ref, code_ref, dqkv_ref,
    q_s, k_s, v_s, do_s, code_s, delta_s, dq_s, dk_s, dv_s,
):
    slope = slope_ref[0, 0]
    feat_self = table_ref[2, 0]
    first, last = table_ref[2, 1], table_ref[2, 2]
    slots, feats, sides, rows, _ = qkv_ref.shape
    unpack_qkv(qkv_ref, q_s, k_s, v_s, feat_self)
    spread_codes(code_ref, code_s)
    tile = distance_tile()
    for unit in range(slots // 2):
        for feat in range(FEATS):
            for core in range(2):
                piece = dout_ref[(unit * FEATS + feat) * 2 + core]
                for side in range(2):
                    start = place(unit, side, feat, core, rows)
                    do_s[start : start + rows, :] = piece[:, side * HEAD_DIM : (side + 1) * HEAD_DIM]
    dq_s[...] = jnp.zeros_like(dq_s)

    def delta_step(i, carry):
        here = pl.ds(pl.multiple_of(i * BLOCK, BLOCK), BLOCK)
        turned = jnp.transpose(do_s[here, :].astype(f32))
        delta_s[:, here] = jnp.sum(turned * ot_ref[:, here], axis=0, keepdims=True)
        return carry

    lax.fori_loop(first, last, delta_step, 0)

    def key_step(j, carry):
        there = pl.ds(pl.multiple_of(j * BLOCK, BLOCK), BLOCK)
        k_part, v_part, code_part = k_s[there, :], v_s[there, :], code_s[there, :]

        def query_step(i, state):
            dk, dv = state
            here = pl.ds(pl.multiple_of(i * BLOCK, BLOCK), BLOCK)
            q_part, do_part = q_s[here, :], do_s[here, :]
            offset = ((i - j) * BLOCK).astype(f32)
            scores, allowed = score_tile(
                q_part, k_part, code_part, seg_ref[:, here], tile, offset, slope
            )
            probs = jnp.exp(jnp.where(allowed, scores - lse_ref[:, here], masked_value))
            back_probs = dot(v_part, do_part, 1, 1)
            back_scores = (probs * (back_probs - delta_s[:, here])).astype(bf16)
            dv = dv + dot(probs.astype(bf16), do_part)
            dk = dk + dot(back_scores, q_part)
            dq_s[here, :] += dot(back_scores, k_part, 0, 0)
            return dk, dv

        zero = jnp.zeros((BLOCK, HEAD_DIM), f32)
        dk, dv = lax.fori_loop(
            jnp.maximum(table_ref[0, j], first),
            jnp.minimum(table_ref[1, j], last),
            query_step,
            (zero, zero),
        )
        dk_s[there, :] = dk
        dv_s[there, :] = dv
        return carry

    lax.fori_loop(0, q_s.shape[0] // BLOCK, key_step, 0)
    for slot in range(slots):
        for k in range(feats):
            for side in range(sides):
                start = pl.multiple_of(place(slot // 2, side, feat_self ^ k, slot % 2, rows), rows)
                here = pl.ds(start, rows)
                dqkv_ref[slot, k, side] = jnp.concatenate(
                    [
                        dq_s[here, :] * (HEAD_DIM**-0.5),
                        dk_s[here, :],
                        dv_s[here, :],
                        jnp.zeros((rows, HEAD_DIM), f32),
                    ],
                    axis=1,
                ).astype(bf16)


def attend(table, slope, qkv, seg_row, code_row):
    slots, feats, sides, rows, _ = qkv.shape
    length = slots * feats * sides * rows
    vmem = pl.BlockSpec(memory_space=pltpu.VMEM)
    smem = pl.BlockSpec(memory_space=pltpu.SMEM)
    return pl.pallas_call(
        attend_kernel,
        out_shape=(
            jax.ShapeDtypeStruct((slots * feats, rows, 2 * HEAD_DIM), bf16),
            jax.ShapeDtypeStruct((1, length), f32),
            jax.ShapeDtypeStruct((HEAD_DIM, length), f32),
        ),
        in_specs=[smem, smem, vmem, vmem, vmem],
        out_specs=(vmem, vmem, vmem),
        scratch_shapes=[pltpu.VMEM((length, HEAD_DIM), bf16)] * 3
        + [pltpu.VMEM((length, HEAD_DIM), f32), pltpu.VMEM((length, 128), f32)],
        name="attend",
    )(table, slope, qkv, seg_row, code_row)


def attend_back(table, slope, qkv, dout, o_turned, lse, seg_row, code_row):
    slots, feats, sides, rows, _ = qkv.shape
    length = slots * feats * sides * rows
    vmem = pl.BlockSpec(memory_space=pltpu.VMEM)
    smem = pl.BlockSpec(memory_space=pltpu.SMEM)
    return pl.pallas_call(
        attend_back_kernel,
        out_shape=jax.ShapeDtypeStruct(qkv.shape, bf16),
        in_specs=[smem, smem] + [vmem] * 6,
        out_specs=vmem,
        scratch_shapes=[pltpu.VMEM((length, HEAD_DIM), bf16)] * 4
        + [pltpu.VMEM((length, 128), f32), pltpu.VMEM((1, length), f32)]
        + [pltpu.VMEM((length, HEAD_DIM), f32)] * 3,
        name="attend_back",
    )(table, slope, qkv, dout, o_turned, lse, seg_row, code_row)


def norm_forward(values, gain, shift):
    centred = values - jnp.mean(values, axis=-1, keepdims=True)
    inverse = lax.rsqrt(jnp.mean(centred * centred, axis=-1, keepdims=True) + norm_epsilon)
    normed = centred * inverse
    return normed * gain + shift, normed, inverse


def norm_backward(upstream, normed, inverse, gain):
    scaled = upstream * gain
    adjusted = (
        scaled
        - jnp.mean(scaled, axis=-1, keepdims=True)
        - normed * jnp.mean(scaled * normed, axis=-1, keepdims=True)
    )
    return adjusted * inverse, jnp.sum(upstream * normed, axis=0), jnp.sum(upstream, axis=0)


def on_device(
    layer_input, segment_ids, token_live, w_query, b_query, w_key, w_value, b_value,
    w_output, b_output, first_gain, first_shift, w_gate, w_up, w_down, b_down,
    second_gain, second_shift, output_grad,
):
    units = lax.axis_size("u")
    unit, side, feat, core = (lax.axis_index(name) for name in ("u", "s", "f", "c"))
    devices = units * 2 * FEATS * 2
    sequences, rows, width = layer_input.shape
    length = rows * devices
    w_rows = w_query.shape[0]
    down_rows, ff_part = w_down.shape[0], w_gate.shape[1] // FEATS
    slots = units * 2
    heads = HEADS // FEATS
    head_width = heads * HEAD_DIM
    ranges = slots // SLOTS
    local = 2 * rows
    group = FEATS * local

    def exchange_sides(values):
        kept = jnp.where(side == 0, values[0], values[1])
        got = swap(jnp.where(side == 0, values[1], values[0]), "s")
        return kept, got

    def to_tokens(values):
        kept, got = exchange_sides(values)
        return jnp.concatenate(
            [jnp.where(side == 0, kept, got), jnp.where(side == 0, got, kept)], axis=0
        )

    def from_tokens(values):
        kept, got = exchange_sides(values.reshape(2, rows, width))
        return jnp.stack([jnp.where(side == 0, kept, got), jnp.where(side == 0, got, kept)])

    tokens = to_tokens(layer_input)
    token_parts = gather_feats(tokens)

    codes = jnp.where(token_live == 1, segment_ids, -1)
    vectors = jnp.stack(
        [b_query, b_value, b_output, first_gain, first_shift, b_down, second_gain, second_shift],
        axis=1,
    )
    seg_lanes = jnp.pad(
        jnp.concatenate([segment_ids, codes], axis=0).astype(bf16),
        ((0, w_rows - 2 * sequences), (0, HEAD_DIM - rows)),
    )
    vec_lanes = jnp.pad(vectors, ((0, 0), (0, HEAD_DIM - vectors.shape[1])))
    extra = jnp.stack([jnp.zeros_like(seg_lanes), seg_lanes, vec_lanes], axis=1)
    by_head = [w.reshape(w_rows, FEATS, heads, HEAD_DIM) for w in (w_query, w_key, w_value)]
    by_head.append(jnp.broadcast_to(extra[:, None], by_head[0].shape))
    half = heads * PACK // 2
    early = jnp.concatenate(by_head, axis=-1).reshape(w_rows, FEATS, 2, half)
    early = jnp.broadcast_to(
        early.transpose(1, 2, 0, 3)[None], (slots, FEATS, 2, w_rows, half)
    ).reshape(devices * w_rows, half)
    early_mine = all_to_all(early, ("u", "s", "f", "c"))
    early_other = swap(early_mine, "c")
    w_attn = jnp.concatenate(
        [
            jnp.where(core == 0, early_mine, early_other),
            jnp.where(core == 0, early_other, early_mine),
        ],
        axis=1,
    )

    gate_cols = w_gate.reshape(w_rows, slots, FEATS, 2 * down_rows).transpose(2, 0, 1, 3)
    up_cols = w_up.reshape(w_rows, slots, FEATS, 2 * down_rows).transpose(2, 0, 1, 3)
    late = jnp.concatenate(
        [
            jnp.broadcast_to(w_output[None], (FEATS, w_rows, width)),
            gate_cols.reshape(FEATS, w_rows, ff_part),
            up_cols.reshape(FEATS, w_rows, ff_part),
        ],
        axis=-1,
    )
    late_half = late.shape[-1] // 2
    late = late.reshape(FEATS, w_rows, 2, late_half).transpose(0, 2, 1, 3)
    late = all_to_all(late.reshape(FEATS * 2 * w_rows, late_half), ("f", "c"))
    late_rows = late.shape[0]
    late = jnp.concatenate([late, jnp.pad(w_down, ((0, 0), (0, late_half - width)))], axis=0)
    late = gather_axis(gather_axis(late, "s"), "u")
    late_other = swap(late, "c")
    late_zero = jnp.where(core == 0, late, late_other)
    late_one = jnp.where(core == 0, late_other, late)

    def upper(values):
        return values[:, :, :late_rows].reshape(width, late_half)

    late_zero_top, late_one_top = upper(late_zero), upper(late_one)
    full_output = late_zero_top[:, :width]
    full_gate = jnp.concatenate(
        [late_zero_top[:, width:], late_one_top[:, : ff_part - (late_half - width)]], axis=1
    )
    full_up = late_one_top[:, late_half - ff_part :]
    full_down = jnp.stack(
        [late_zero[:, :, late_rows:, :width], late_one[:, :, late_rows:, :width]], axis=2
    ).reshape(ff_part, width)

    vec_start = heads * PACK - HEAD_DIM
    params = w_attn[:, vec_start : vec_start + 8].astype(f32).T
    bias_output, gain_one, shift_one, bias_down, gain_two, shift_two = (
        params[index] for index in range(2, 8)
    )
    bias_parts = [
        lax.dynamic_slice_in_dim(params[index], feat * head_width, head_width).reshape(heads, 1, HEAD_DIM)
        for index in (0, 1)
    ]
    no_bias = jnp.zeros_like(bias_parts[0])
    attn_bias = jnp.concatenate([bias_parts[0], no_bias, bias_parts[1], no_bias], axis=1).reshape(
        heads * PACK
    )
    seg_start = 2 * PACK - HEAD_DIM
    seg_all = w_attn.reshape(devices, w_rows, heads * PACK)[
        :, : 2 * sequences, seg_start : seg_start + rows
    ]
    seg_all = seg_all.astype(f32).reshape(devices, 2, sequences, rows)
    seg_here = jnp.where(side == 0, seg_all[:, :, 0], seg_all[:, :, 1])
    seg_row = seg_here[:, 0].reshape(1, length)
    code_row = seg_here[:, 1].reshape(1, length)

    tokens_group = jnp.concatenate(token_parts, axis=0)
    projected = (dot(tokens_group, w_attn) + attn_bias).astype(bf16)
    pieces = [projected[:, h * PACK : (h + 1) * PACK] for h in range(heads)]
    sent = jnp.concatenate([pieces[min(slot % SLOTS, heads - 1)] for slot in range(slots)], axis=0)
    qkv = all_to_all(sent, ("u", "c")).reshape(slots, FEATS, 2, rows, PACK)

    blocks = length // BLOCK
    slot_self = unit * 2 + core
    range_self = slot_self // SLOTS
    head_self = feat * heads + jnp.minimum(slot_self % SLOTS, heads - 1)
    slope = jnp.asarray(alibi_slopes(HEADS))[head_self].reshape(1, 1)
    seg_blocks = seg_row.reshape(blocks, BLOCK)
    seg_low, seg_high = seg_blocks[:, 0], seg_blocks[:, -1]
    key_low = jnp.sum(seg_high[None, :] < seg_low[:, None], axis=1, dtype=jnp.int32)
    key_high = jnp.sum(seg_low[None, :] <= seg_high[:, None], axis=1, dtype=jnp.int32)
    own = jnp.stack(
        [feat, range_self * (blocks // ranges), (range_self + 1) * (blocks // ranges)]
    ).astype(jnp.int32)
    table = jnp.stack([key_low, key_high, jnp.pad(own, (0, blocks - 3))])
    out_blocks, lse, o_turned = attend(table, slope, qkv, seg_row, code_row)

    heads_in = all_to_all(out_blocks.reshape(-1, 2 * HEAD_DIM), ("u", "f", "c"))
    heads_in = heads_in.reshape(units, FEATS, 2, rows, 2, HEAD_DIM).transpose(4, 3, 1, 0, 2, 5)
    heads_in = heads_in.reshape(2, rows, FEATS, ranges, SLOTS, HEAD_DIM)
    my_range = (unit * 2) // SLOTS
    if ranges > 1:
        heads_in = lax.dynamic_index_in_dim(heads_in, my_range, 3, keepdims=False)
    else:
        heads_in = heads_in[:, :, :, 0]
    attended = heads_in[:, :, :, :heads].reshape(local, width)

    branch = dot(attended, full_output) + bias_output
    first_norm, normed_one, inverse_one = norm_forward(
        tokens.astype(f32) + branch, gain_one, shift_one
    )
    first_low = jnp.concatenate(gather_feats(first_norm.astype(bf16)), axis=0)
    gate_rows = dot(first_low, full_gate)
    up_rows = dot(first_low, full_up)
    spread = 0.5 * (1.0 + lax.erf(gate_rows * (0.5**0.5)))
    gelu = gate_rows * spread
    hidden = (gelu * up_rows).astype(bf16)
    mixed = scatter_feats(dot(hidden, full_down)) + bias_down
    layer_wide, normed_two, inverse_two = norm_forward(first_norm + mixed, gain_two, shift_two)
    layer_output = from_tokens(layer_wide.astype(bf16))

    upstream = to_tokens(output_grad).astype(f32)
    back_second, grad_gain_two, grad_shift_two = norm_backward(
        upstream, normed_two, inverse_two, gain_two
    )
    back_low = back_second.astype(bf16)
    grad_down_bias = jnp.sum(back_low.astype(f32), axis=0)
    back_mixed = jnp.concatenate(gather_feats(back_low), axis=0)
    back_hidden = dot(back_mixed, full_down, 1, 1)
    density = jnp.exp(-0.5 * gate_rows * gate_rows) * (1.0 / math.sqrt(2.0 * math.pi))
    back_gate = (back_hidden * up_rows * (spread + gate_rows * density)).astype(bf16)
    back_up = (back_hidden * gelu).astype(bf16)
    back_first = back_second + scatter_feats(
        dot(back_gate, full_gate, 1, 1) + dot(back_up, full_up, 1, 1)
    )

    def reduce_units(values, stages):
        for axis in stages:
            values = scatter_axis(values, axis)
        return values

    grad_down = dot(hidden, back_mixed, 0, 0).reshape(units, 2, 2, down_rows, width)
    grad_down = scatter_axis(jnp.moveaxis(grad_down, 2, 0), "c")
    grad_down = scatter_axis(scatter_axis(jnp.moveaxis(grad_down, 1, 0), "s"), "u")
    grad_ff = jnp.concatenate(
        [dot(first_low, back_gate, 0, 0), dot(first_low, back_up, 0, 0)], axis=1
    ).reshape(units, 2, FEATS, 2, w_rows, 2 * ff_part)
    grad_ff = scatter_axis(jnp.moveaxis(grad_ff, 3, 0), "c")
    grad_ff = scatter_axis(scatter_axis(jnp.moveaxis(grad_ff, 1, 0), "s"), "u")
    grad_ff = all_to_all(grad_ff.astype(bf16).reshape(FEATS * w_rows, 2 * ff_part), ("f",))
    grad_ff = grad_ff.astype(f32).reshape(FEATS, w_rows, 2, slots, 2 * down_rows)
    grad_ff = grad_ff.transpose(2, 1, 3, 0, 4).reshape(2, w_rows, FEATS * ff_part)

    back_inner, grad_gain_one, grad_shift_one = norm_backward(
        back_first, normed_one, inverse_one, gain_one
    )
    back_branch = back_inner.astype(bf16)
    grad_output_bias = jnp.sum(back_branch.astype(f32), axis=0)
    grad_output = dot(attended, back_branch, 0, 0)
    back_attended = dot(back_branch, full_output, 1, 1).astype(bf16)
    back_attended = back_attended.reshape(2, rows, FEATS, heads, HEAD_DIM)
    back_attended = jnp.concatenate([back_attended, back_attended[:, :, :, :1]], axis=3)
    back_attended = back_attended.transpose(3, 2, 1, 0, 4).reshape(
        2, 2, FEATS, rows, 2 * HEAD_DIM
    )
    back_attended = jnp.broadcast_to(
        back_attended.transpose(0, 2, 1, 3, 4)[None],
        (ranges, 2, FEATS, 2, rows, 2 * HEAD_DIM),
    )
    dout = all_to_all(back_attended.reshape(-1, 2 * HEAD_DIM), ("u", "f", "c"))
    dout = dout.reshape(slots * FEATS, rows, 2 * HEAD_DIM)
    dqkv = attend_back(table, slope, qkv, dout, o_turned, lse, seg_row, code_row)
    dqkv = all_to_all(dqkv.reshape(-1, PACK), ("u", "c")).reshape(ranges, SLOTS, group, PACK)
    dqkv = dqkv[:, :heads]
    if ranges > 1:
        dqkv = jnp.sum(dqkv.astype(f32), axis=0).astype(bf16)
    else:
        dqkv = dqkv[0]
    back_projected = dqkv.transpose(1, 0, 2).reshape(group, heads * PACK)
    partial_input = scatter_feats(dot(back_projected, w_attn, 1, 1))
    input_grad = from_tokens((back_inner + partial_input).astype(bf16))

    sums = jnp.sum(back_projected.astype(f32), axis=0).reshape(heads, 4, HEAD_DIM)

    def placed(values):
        return lax.dynamic_update_slice_in_dim(
            jnp.zeros((width,), f32), values.reshape(head_width), feat * head_width, 0
        )

    vector_grads = jnp.stack(
        [
            placed(sums[:, 0]), placed(sums[:, 2]), grad_output_bias, grad_gain_one,
            grad_shift_one, grad_down_bias, grad_gain_two, grad_shift_two,
        ],
        axis=1,
    )
    grad_attn = dot(tokens_group, back_projected, 0, 0)
    grad_attn = grad_attn + jnp.pad(vector_grads, ((0, 0), (vec_start, HEAD_DIM - 8)))
    grad_attn = jnp.concatenate([grad_attn, grad_output], axis=1)
    attn_cols = heads * PACK + width
    grad_attn = grad_attn.reshape(slots * FEATS, 2, w_rows, attn_cols)
    grad_attn = scatter_axis(jnp.moveaxis(grad_attn, 1, 0), "c").astype(bf16)
    grad_attn = all_to_all(grad_attn.reshape(-1, attn_cols), ("u", "s", "f"))
    grad_attn = jnp.sum(grad_attn.reshape(slots, FEATS, w_rows, attn_cols).astype(f32), axis=0)
    grad_output = jnp.sum(grad_attn[:, :, heads * PACK :], axis=0)
    vectors_out = jnp.sum(grad_attn[:, :, vec_start : vec_start + 8], axis=0)
    grad_attn = grad_attn[:, :, : heads * PACK].reshape(FEATS, w_rows, heads, 4, HEAD_DIM)
    grad_query, grad_key, grad_value = (
        grad_attn[:, :, :, index].transpose(1, 0, 2, 3).reshape(w_rows, width) for index in range(3)
    )
    return (
        layer_output, input_grad, grad_query, vectors_out[:, 0], grad_key, grad_value,
        vectors_out[:, 1], grad_output, vectors_out[:, 2], vectors_out[:, 3], vectors_out[:, 4],
        grad_ff[0], grad_ff[1], grad_down, vectors_out[:, 5], vectors_out[:, 6], vectors_out[:, 7],
    )


def solution(mesh):
    devices = mesh.devices
    names = ("u", "s", "f", "c")
    inner = Mesh(devices.reshape(devices.size // (4 * FEATS), 2, FEATS, 2), names)
    tokens, matrix, vector = P(None, names, None), P(names, None), P(names)
    ids = P(None, names)
    return jax.shard_map(
        on_device,
        mesh=inner,
        in_specs=(
            tokens, ids, ids, matrix, vector, matrix, matrix, vector, matrix, vector, vector,
            vector, matrix, matrix, matrix, vector, vector, vector, tokens,
        ),
        out_specs=(
            tokens, tokens, matrix, vector, matrix, matrix, vector, matrix, vector, vector,
            vector, matrix, matrix, matrix, vector, vector, vector,
        ),
        check_vma=False,
    )
```

```python
import functools
import math

import jax
import jax.numpy as jnp
import numpy as np
from jax import lax
from jax.experimental import pallas as pl
from jax.experimental.pallas import tpu as pltpu
from jax.sharding import Mesh
from jax.sharding import PartitionSpec as P

HEADS = 12
HEAD_DIM = 64
FEATS = 4
SLOTS = 4
PACK = 4 * HEAD_DIM
BLOCK = 256

norm_epsilon = 1e-12
masked_value = -1e30
f32 = jnp.float32
bf16 = jnp.bfloat16


def alibi_slopes(head_total):
    nearest = 2 ** int(math.floor(math.log2(head_total)))
    slopes = [2.0 ** (-8.0 * (index + 1) / nearest) for index in range(nearest)]
    extra = [2.0 ** (-8.0 * (index + 1) / (2 * nearest)) for index in range(2 * nearest)]
    slopes = slopes + extra[0::2][: head_total - nearest]
    return np.array(slopes, dtype=np.float32)


def dot(left, right, left_dim=1, right_dim=0):
    return lax.dot_general(
        left, right, (((left_dim,), (right_dim,)), ((), ())), preferred_element_type=f32
    )


def swap(values, axis, step=1):
    size = lax.axis_size(axis)
    return lax.ppermute(values, axis, [(i, i ^ step) for i in range(size)])


def in_order(parts, me):
    if len(parts) == 2:
        mine, other = parts
        return jnp.stack([jnp.where(me == 0, mine, other), jnp.where(me == 0, other, mine)])
    return jnp.take(jnp.stack(parts), jnp.arange(len(parts)) ^ me, axis=0)


def gather_axis(values, axis):
    size = lax.axis_size(axis)
    parts = [values] + [swap(values, axis, k) for k in range(1, size)]
    return in_order(parts, lax.axis_index(axis))


def scatter_axis(values, axis):
    size = lax.axis_size(axis)
    me = lax.axis_index(axis)

    def pick(k):
        if size == 2:
            return jnp.where((me ^ k) == 0, values[0], values[1])
        return lax.dynamic_index_in_dim(values, me ^ k, 0, keepdims=False)

    total = pick(0)
    for k in range(1, size):
        total = total + swap(pick(k).astype(bf16), axis, k).astype(f32)
    return total


def gather_feats(values):
    return [values] + [swap(values, "f", k) for k in range(1, FEATS)]


def scatter_feats(values):
    rows = values.shape[0] // FEATS
    total = values[:rows]
    for k in range(1, FEATS):
        total = total + swap(values[k * rows : (k + 1) * rows].astype(bf16), "f", k).astype(f32)
    return total


def all_to_all(values, axes):
    return lax.all_to_all(values, axes, split_axis=0, concat_axis=0, tiled=True)


def place(unit, side, feat, core, rows):
    return (((unit * 2 + side) * FEATS + feat) * 2 + core) * rows


def unpack_qkv(qkv_ref, nat_s, feat, rows):
    slots, lines, _ = qkv_ref.shape
    group = 2 * FEATS * rows
    nothing = jnp.zeros((rows, HEAD_DIM), bf16)
    for slot in range(slots):
        for k in range(FEATS):
            for side in range(2):
                here = pl.ds(
                    pl.multiple_of(place(slot // 2, side, feat ^ k, slot % 2, rows), rows), rows
                )
                start = (2 * k + side) * rows
                nat_s[here, :128] = qkv_ref[slot, start : start + rows, :]
                start = group + (2 * (k % 2) + side) * rows
                lanes = slice((k // 2) * HEAD_DIM, (k // 2 + 1) * HEAD_DIM)
                value = qkv_ref[slot, start : start + rows, lanes]
                nat_s[here, 128:] = jnp.concatenate([value, nothing], axis=1)


def turn(values):
    return jnp.transpose(values.astype(f32))


def spread_codes(code_ref, code_s):
    for start in range(0, code_ref.shape[1], 128):
        row = code_ref[:, start : start + 128]
        code_s[start : start + 128, :] = jnp.transpose(jnp.broadcast_to(row, (128, 128)))


def distance_tile():
    rows = lax.broadcasted_iota(jnp.int32, (BLOCK, BLOCK), 0)
    cols = lax.broadcasted_iota(jnp.int32, (BLOCK, BLOCK), 1)
    return (cols - rows).astype(f32)


def span(index):
    return pl.ds(pl.multiple_of(index * BLOCK, BLOCK), BLOCK)


def even_range(low, high, first, last):
    low, high = jnp.maximum(low, first), jnp.minimum(high, last)
    high = jnp.maximum(low, high)
    odd = (high - low) % 2
    up = odd * (high < last).astype(jnp.int32)
    low = low - (odd - up)
    return low, (high + up - low) // 2


def score_tile(qk_part, qz_part, code_part, seg_part, offset, slope):
    distance = distance_tile() + offset
    scores = dot(qk_part, qz_part) - slope * jnp.abs(distance)
    codes = jnp.concatenate([code_part] * (BLOCK // 128), axis=1)
    allowed = (codes == seg_part) | (distance == 0.0)
    return jnp.where(allowed, scores, masked_value)


def attend_kernel(
    table_ref, slope_ref, qkv_ref, seg_ref, code_ref, out_ref, lse_ref, ot_ref,
    nat_s, qz_s, vt_s, o_s, code_s,
):
    slope = slope_ref[0, 0]
    units = qkv_ref.shape[0] // 2
    rows = out_ref.shape[1]
    unpack_qkv(qkv_ref, nat_s, table_ref[2, 0], rows)
    spread_codes(code_ref, code_s)
    length = nat_s.shape[0]
    blocks = length // BLOCK
    qz_s[:HEAD_DIM, :] = jnp.zeros((HEAD_DIM, length), bf16)
    for start in range(0, length, 128):
        here = slice(start, start + 128)
        qk_turned = turn(nat_s[here, :128])
        qz_s[HEAD_DIM:, here] = (qk_turned[:HEAD_DIM] * (HEAD_DIM**-0.5)).astype(bf16)
        vt_s[:, here] = turn(nat_s[here, 128:])[:HEAD_DIM].astype(bf16)
    if qkv_ref.shape[0] > SLOTS:
        o_s[...] = jnp.zeros_like(o_s)
        ot_ref[...] = jnp.zeros_like(ot_ref)
        lse_ref[...] = jnp.zeros_like(lse_ref)

    def query_step(i, carry):
        here = span(i)
        qz_part = qz_s[:, here]
        seg_part = seg_ref[:, here]
        low, pairs = even_range(table_ref[0, i], table_ref[1, i], 0, blocks)

        def key_step(pair, state):
            top, total, mixed = state
            keys = [low + 2 * pair, low + 2 * pair + 1]
            scores = [
                score_tile(
                    nat_s[span(j), :128], qz_part, code_s[span(j), :], seg_part,
                    ((i - j) * BLOCK).astype(f32), slope,
                )
                for j in keys
            ]
            tops = [jnp.max(values, axis=0, keepdims=True) for values in scores]
            top_new = jnp.maximum(top, jnp.maximum(tops[0], tops[1]))
            factor = jnp.exp(top - top_new)
            total, mixed = total * factor, mixed * factor
            for j, values in zip(keys, scores):
                probs = jnp.exp(values - top_new)
                total = total + jnp.sum(probs, axis=0, keepdims=True)
                mixed = mixed + dot(vt_s[:, span(j)], probs.astype(bf16))
            return top_new, total, mixed

        top, total, mixed = lax.fori_loop(
            0,
            pairs,
            key_step,
            (
                jnp.full((1, BLOCK), masked_value, f32),
                jnp.zeros((1, BLOCK), f32),
                jnp.zeros((HEAD_DIM, BLOCK), f32),
            ),
        )
        mixed = mixed / total
        ot_ref[:, here] = mixed
        lse_ref[:, here] = top + jnp.log(total)
        o_s[here, :] = jnp.transpose(mixed)
        return carry

    lax.fori_loop(table_ref[2, 1], table_ref[2, 2], query_step, 0)
    for unit in range(units):
        for feat in range(FEATS):
            for core in range(2):
                starts = [place(unit, side, feat, core, rows) for side in range(2)]
                sides = [o_s[start : start + rows, :] for start in starts]
                out_ref[(unit * FEATS + feat) * 2 + core] = jnp.concatenate(sides, axis=1).astype(bf16)


def attend_back_kernel(
    table_ref, slope_ref, qkv_ref, dout_ref, ot_ref, lse_ref, seg_ref, code_ref, dqkv_ref,
    nat_s, qz_s, kt_s, do_s, dz_s, code_s, delta_s, dqt_s, dq_s, dk_s, dv_s,
):
    slope = slope_ref[0, 0]
    feat_self = table_ref[2, 0]
    first, last = table_ref[2, 1], table_ref[2, 2]
    slots, rows = qkv_ref.shape[0], dout_ref.shape[1]
    group = 2 * FEATS * rows
    length = nat_s.shape[0]
    blocks = length // BLOCK
    unpack_qkv(qkv_ref, nat_s, feat_self, rows)
    spread_codes(code_ref, code_s)
    for unit in range(slots // 2):
        for feat in range(FEATS):
            for core in range(2):
                piece = dout_ref[(unit * FEATS + feat) * 2 + core]
                for side in range(2):
                    start = place(unit, side, feat, core, rows)
                    do_s[start : start + rows, :] = piece[:, side * HEAD_DIM : (side + 1) * HEAD_DIM]
    zero_half = jnp.zeros((HEAD_DIM, length), bf16)
    qz_s[:HEAD_DIM, :] = zero_half
    dz_s[HEAD_DIM:, :] = zero_half
    dqt_s[...] = jnp.zeros_like(dqt_s)
    for start in range(0, length, 128):
        here = slice(start, start + 128)
        qk_turned = turn(nat_s[here, :128])
        qz_s[HEAD_DIM:, here] = (qk_turned[:HEAD_DIM] * (HEAD_DIM**-0.5)).astype(bf16)
        kt_s[:, here] = qk_turned[HEAD_DIM:].astype(bf16)
        do_turned = turn(do_s[here, :])
        dz_s[:HEAD_DIM, here] = do_turned.astype(bf16)
        delta_s[:, here] = jnp.sum(do_turned * ot_ref[:, here], axis=0, keepdims=True)

    def key_step(j, carry):
        there = span(j)
        qk_part, vx_part = nat_s[there, :128], nat_s[there, 128:]
        code_part, kt_part = code_s[there, :], kt_s[:, there]
        low, pairs = even_range(table_ref[0, j], table_ref[1, j], first, last)

        def query_step(pair, state):
            dk, dv = state
            for i in (low + 2 * pair, low + 2 * pair + 1):
                here = span(i)
                scores = score_tile(
                    qk_part, qz_s[:, here], code_part, seg_ref[:, here],
                    ((i - j) * BLOCK).astype(f32), slope,
                )
                probs = jnp.exp(scores - lse_ref[:, here])
                back_probs = dot(vx_part, dz_s[:, here])
                back_scores = (probs * (back_probs - delta_s[:, here])).astype(bf16)
                dv = dv + dot(probs.astype(bf16), do_s[here, :])
                dk = dk + dot(back_scores, nat_s[here, :HEAD_DIM])
                dqt_s[:, here] += dot(kt_part, back_scores)
            return dk, dv

        zero = jnp.zeros((BLOCK, HEAD_DIM), f32)
        dk, dv = lax.fori_loop(0, pairs, query_step, (zero, zero))
        dk_s[there, :] = dk
        dv_s[there, :] = dv
        return carry

    lax.fori_loop(0, blocks, key_step, 0)
    for start in range(0, length, 128):
        here = slice(start, start + 128)
        dq_s[here, :] = jnp.transpose(dqt_s[:, here])
    for slot in range(slots):
        for k in range(FEATS):
            for side in range(2):
                here = pl.ds(
                    pl.multiple_of(place(slot // 2, side, feat_self ^ k, slot % 2, rows), rows), rows
                )
                start = (2 * k + side) * rows
                both = jnp.concatenate([dq_s[here, :], dk_s[here, :]], axis=1) * (HEAD_DIM**-0.5)
                dqkv_ref[slot, start : start + rows, :] = both.astype(bf16)
                start = group + (2 * (k % 2) + side) * rows
                lanes = slice((k // 2) * HEAD_DIM, (k // 2 + 1) * HEAD_DIM)
                dqkv_ref[slot, start : start + rows, lanes] = dv_s[here, :].astype(bf16)


def attend(table, slope, qkv, seg_row, code_row):
    slots, length = qkv.shape[0], seg_row.shape[1]
    rows = length // (slots * FEATS * 2)
    vmem = pl.BlockSpec(memory_space=pltpu.VMEM)
    smem = pl.BlockSpec(memory_space=pltpu.SMEM)
    return pl.pallas_call(
        attend_kernel,
        out_shape=(
            jax.ShapeDtypeStruct((slots * FEATS, rows, 2 * HEAD_DIM), bf16),
            jax.ShapeDtypeStruct((1, length), f32),
            jax.ShapeDtypeStruct((HEAD_DIM, length), f32),
        ),
        in_specs=[smem, smem, vmem, vmem, vmem],
        out_specs=(vmem, vmem, vmem),
        scratch_shapes=[
            pltpu.VMEM((length, PACK), bf16),
            pltpu.VMEM((2 * HEAD_DIM, length), bf16),
            pltpu.VMEM((HEAD_DIM, length), bf16),
            pltpu.VMEM((length, HEAD_DIM), f32),
            pltpu.VMEM((length, 128), f32),
        ],
        name="attend",
    )(table, slope, qkv, seg_row, code_row)


def attend_back(table, slope, qkv, dout, o_turned, lse, seg_row, code_row):
    slots, length = qkv.shape[0], seg_row.shape[1]
    rows = length // (slots * FEATS * 2)
    vmem = pl.BlockSpec(memory_space=pltpu.VMEM)
    smem = pl.BlockSpec(memory_space=pltpu.SMEM)
    return pl.pallas_call(
        attend_back_kernel,
        out_shape=jax.ShapeDtypeStruct(qkv.shape, bf16),
        in_specs=[smem, smem] + [vmem] * 6,
        out_specs=vmem,
        scratch_shapes=[
            pltpu.VMEM((length, PACK), bf16),
            pltpu.VMEM((2 * HEAD_DIM, length), bf16),
            pltpu.VMEM((HEAD_DIM, length), bf16),
            pltpu.VMEM((length, HEAD_DIM), bf16),
            pltpu.VMEM((2 * HEAD_DIM, length), bf16),
            pltpu.VMEM((length, 128), f32),
            pltpu.VMEM((1, length), f32),
            pltpu.VMEM((HEAD_DIM, length), f32),
            pltpu.VMEM((length, HEAD_DIM), f32),
            pltpu.VMEM((length, HEAD_DIM), f32),
            pltpu.VMEM((length, HEAD_DIM), f32),
        ],
        name="attend_back",
    )(table, slope, qkv, dout, o_turned, lse, seg_row, code_row)


def norm_forward(values, gain, shift):
    centred = values - jnp.mean(values, axis=-1, keepdims=True)
    inverse = lax.rsqrt(jnp.mean(centred * centred, axis=-1, keepdims=True) + norm_epsilon)
    normed = centred * inverse
    return normed * gain + shift, normed, inverse


def norm_backward(upstream, normed, inverse, gain):
    scaled = upstream * gain
    adjusted = (
        scaled
        - jnp.mean(scaled, axis=-1, keepdims=True)
        - normed * jnp.mean(scaled * normed, axis=-1, keepdims=True)
    )
    sums = [jnp.sum(upstream * normed, axis=0, keepdims=True), jnp.sum(upstream, axis=0, keepdims=True)]
    return adjusted * inverse, sums[0], sums[1]


def call(kernel, shapes, name, where, scratch=(), aliases={}):
    spaces = {"s": pltpu.SMEM, "v": pltpu.VMEM}
    return pl.pallas_call(
        kernel,
        out_shape=shapes,
        in_specs=[pl.BlockSpec(memory_space=spaces[key]) for key in where],
        out_specs=tuple(pl.BlockSpec(memory_space=pltpu.VMEM) for _ in shapes),
        scratch_shapes=list(scratch),
        input_output_aliases=aliases,
        name=name,
    )


def pack_kernel(query_ref, key_ref, value_ref, *refs, heads):
    vector_refs, (seg_ref, live_ref, out_ref, vec_s) = refs[:-4], refs[-4:]
    w_rows = query_ref.shape[0]
    sequences, rows = seg_ref.shape
    vec_s[...] = jnp.zeros_like(vec_s)
    for index, ref in enumerate(vector_refs):
        vec_s[index : index + 1, :w_rows] = ref[...].astype(f32)
    columns = jnp.transpose(vec_s[...])[:w_rows, :HEAD_DIM]
    seg = seg_ref[...]
    codes = jnp.where(live_ref[...] == 1, seg, -1)
    lines = jnp.concatenate([seg.astype(f32), codes.astype(f32)], axis=0)
    lines = jnp.concatenate([lines, jnp.zeros((w_rows - 2 * sequences, rows), f32)], axis=0)
    if rows < HEAD_DIM:
        lines = jnp.concatenate([lines, jnp.zeros((w_rows, HEAD_DIM - rows), f32)], axis=1)
    half = heads * 2 * HEAD_DIM
    for feat in range(FEATS):
        pair, single = [], []
        for h in range(heads):
            lanes = slice((feat * heads + h) * HEAD_DIM, (feat * heads + h + 1) * HEAD_DIM)
            pair += [query_ref[:, lanes].astype(f32), key_ref[:, lanes].astype(f32)]
            single.append(value_ref[:, lanes].astype(f32))
        single += [lines, columns, jnp.zeros((w_rows, HEAD_DIM), f32)]
        for core, pieces in ((0, pair), (1, single)):
            wide = jnp.concatenate(pieces, axis=1).astype(bf16)
            for slot in range(out_ref.shape[0]):
                out_ref[slot, feat, core] = wide


def pack_late_kernel(place_ref, w_ref, gate_ref, up_ref, kept_ref, sent_ref, *, slots):
    half = w_ref.shape[1] // 2
    cols = gate_ref.shape[1] // (FEATS * slots)

    def write(core, source_ref, target_ref):
        for feat in range(FEATS):
            pieces = [w_ref[:, core * half : (core + 1) * half]]
            for slot in range(slots):
                start = (slot * FEATS + feat) * cols
                pieces.append(source_ref[:, start : start + cols])
            target_ref[feat] = jnp.concatenate([p.astype(f32) for p in pieces], axis=1).astype(bf16)

    @pl.when(place_ref[0] == 0)
    def _():
        write(0, gate_ref, kept_ref)
        write(1, up_ref, sent_ref)

    @pl.when(place_ref[0] == 1)
    def _():
        write(0, gate_ref, sent_ref)
        write(1, up_ref, kept_ref)


def route_kernel(place_ref, kept_ref, got_ref, *out_refs):
    rows = kept_ref.shape[1]
    first, second = pl.ds(0, rows), pl.ds(rows, rows)
    for k in range(FEATS):
        target = place_ref[2] ^ k
        kept, got = kept_ref[target].astype(f32), got_ref[target].astype(f32)
        first_core = place_ref[0] == 0
        both = [jnp.where(first_core, kept, got), jnp.where(first_core, got, kept)]
        out_refs[k][...] = jnp.concatenate(both, axis=0).astype(bf16)


def piece_row(place_ref, index, piece_rows):
    member = (place_ref[3] ^ (index // 2)) * 2 + (place_ref[1] ^ (index % 2))
    return pl.multiple_of(member * piece_rows, 16)


def qkv_kernel(place_ref, mine_ref, other_ref, *refs, w_rows, rows, heads, pieces):
    token_refs = refs[:FEATS]
    sent_ref, w_ref, params_ref, seg_ref, code_ref, wide_s, vec_s = refs[FEATS:]
    first_core = place_ref[0] == 0
    side, feat = place_ref[1], place_ref[2]
    half = mine_ref.shape[1]
    mine, other = mine_ref[...], other_ref[...]
    w_ref[:, :half] = jnp.where(first_core, mine, other)
    w_ref[:, half:] = jnp.where(first_core, other, mine)
    vec_s[...] = w_ref[:, 2 * half - 128 :].astype(f32)
    wide_s[...] = w_ref[:, 2 * half - 256 : 2 * half - 128].astype(f32)
    head_width = heads * HEAD_DIM
    own = vec_s[pl.ds(pl.multiple_of(feat * head_width, HEAD_DIM), head_width), :]
    own = jnp.concatenate([own, jnp.zeros((256 - head_width, 128), f32)], axis=0)
    own = jnp.concatenate([jnp.transpose(own[:128]), jnp.transpose(own[128:])], axis=1)
    local = token_refs[0].shape[0]
    group = FEATS * local
    rest = jnp.zeros((1, half - head_width), f32)
    value_bias = jnp.concatenate([own[1:2, :head_width], rest], axis=1)
    for k in range(FEATS):
        tokens = token_refs[k][...]
        values = (dot(tokens, w_ref[:, half:]) + value_bias).astype(bf16)
        pairs = dot(tokens, w_ref[:, :half])
        for h in range(heads):
            bias = own[0:1, h * HEAD_DIM : (h + 1) * HEAD_DIM]
            bias = jnp.concatenate([bias, jnp.zeros((1, HEAD_DIM), f32)], axis=1)
            made = (pairs[:, 2 * h * HEAD_DIM : 2 * (h + 1) * HEAD_DIM] + bias).astype(bf16)
            value = values[:, h * HEAD_DIM : (h + 1) * HEAD_DIM]
            start = group + (k % 2) * local
            lanes = slice((k // 2) * HEAD_DIM, (k // 2 + 1) * HEAD_DIM)
            for slot in range(pieces):
                if min(slot % SLOTS, heads - 1) == h:
                    sent_ref[slot, k * local : (k + 1) * local, :] = made
                    sent_ref[slot, start : start + local, lanes] = value
    for start in range(0, w_ref.shape[0], 128):
        turned = jnp.transpose(vec_s[start : start + 128, :])
        params_ref[:, start : start + 128] = turned[:8]
    devices = w_ref.shape[0] // w_rows
    for ref, row in ((seg_ref, 0), (code_ref, 2)):
        for device in range(0, devices, 2):
            lines = []
            for start in (device * w_rows + row, (device + 1) * w_rows + row):
                pair = wide_s[start : start + 2, HEAD_DIM : HEAD_DIM + rows]
                lines.append(jnp.where(side == 0, pair[:1], pair[1:]))
            ref[:, device * rows : (device + 2) * rows] = jnp.concatenate(lines, axis=1)


def split_rows(first_core, values, kept_ref, sent_ref, lanes, rows):
    def write(first, second):
        for block in range(values.shape[0] // (2 * rows)):
            start = 2 * rows * block
            first[block, :, lanes] = values[start : start + rows].astype(bf16)
            second[block, :, lanes] = values[start + rows : start + 2 * rows].astype(bf16)

    @pl.when(first_core)
    def _():
        write(kept_ref, sent_ref)

    @pl.when(jnp.logical_not(first_core))
    def _():
        write(sent_ref, kept_ref)


def collect_kernel(dqkv_ref, out_ref, *, heads):
    half = heads * 2 * HEAD_DIM
    group = out_ref.shape[0]
    quarter = group // 2
    out_ref[:, half + heads * HEAD_DIM :] = jnp.zeros((group, half - heads * HEAD_DIM), bf16)
    for h in range(heads):
        out_ref[:, 2 * h * HEAD_DIM : 2 * (h + 1) * HEAD_DIM] = dqkv_ref[h, :group, :]
        lanes = slice(half + h * HEAD_DIM, half + (h + 1) * HEAD_DIM)
        out_ref[:quarter, lanes] = dqkv_ref[h, group:, :HEAD_DIM]
        out_ref[quarter:, lanes] = dqkv_ref[h, group:, HEAD_DIM:]


def grad_qkv_kernel(place_ref, *refs, heads, w_rows):
    token_refs = refs[:FEATS]
    back_ref, sums_ref, kept_ref, sent_ref, wide_s, vec_s = refs[FEATS:]
    first_core = place_ref[0] == 0
    width = wide_s.shape[1]
    wide_s[...] = jnp.zeros_like(wide_s)
    wide_s[2 : 2 + sums_ref.shape[0], :] = sums_ref[...]
    for start in range(0, width, 128):
        vec_s[start : start + 128, :] = jnp.transpose(wide_s[:, start : start + 128])
    head_width = heads * HEAD_DIM
    half = 2 * head_width
    tokens = jnp.concatenate([ref[...] for ref in token_refs], axis=0)
    back = back_ref[...]
    sums = jnp.sum(back.astype(f32), axis=0, keepdims=True)
    queries = [sums[:, 2 * h * HEAD_DIM : (2 * h + 1) * HEAD_DIM] for h in range(heads)]
    none = jnp.zeros((1, 256 - head_width), f32)
    own = jnp.concatenate(
        [
            jnp.concatenate(queries + [none], axis=1),
            sums[:, half : half + 256],
            jnp.zeros((126, 256), f32),
        ],
        axis=0,
    )
    own = jnp.concatenate([jnp.transpose(own[:, :128]), jnp.transpose(own[:, 128:])], axis=0)
    here = pl.ds(pl.multiple_of(place_ref[2] * head_width, HEAD_DIM), head_width)
    vec_s[here, :] += own[:head_width]
    grad = dot(tokens, back, 0, 0)
    grad = jnp.concatenate([grad[:, : 2 * half - 128], grad[:, 2 * half - 128 :] + vec_s[...]], axis=1)
    split_rows(first_core, grad, kept_ref, sent_ref, slice(None), w_rows)


def place_first_kernel(place_ref, *refs, pieces, down_rows):
    mine_refs, other_refs = refs[:pieces], refs[pieces : 2 * pieces]
    out_ref, down_ref = refs[2 * pieces :]
    out_rows, half = mine_refs[0].shape
    out_rows = out_rows - 2 * down_rows
    feat_rows = out_rows // FEATS

    def fill(cores):
        for index in range(pieces):
            for core in range(2):
                ref = cores[core][index]
                columns = slice(core * half, (core + 1) * half)
                for k in range(FEATS):
                    start = piece_row(place_ref, index, out_rows) + (place_ref[2] ^ k) * feat_rows
                    here = pl.ds(pl.multiple_of(start, 4), feat_rows)
                    out_ref[here, columns] = ref[k * feat_rows : (k + 1) * feat_rows, :]
                start = piece_row(place_ref, index, 2 * down_rows) + core * down_rows
                here = pl.ds(pl.multiple_of(start, 8), down_rows)
                down_ref[here, :half] = ref[out_rows : out_rows + down_rows, :]
                down_ref[here, half:] = ref[out_rows + down_rows :, :]

    @pl.when(place_ref[0] == 0)
    def _():
        fill((mine_refs, other_refs))

    @pl.when(place_ref[0] == 1)
    def _():
        fill((other_refs, mine_refs))


def place_second_kernel(place_ref, *refs, indices):
    pieces = len(indices)
    mine_refs, other_refs = refs[:pieces], refs[pieces : 2 * pieces]
    gate_ref, up_ref = refs[-2:]
    rows = mine_refs[0].shape[0]
    feat_rows = rows // FEATS

    def fill(gate_refs, up_refs):
        for position, index in enumerate(indices):
            for k in range(FEATS):
                start = piece_row(place_ref, index, rows) + (place_ref[2] ^ k) * feat_rows
                here = pl.ds(pl.multiple_of(start, 4), feat_rows)
                source = slice(k * feat_rows, (k + 1) * feat_rows)
                gate_ref[here, :] = gate_refs[position][source, :]
                up_ref[here, :] = up_refs[position][source, :]

    @pl.when(place_ref[0] == 0)
    def _():
        fill(mine_refs, other_refs)

    @pl.when(place_ref[0] == 1)
    def _():
        fill(other_refs, mine_refs)


def join_kernel(
    heads_ref, tokens_ref, w_ref, params_ref,
    attended_ref, norm_ref, low_ref, normed_ref, inverse_ref, *, heads,
):
    sides = []
    for side in range(2):
        lanes = slice(side * HEAD_DIM, (side + 1) * HEAD_DIM)
        pieces = [
            heads_ref[((h // 2) * FEATS + feat) * 2 + h % 2][:, lanes]
            for feat in range(FEATS)
            for h in range(heads)
        ]
        sides.append(jnp.concatenate(pieces, axis=1))
    attended = jnp.concatenate(sides, axis=0)
    attended_ref[...] = attended
    branch = dot(attended, w_ref[...])
    first, normed, inverse = norm_forward(
        tokens_ref[...].astype(f32) + branch + params_ref[2:3, :],
        params_ref[3:4, :],
        params_ref[4:5, :],
    )
    norm_ref[...] = first
    low_ref[...] = first.astype(bf16)
    normed_ref[...] = normed
    inverse_ref[...] = inverse


def part_kernel(
    place_ref, second_ref, own_ref, got_a_ref, got_b_ref, got_c_ref, normed_ref, inverse_ref,
    params_ref, w_ref, attended_ref,
    inner_ref, dout_ref, kept_ref, sent_ref, sums_ref, *, heads, rows,
):
    back_first = second_ref[...] + own_ref[...].astype(f32) + got_a_ref[...].astype(f32)
    back_first = back_first + got_b_ref[...].astype(f32) + got_c_ref[...].astype(f32)
    inner, gain_sum, shift_sum = norm_backward(
        back_first, normed_ref[...], inverse_ref[...], params_ref[3:4, :]
    )
    inner_ref[...] = inner
    branch = inner.astype(bf16)
    sums_ref[...] = jnp.concatenate(
        [jnp.sum(branch.astype(f32), axis=0, keepdims=True), gain_sum, shift_sum], axis=0
    )
    back = dot(branch, w_ref[...], 1, 1).astype(bf16)
    for slot in range(SLOTS):
        for feat in range(FEATS):
            start = (feat * heads + min(slot, heads - 1)) * HEAD_DIM
            piece = back[:, start : start + HEAD_DIM]
            dout_ref[((slot // 2) * FEATS + feat) * 2 + slot % 2] = jnp.concatenate(
                [piece[:rows], piece[rows:]], axis=1
            )
    half = branch.shape[1] // 2
    grad = dot(attended_ref[...], branch, 0, 0).astype(bf16)
    first_core = place_ref[0] == 0
    kept_ref[...] = jnp.where(first_core, grad[:, :half], grad[:, half:])
    sent_ref[...] = jnp.where(first_core, grad[:, half:], grad[:, :half])


def finish_kernel(parts_ref, query_ref, key_ref, value_ref, *refs, heads):
    vector_refs, vec_s = refs[:-1], refs[-1]
    groups = parts_ref.shape[0] // FEATS
    vec_s[...] = jnp.zeros_like(vec_s)
    w_rows = parts_ref.shape[1]
    half = heads * 2 * HEAD_DIM
    head_width = heads * HEAD_DIM
    vectors = jnp.zeros((w_rows, 128), f32)
    for feat in range(FEATS):
        total = parts_ref[feat].astype(f32)
        for group in range(1, groups):
            total = total + parts_ref[group * FEATS + feat].astype(f32)
        lanes = slice(feat * head_width, (feat + 1) * head_width)
        for index, ref in enumerate((query_ref, key_ref)):
            starts = [(2 * h + index) * HEAD_DIM for h in range(heads)]
            ref[:, lanes] = jnp.concatenate([total[:, at : at + HEAD_DIM] for at in starts], axis=1)
        value_ref[:, lanes] = total[:, half : half + head_width]
        vectors = vectors + total[:, 2 * half - 128 :]
    vec_s[:w_rows, :] = vectors
    turned = jnp.transpose(vec_s[...])
    for index, ref in enumerate(vector_refs):
        ref[...] = turned[index : index + 1, :w_rows]


def fold_kernel(
    place_ref, ff_kept_ref, ff_got_ref, down_kept_ref, down_got_ref, out_kept_ref, out_got_ref, *refs,
    units,
):
    ff_refs, down_refs, out_refs = refs[:2], refs[2 : 2 + units], refs[2 + units :]
    rows = ff_kept_ref.shape[0] // (2 * units)
    for k, ref in enumerate(ff_refs):
        for unit in range(units):
            start = (unit * 2 + (place_ref[1] ^ k)) * rows
            here = pl.ds(pl.multiple_of(start, 16), rows)
            value = ff_kept_ref[here, :].astype(f32) + ff_got_ref[here, :].astype(f32)
            ref[unit] = value.astype(bf16)
    for kept_ref, got_ref, moved_refs in (
        (down_kept_ref, down_got_ref, down_refs),
        (out_kept_ref, out_got_ref, out_refs),
    ):
        rows = kept_ref.shape[0] // units
        for k, ref in enumerate(moved_refs):
            here = pl.ds(pl.multiple_of((place_ref[3] ^ k) * rows, 16), rows)
            value = kept_ref[here, :].astype(f32) + got_ref[here, :].astype(f32)
            ref[...] = value.astype(bf16)


def finish_late_kernel(place_ref, *refs, ff_part):
    part_refs, (kept_ref, sent_ref) = refs[:FEATS], refs[FEATS:]
    w_rows = kept_ref.shape[0]
    total = part_refs[0][:, ff_part:].astype(f32)
    for part in part_refs[1:]:
        total = total + part[:, ff_part:].astype(f32)
    for core in range(2):

        @pl.when(place_ref[0] == core)
        def _():
            for ref, rows in (
                (kept_ref, slice(core * w_rows, (core + 1) * w_rows)),
                (sent_ref, slice((1 - core) * w_rows, (2 - core) * w_rows)),
            ):
                ref[:, FEATS * ff_part :] = total[rows].astype(bf16)
                for k in range(FEATS):
                    lanes = pl.ds(pl.multiple_of((place_ref[2] ^ k) * ff_part, 128), ff_part)
                    ref[:, lanes] = part_refs[k][rows, :ff_part]


def finish_wide_kernel(
    place_ref, kept_ref, got_ref, down_kept_ref, down_got_ref,
    gate_ref, up_ref, out_ref, down_ref, *, slots,
):
    total = gate_ref.shape[1]
    cols = total // (FEATS * slots)
    half = out_ref.shape[1] // 2

    def write(first, second, down_first, down_second):
        for source, target in ((first, gate_ref), (second, up_ref)):
            for slot in range(slots):
                pieces = []
                for feat in range(FEATS):
                    start = (feat * slots + slot) * cols
                    pieces.append(source[:, start : start + cols].astype(f32))
                start = slot * FEATS * cols
                target[:, start : start + FEATS * cols] = jnp.concatenate(pieces, axis=1)
        out_ref[:, :half] = first[:, total:].astype(f32)
        out_ref[:, half:] = second[:, total:].astype(f32)
        down_ref[:, :half] = down_first[...].astype(f32)
        down_ref[:, half:] = down_second[...].astype(f32)

    @pl.when(place_ref[0] == 0)
    def _():
        write(kept_ref, got_ref, down_kept_ref, down_got_ref)

    @pl.when(place_ref[0] == 1)
    def _():
        write(got_ref, kept_ref, down_got_ref, down_kept_ref)


def after(values, *others):
    return lax.optimization_barrier((values,) + others)[0]


def tie(*values):
    return lax.optimization_barrier(values)


def on_device(
    layer_input, segment_ids, token_live, w_query, b_query, w_key, w_value, b_value,
    w_output, b_output, first_gain, first_shift, w_gate, w_up, w_down, b_down,
    second_gain, second_shift, output_grad,
):
    units = lax.axis_size("u")
    unit, side, feat, core = (lax.axis_index(name) for name in ("u", "s", "f", "c"))
    devices = units * 2 * FEATS * 2
    sequences, rows, width = layer_input.shape
    length = rows * devices
    w_rows = w_query.shape[0]
    down_rows, ff_part = w_down.shape[0], w_gate.shape[1] // FEATS
    slots = units * 2
    heads = HEADS // FEATS
    head_width = heads * HEAD_DIM
    ranges = slots // SLOTS
    local = 2 * rows
    group = FEATS * local
    here = jnp.stack([core, side, feat, unit]).astype(jnp.int32)
    parts = slots

    def exchange_sides(values):
        kept = jnp.where(side == 0, values[0], values[1])
        got = swap(jnp.where(side == 0, values[1], values[0]), "s")
        return kept, got

    def to_tokens(values):
        kept, got = exchange_sides(values)
        return jnp.concatenate(
            [jnp.where(side == 0, kept, got), jnp.where(side == 0, got, kept)], axis=0
        )

    def from_tokens(values):
        kept, got = exchange_sides(values.reshape(2, rows, width))
        return jnp.stack([jnp.where(side == 0, kept, got), jnp.where(side == 0, got, kept)])

    def to_group(blocks):
        return all_to_all(blocks.reshape(-1, blocks.shape[-1]), ("f", "c"))

    def from_units(own, other_side, pin=None):
        pieces = [own, other_side]
        for k in range(1, units):
            for piece in (own, other_side):
                pieces.append(swap(piece if pin is None else after(piece, pin), "u", k))
        return pieces

    tokens = to_tokens(layer_input)

    vectors = [
        values.reshape(1, w_rows)
        for values in (
            b_query, b_value, b_output, first_gain, first_shift, b_down, second_gain, second_shift
        )
    ]
    half = heads * 2 * HEAD_DIM
    (early,) = call(
        functools.partial(pack_kernel, heads=heads),
        (jax.ShapeDtypeStruct((slots, FEATS, 2, w_rows, half), bf16),),
        "pack_attn",
        "v" * 13,
        [pltpu.VMEM((128, 128), f32)],
    )(w_query, w_key, w_value, *vectors, segment_ids, token_live)
    early, tokens = tie(early, tokens)
    early_mine = all_to_all(early.reshape(-1, half), ("u", "s", "f", "c"))
    token_parts = gather_feats(tokens)

    late_cols = width // 2 + ff_part
    late_shape = jax.ShapeDtypeStruct((FEATS, w_rows, late_cols), bf16)
    late_kept, late_sent = call(
        functools.partial(pack_late_kernel, slots=slots), (late_shape, late_shape), "pack_late", "svvv"
    )(here, w_output, w_gate, w_up)
    routed = call(
        route_kernel,
        (jax.ShapeDtypeStruct((2 * w_rows, late_cols), bf16),) * FEATS,
        "route_late",
        "svv",
    )(here, late_kept, swap(late_sent, "c"))
    out_half = width // 2
    late_feats = [routed[0]] + [swap(routed[k], "f", k) for k in range(1, FEATS)]
    early_mine, *token_parts = tie(early_mine, *token_parts)
    early_other = swap(early_mine, "c")
    here_qkv, *late_feats = tie(here, *late_feats)
    first_own = jnp.concatenate(
        [piece[:, :out_half] for piece in late_feats] + [w_down[:, :out_half], w_down[:, out_half:]]
    )
    second_own = jnp.concatenate([piece[:, out_half:] for piece in late_feats])
    others = range(1, units)

    sent, w_attn, params, seg_row, code_row = call(
        functools.partial(qkv_kernel, w_rows=w_rows, rows=rows, heads=heads, pieces=parts),
        (
            jax.ShapeDtypeStruct((slots, group * 3 // 2, 2 * HEAD_DIM), bf16),
            jax.ShapeDtypeStruct((width, 2 * half), bf16),
            jax.ShapeDtypeStruct((8, width), f32),
            jax.ShapeDtypeStruct((1, length), f32),
            jax.ShapeDtypeStruct((1, length), f32),
        ),
        "qkv",
        "s" + "v" * (2 + FEATS),
        [pltpu.VMEM((width, 128), f32)] * 2,
    )(here_qkv, early_mine, early_other, *token_parts)
    qkv = all_to_all(sent.reshape(-1, 2 * HEAD_DIM), ("u", "c"))
    first_side = swap(first_own, "s")
    first_units = [swap(first_own, "u", k) for k in others]
    first_swaps = [swap(piece, "c") for piece in [first_own, first_side] + first_units]
    second_swaps = [swap(second_own, "c")]
    qkv, first_side, second_swaps[0], *moved = tie(
        qkv, first_side, second_swaps[0], *first_units, *first_swaps
    )
    first_units, first_swaps = moved[: units - 1], moved[units - 1 :]
    qkv = qkv.reshape(sent.shape)

    blocks = length // BLOCK
    slot_self = unit * 2 + core
    range_self = slot_self // SLOTS
    head_self = feat * heads + jnp.minimum(slot_self % SLOTS, heads - 1)
    slope = jnp.asarray(alibi_slopes(HEADS))[head_self].reshape(1, 1)
    seg_blocks = seg_row.reshape(blocks, BLOCK)
    seg_low, seg_high = seg_blocks[:, 0], seg_blocks[:, -1]
    key_low = jnp.sum(seg_high[None, :] < seg_low[:, None], axis=1, dtype=jnp.int32)
    key_high = jnp.sum(seg_low[None, :] <= seg_high[:, None], axis=1, dtype=jnp.int32)
    own = jnp.stack(
        [feat, range_self * (blocks // ranges), (range_self + 1) * (blocks // ranges)]
    ).astype(jnp.int32)
    table = jnp.stack([key_low, key_high, jnp.pad(own, (0, blocks - 3))])
    second_side = swap(second_own, "s")
    second_units = [swap(second_own, "u", k) for k in others]
    first_far = [swap(first_side, "u", k) for k in others]
    out_blocks, lse, o_turned = attend(table, slope, qkv, seg_row, code_row)
    out_blocks, second_side, *moved = tie(out_blocks, second_side, *second_units, *first_far)
    second_units, first_far = moved[: units - 1], moved[units - 1 :]
    second_far = [swap(second_side, "u", k) for k in others]
    first_swaps += [swap(piece, "c") for piece in first_far]
    second_swaps += [swap(piece, "c") for piece in [second_side] + second_units]

    def by_distance(own, other_side, near, far):
        pieces = [own, other_side]
        for index in range(units - 1):
            pieces += [near[index], far[index]]
        return pieces

    first_pieces = by_distance(first_own, first_side, first_units, first_far)
    first_others = by_distance(
        first_swaps[0], first_swaps[1], first_swaps[2 : 1 + units], first_swaps[1 + units :]
    )
    aligned = w_rows % 8 == 0

    def in_rows(pieces, feats):
        cols = pieces[0].shape[1]
        values = jnp.stack(pieces).reshape(units, 2, feats, -1, cols)
        values = jnp.take(values, jnp.arange(units) ^ unit, axis=0)
        values = jnp.take(values, jnp.arange(2) ^ side, axis=1)
        if feats == FEATS:
            values = jnp.take(values, jnp.arange(FEATS) ^ feat, axis=2)
        return values.reshape(-1, cols)

    def by_core(mine, others_):
        mine, others_ = in_rows(mine, FEATS), in_rows(others_, FEATS)
        return jnp.where(core == 0, mine, others_), jnp.where(core == 0, others_, mine)

    if aligned:
        full_output, full_down = call(
            functools.partial(place_first_kernel, pieces=parts, down_rows=down_rows),
            (
                jax.ShapeDtypeStruct((width, width), bf16),
                jax.ShapeDtypeStruct((ff_part, width), bf16),
            ),
            "place_first",
            "s" + "v" * 2 * parts,
        )(here, *first_pieces, *first_others)
    else:
        out_rows = 2 * FEATS * w_rows
        full_output = jnp.concatenate(
            by_core([p[:out_rows] for p in first_pieces], [p[:out_rows] for p in first_others]), axis=1
        )

        def down_of(pieces):
            return in_rows(
                [
                    jnp.concatenate([p[out_rows : out_rows + down_rows], p[out_rows + down_rows :]], axis=1)
                    for p in pieces
                ],
                1,
            ).reshape(slots, down_rows, width)

        down_mine, down_others = down_of(first_pieces), down_of(first_others)
        full_down = jnp.stack(
            [jnp.where(core == 0, down_mine, down_others), jnp.where(core == 0, down_others, down_mine)],
            axis=1,
        ).reshape(ff_part, width)

    heads_in = all_to_all(out_blocks.reshape(-1, 2 * HEAD_DIM), ("u", "f", "c"))
    heads_in, *second_swaps[1:] = tie(heads_in, *second_swaps[1:])
    heads_in = heads_in.reshape(ranges, SLOTS * FEATS, rows, 2 * HEAD_DIM)
    if ranges > 1:
        heads_in = lax.dynamic_index_in_dim(heads_in, unit * 2 // SLOTS, 0, keepdims=False)
    else:
        heads_in = heads_in[0]
    attended, first_norm, first_low_own, normed_one, inverse_one = call(
        functools.partial(join_kernel, heads=heads),
        (
            jax.ShapeDtypeStruct((local, width), bf16),
            jax.ShapeDtypeStruct((local, width), f32),
            jax.ShapeDtypeStruct((local, width), bf16),
            jax.ShapeDtypeStruct((local, width), f32),
            jax.ShapeDtypeStruct((local, 1), f32),
        ),
        "join_heads",
        "vvvv",
    )(heads_in, tokens, full_output, params)

    first_low_own, *second_far = tie(first_low_own, *second_far)
    second_swaps += [swap(piece, "c") for piece in second_far]
    ff_square = jax.ShapeDtypeStruct((width, ff_part), bf16)
    indices = [0, 1] + [2 * k for k in others] + [2 * k + 1 for k in others]
    second_pieces = [second_own, second_side, *second_units, *second_far]
    if aligned:
        full_gate, full_up = call(
            functools.partial(place_second_kernel, indices=indices),
            (ff_square, ff_square),
            "place_second",
            "s" + "v" * 2 * parts,
        )(here, *second_pieces, *second_swaps)
    else:
        order = [indices.index(position) for position in range(parts)]
        full_gate, full_up = by_core(
            [second_pieces[position] for position in order],
            [second_swaps[position] for position in order],
        )
    low_parts = gather_feats(first_low_own)
    full_gate, full_up, *low_parts = tie(full_gate, full_up, *low_parts)
    first_low = jnp.concatenate(low_parts, axis=0)
    gate_rows = dot(first_low, full_gate)
    up_rows = dot(first_low, full_up)
    spread = 0.5 * (1.0 + lax.erf(gate_rows * (0.5**0.5)))
    gelu = gate_rows * spread
    hidden = (gelu * up_rows).astype(bf16)
    partial_mixed = dot(hidden, full_down).astype(bf16).reshape(FEATS, local, width)
    partial_mixed, gate_kept, up_kept = tie(partial_mixed, gate_rows, up_rows)
    mixed_got = [swap(partial_mixed[k], "f", k) for k in range(1, FEATS)]
    spread = 0.5 * (1.0 + lax.erf(gate_kept * (0.5**0.5)))
    density = jnp.exp(-0.5 * gate_kept * gate_kept) * (1.0 / math.sqrt(2.0 * math.pi))
    gate_factor = (up_kept * (spread + gate_kept * density)).astype(bf16)
    up_factor = (gate_kept * spread).astype(bf16)
    bias_down, gate_factor, up_factor = tie(params[5], gate_factor, up_factor)
    mixed = partial_mixed[0].astype(f32) + bias_down
    for piece in mixed_got:
        mixed = mixed + piece.astype(f32)
    gain_two = params[6]
    layer_wide, normed_two, inverse_two = norm_forward(first_norm + mixed, gain_two, params[7])

    upstream = to_tokens(after(output_grad, out_blocks)).astype(f32)
    back_second, grad_gain_two, grad_shift_two = norm_backward(
        upstream, normed_two, inverse_two, gain_two
    )
    back_low = back_second.astype(bf16)
    grad_down_bias = jnp.sum(back_low.astype(f32), axis=0, keepdims=True)
    back_mixed = jnp.concatenate(gather_feats(back_low), axis=0)
    back_hidden = dot(back_mixed, full_down, 1, 1)
    back_gate = (back_hidden * gate_factor.astype(f32)).astype(bf16)
    back_up = (back_hidden * up_factor.astype(f32)).astype(bf16)
    partial_first = (dot(back_gate, full_gate, 1, 1) + dot(back_up, full_up, 1, 1)).astype(bf16)
    partial_first = partial_first.reshape(FEATS, local, width)
    partial_got = [swap(partial_first[k], "f", k) for k in range(1, FEATS)]
    partial_got[0], back_gate, back_up, back_mixed = tie(partial_got[0], back_gate, back_up, back_mixed)
    half_width = width // 2

    def chosen(first, second):
        return jnp.where(core == 0, first, second)

    left, right = back_mixed[:, :half_width], back_mixed[:, half_width:]

    def outer(rows_side, cols_side):
        return dot(cols_side, rows_side, 0, 0).astype(bf16).T

    ff_sent = outer(first_low, chosen(back_up, back_gate))
    down_sent = outer(hidden, chosen(right, left))
    ff_kept = outer(first_low, chosen(back_gate, back_up))
    down_kept = outer(hidden, chosen(left, right))
    here_join, ff_sent, down_sent, ff_kept, down_kept = tie(here, ff_sent, down_sent, ff_kept, down_kept)
    ff_got, down_got = None, None
    inner_shape = jax.ShapeDtypeStruct((local, width), f32)
    back_inner, dout_blocks, out_kept, out_sent, sums_one = call(
        functools.partial(part_kernel, heads=heads, rows=rows),
        (
            inner_shape,
            jax.ShapeDtypeStruct((SLOTS * FEATS, rows, 2 * HEAD_DIM), bf16),
            jax.ShapeDtypeStruct((width, half_width), bf16),
            jax.ShapeDtypeStruct((width, half_width), bf16),
            jax.ShapeDtypeStruct((3, width), f32),
        ),
        "back_join",
        "s" + "v" * 10,
    )(
        here_join, back_second, partial_first[0], *partial_got, normed_one, inverse_one, params,
        full_output, attended,
    )
    dout_sent = jnp.broadcast_to(dout_blocks[None], (ranges,) + dout_blocks.shape)
    dout = all_to_all(dout_sent.reshape(-1, 2 * HEAD_DIM), ("u", "f", "c"))
    dout = dout.reshape(slots * FEATS, rows, 2 * HEAD_DIM)

    def fold(values, axis):
        return scatter_axis(values, axis).astype(bf16)

    def added(kept, got):
        return (kept.astype(f32) + got.astype(f32)).astype(bf16)

    out_got = swap(out_sent, "c")
    ff_got, down_got = swap(after(ff_sent, dout_blocks), "c"), swap(after(down_sent, dout_blocks), "c")
    ff_rows, down_half = 2 * FEATS * w_rows, width // units
    ff_shape = jax.ShapeDtypeStruct((units, ff_rows, ff_part), bf16)
    half_shape = jax.ShapeDtypeStruct((down_half, half_width), bf16)
    folded = call(
        functools.partial(fold_kernel, units=units),
        (ff_shape,) * 2 + (half_shape,) * (2 * units),
        "fold_cores",
        "s" + "v" * 6,
    )(after(here, dout), ff_kept, ff_got, down_kept, down_got, out_kept, out_got)
    grad_ff, ff_moved = folded[0], [swap(folded[1], "s")]
    grad_down = folded[2]
    down_moved = [swap(folded[2 + k], "u", k) for k in range(1, units)]
    grad_out = folded[2 + units]
    out_moved = [swap(folded[2 + units + k], "u", k) for k in range(1, units)]

    def parts_of(values, axis):
        size, me = lax.axis_size(axis), lax.axis_index(axis)
        if size == 2:
            return [jnp.where(me == 0, values[0], values[1]), jnp.where(me == 0, values[1], values[0])]
        return [lax.dynamic_index_in_dim(values, me ^ k, 0, keepdims=False) for k in range(size)]

    def send(values, axis):
        own, *rest = parts_of(values, axis)
        return own, [swap(piece, axis, k + 1) for k, piece in enumerate(rest)]

    def total(own, got):
        result = own.astype(f32)
        for piece in got:
            result = result + piece.astype(f32)
        return result

    dout, grad_ff, grad_down, grad_out = tie(dout, grad_ff, grad_down, grad_out)
    dqkv = attend_back(table, slope, qkv, dout, o_turned, lse, seg_row, code_row)
    dqkv, *moved = tie(dqkv, *ff_moved, *down_moved, *out_moved)
    ff_moved, down_moved, out_moved = moved[:1], moved[1:units], moved[units:]
    grad_ff = total(grad_ff, ff_moved).astype(bf16)
    grad_down = total(grad_down, down_moved).astype(bf16).reshape(2, 2 * down_rows, half_width)
    grad_out = total(grad_out, out_moved).astype(bf16).reshape(2, FEATS * 2 * w_rows, half_width)
    grad_ff, ff_moved = send(grad_ff, "u")
    grad_down, down_moved = send(grad_down, "s")
    dqkv = all_to_all(dqkv.reshape(-1, 2 * HEAD_DIM), ("u", "c"))
    dqkv, *moved = tie(dqkv, *ff_moved, *down_moved)
    ff_moved, down_moved = moved[:-1], moved[-1:]
    grad_out, out_moved = send(after(grad_out, dqkv), "s")
    layer_wide_low = after(layer_wide.astype(bf16), dqkv)
    dqkv = dqkv.reshape(ranges, SLOTS, group * 3 // 2, 2 * HEAD_DIM)
    if ranges > 1:
        dqkv = jnp.sum(dqkv.astype(f32), axis=0).astype(bf16)
    else:
        dqkv = dqkv[0]
    vector_sums = jnp.concatenate([sums_one, grad_down_bias, grad_gain_two, grad_shift_two], axis=0)
    (back_projected,) = call(
        functools.partial(collect_kernel, heads=heads),
        (jax.ShapeDtypeStruct((group, 2 * half), bf16),),
        "collect",
        "v",
    )(dqkv)
    attn_shape = jax.ShapeDtypeStruct((slots * FEATS, w_rows, 2 * half), bf16)
    attn_kept, attn_sent = call(
        functools.partial(grad_qkv_kernel, heads=heads, w_rows=w_rows),
        (attn_shape, attn_shape),
        "grad_qkv",
        "s" + "v" * (FEATS + 2),
        [pltpu.VMEM((128, width), f32), pltpu.VMEM((width, 128), f32)],
    )(here, *token_parts, back_projected, vector_sums)
    attn_sent, back_projected = tie(attn_sent, back_projected)
    partial_input = dot(back_projected, w_attn, 1, 1).astype(bf16).reshape(FEATS, local, width)
    input_got = [swap(partial_input[k], "f", k) for k in range(1, FEATS)]
    grad_attn = added(after(attn_kept, partial_input), swap(attn_sent, "c"))
    back_inner, grad_attn, grad_ff = tie(back_inner, grad_attn, grad_ff)
    grad_attn = all_to_all(grad_attn.reshape(-1, 2 * half), ("u", "s", "f"))
    grad_ff = total(grad_ff, ff_moved)
    grad_out = total(grad_out, out_moved)
    grad_down = total(grad_down, down_moved).reshape(2, down_rows, half_width)
    grad_late = jnp.concatenate([grad_ff, grad_out], axis=1).astype(bf16)
    grad_late = grad_late.reshape(FEATS, 2 * w_rows, ff_part + half_width)

    input_sum = back_inner + partial_input[0].astype(f32)
    for piece in input_got:
        input_sum = input_sum + piece.astype(f32)
    input_grad = from_tokens(input_sum.astype(bf16))
    layer_output = from_tokens(layer_wide_low)

    late_got = [lax.dynamic_index_in_dim(grad_late, feat, 0, keepdims=False)]
    late_got += [
        swap(lax.dynamic_index_in_dim(grad_late, feat ^ k, 0, keepdims=False), "f", k)
        for k in range(1, FEATS)
    ]
    wide_shape = jax.ShapeDtypeStruct((w_rows, FEATS * ff_part + half_width), bf16)
    wide_kept, wide_sent = call(
        functools.partial(finish_late_kernel, ff_part=ff_part),
        (wide_shape, wide_shape),
        "finish_late",
        "s" + "v" * FEATS,
    )(here, *late_got)
    wide_got = swap(wide_sent, "c")
    down_kept = chosen(grad_down[0], grad_down[1])
    down_got = swap(chosen(grad_down[1], grad_down[0]).astype(bf16), "c")
    ff_out_shape = jax.ShapeDtypeStruct((w_rows, FEATS * ff_part), f32)
    grad_gate, grad_up, grad_output, grad_down = call(
        functools.partial(finish_wide_kernel, slots=slots),
        (
            ff_out_shape,
            ff_out_shape,
            jax.ShapeDtypeStruct((w_rows, width), f32),
            jax.ShapeDtypeStruct((down_rows, width), f32),
        ),
        "finish_wide",
        "svvvv",
    )(here, wide_kept, wide_got, down_kept, down_got)
    matrix_shape = jax.ShapeDtypeStruct((w_rows, width), f32)
    grad_query, grad_key, grad_value, *vectors_out = call(
        functools.partial(finish_kernel, heads=heads),
        (matrix_shape,) * 3 + (jax.ShapeDtypeStruct((1, w_rows), f32),) * 8,
        "finish",
        "v",
        [pltpu.VMEM((128, 128), f32)],
    )(grad_attn.reshape(slots * FEATS, w_rows, 2 * half))
    vectors_out = [values.reshape(w_rows) for values in vectors_out]
    return (
        layer_output, input_grad, grad_query, vectors_out[0], grad_key, grad_value,
        vectors_out[1], grad_output, vectors_out[2], vectors_out[3], vectors_out[4],
        grad_gate, grad_up, grad_down, vectors_out[5], vectors_out[6], vectors_out[7],
    )


def solution(mesh):
    devices = mesh.devices
    names = ("u", "s", "f", "c")
    inner = Mesh(devices.reshape(devices.size // (4 * FEATS), 2, FEATS, 2), names)
    tokens, matrix, vector = P(None, names, None), P(names, None), P(names)
    ids = P(None, names)
    return jax.shard_map(
        on_device,
        mesh=inner,
        in_specs=(
            tokens, ids, ids, matrix, vector, matrix, matrix, vector, matrix, vector, vector,
            vector, matrix, matrix, matrix, vector, vector, vector, tokens,
        ),
        out_specs=(
            tokens, tokens, matrix, vector, matrix, matrix, vector, matrix, vector, vector,
            vector, matrix, matrix, matrix, vector, vector, vector,
        ),
        check_vma=False,
    )
```

```python
import functools
import math

import jax
import jax.numpy as jnp
import numpy as np
from jax import lax
from jax.experimental import pallas as pl
from jax.experimental.pallas import tpu as pltpu
from jax.sharding import Mesh
from jax.sharding import PartitionSpec as P

HEADS = 12
HEAD_DIM = 64
FEATS = 4
SLOTS = 4
PACK = 4 * HEAD_DIM
BLOCK = 256

norm_epsilon = 1e-12
masked_value = -1e30
f32 = jnp.float32
bf16 = jnp.bfloat16


def alibi_slopes(head_total):
    nearest = 2 ** int(math.floor(math.log2(head_total)))
    slopes = [2.0 ** (-8.0 * (index + 1) / nearest) for index in range(nearest)]
    extra = [2.0 ** (-8.0 * (index + 1) / (2 * nearest)) for index in range(2 * nearest)]
    slopes = slopes + extra[0::2][: head_total - nearest]
    return np.array(slopes, dtype=np.float32)


def dot(left, right, left_dim=1, right_dim=0):
    return lax.dot_general(
        left, right, (((left_dim,), (right_dim,)), ((), ())), preferred_element_type=f32
    )


def swap(values, axis, step=1):
    size = lax.axis_size(axis)
    return lax.ppermute(values, axis, [(i, i ^ step) for i in range(size)])


def in_order(parts, me):
    if len(parts) == 2:
        mine, other = parts
        return jnp.stack([jnp.where(me == 0, mine, other), jnp.where(me == 0, other, mine)])
    return jnp.take(jnp.stack(parts), jnp.arange(len(parts)) ^ me, axis=0)


def gather_axis(values, axis):
    size = lax.axis_size(axis)
    parts = [values] + [swap(values, axis, k) for k in range(1, size)]
    return in_order(parts, lax.axis_index(axis))


def scatter_axis(values, axis):
    size = lax.axis_size(axis)
    me = lax.axis_index(axis)

    def pick(k):
        if size == 2:
            return jnp.where((me ^ k) == 0, values[0], values[1])
        return lax.dynamic_index_in_dim(values, me ^ k, 0, keepdims=False)

    total = pick(0)
    for k in range(1, size):
        total = total + swap(pick(k).astype(bf16), axis, k).astype(f32)
    return total


def gather_feats(values):
    return [values] + [swap(values, "f", k) for k in range(1, FEATS)]


def scatter_feats(values):
    rows = values.shape[0] // FEATS
    total = values[:rows]
    for k in range(1, FEATS):
        total = total + swap(values[k * rows : (k + 1) * rows].astype(bf16), "f", k).astype(f32)
    return total


def all_to_all(values, axes):
    return lax.all_to_all(values, axes, split_axis=0, concat_axis=0, tiled=True)


def place(unit, side, feat, core, rows):
    return (((unit * 2 + side) * FEATS + feat) * 2 + core) * rows


def unpack_qkv(qkv_ref, nat_s, feat, rows):
    slots, lines, _ = qkv_ref.shape
    group = 2 * FEATS * rows
    nothing = jnp.zeros((rows, HEAD_DIM), bf16)
    for slot in range(slots):
        for k in range(FEATS):
            for side in range(2):
                here = pl.ds(
                    pl.multiple_of(place(slot // 2, side, feat ^ k, slot % 2, rows), rows), rows
                )
                start = (2 * k + side) * rows
                nat_s[here, :128] = qkv_ref[slot, start : start + rows, :]
                start = group + (2 * (k % 2) + side) * rows
                lanes = slice((k // 2) * HEAD_DIM, (k // 2 + 1) * HEAD_DIM)
                value = qkv_ref[slot, start : start + rows, lanes]
                nat_s[here, 128:] = jnp.concatenate([value, nothing], axis=1)


def turn(values):
    return jnp.transpose(values.astype(f32))


def spread_codes(code_ref, code_s):
    for start in range(0, code_ref.shape[1], 128):
        row = code_ref[:, start : start + 128]
        code_s[start : start + 128, :] = jnp.transpose(jnp.broadcast_to(row, (128, 128)))


def distance_tile():
    rows = lax.broadcasted_iota(jnp.int32, (BLOCK, BLOCK), 0)
    cols = lax.broadcasted_iota(jnp.int32, (BLOCK, BLOCK), 1)
    return (cols - rows).astype(f32)


def span(index):
    return pl.ds(pl.multiple_of(index * BLOCK, BLOCK), BLOCK)


def even_range(low, high, first, last):
    low, high = jnp.maximum(low, first), jnp.minimum(high, last)
    high = jnp.maximum(low, high)
    odd = (high - low) % 2
    up = odd * (high < last).astype(jnp.int32)
    low = low - (odd - up)
    return low, (high + up - low) // 2


def score_tile(qk_part, qz_part, code_part, seg_part, offset, slope):
    distance = distance_tile() + offset
    scores = dot(qk_part, qz_part) - slope * jnp.abs(distance)
    codes = jnp.concatenate([code_part] * (BLOCK // 128), axis=1)
    allowed = (codes == seg_part) | (distance == 0.0)
    return jnp.where(allowed, scores, masked_value)


def attend_kernel(
    table_ref, slope_ref, qkv_ref, seg_ref, code_ref, out_ref, lse_ref, ot_ref,
    nat_s, qz_s, vt_s, o_s, code_s,
):
    slope = slope_ref[0, 0]
    units = qkv_ref.shape[0] // 2
    rows = out_ref.shape[1]
    unpack_qkv(qkv_ref, nat_s, table_ref[2, 0], rows)
    spread_codes(code_ref, code_s)
    length = nat_s.shape[0]
    blocks = length // BLOCK
    qz_s[:HEAD_DIM, :] = jnp.zeros((HEAD_DIM, length), bf16)
    for start in range(0, length, 128):
        here = slice(start, start + 128)
        qk_turned = turn(nat_s[here, :128])
        qz_s[HEAD_DIM:, here] = (qk_turned[:HEAD_DIM] * (HEAD_DIM**-0.5)).astype(bf16)
        vt_s[:, here] = turn(nat_s[here, 128:])[:HEAD_DIM].astype(bf16)
    if qkv_ref.shape[0] > SLOTS:
        o_s[...] = jnp.zeros_like(o_s)
        ot_ref[...] = jnp.zeros_like(ot_ref)
        lse_ref[...] = jnp.zeros_like(lse_ref)

    def query_step(i, carry):
        here = span(i)
        qz_part = qz_s[:, here]
        seg_part = seg_ref[:, here]
        low, pairs = even_range(table_ref[0, i], table_ref[1, i], 0, blocks)

        def key_step(pair, state):
            top, total, mixed = state
            keys = [low + 2 * pair, low + 2 * pair + 1]
            scores = [
                score_tile(
                    nat_s[span(j), :128], qz_part, code_s[span(j), :], seg_part,
                    ((i - j) * BLOCK).astype(f32), slope,
                )
                for j in keys
            ]
            tops = [jnp.max(values, axis=0, keepdims=True) for values in scores]
            top_new = jnp.maximum(top, jnp.maximum(tops[0], tops[1]))
            factor = jnp.exp(top - top_new)
            total, mixed = total * factor, mixed * factor
            for j, values in zip(keys, scores):
                probs = jnp.exp(values - top_new)
                total = total + jnp.sum(probs, axis=0, keepdims=True)
                mixed = mixed + dot(vt_s[:, span(j)], probs.astype(bf16))
            return top_new, total, mixed

        top, total, mixed = lax.fori_loop(
            0,
            pairs,
            key_step,
            (
                jnp.full((1, BLOCK), masked_value, f32),
                jnp.zeros((1, BLOCK), f32),
                jnp.zeros((HEAD_DIM, BLOCK), f32),
            ),
        )
        mixed = mixed / total
        ot_ref[:, here] = mixed
        lse_ref[:, here] = top + jnp.log(total)
        o_s[here, :] = jnp.transpose(mixed)
        return carry

    lax.fori_loop(table_ref[2, 1], table_ref[2, 2], query_step, 0)
    for unit in range(units):
        for feat in range(FEATS):
            for core in range(2):
                starts = [place(unit, side, feat, core, rows) for side in range(2)]
                sides = [o_s[start : start + rows, :] for start in starts]
                out_ref[(unit * FEATS + feat) * 2 + core] = jnp.concatenate(sides, axis=1).astype(bf16)


def attend_back_kernel(
    table_ref, slope_ref, qkv_ref, dout_ref, ot_ref, lse_ref, seg_ref, code_ref, dqkv_ref,
    nat_s, qz_s, kt_s, do_s, dz_s, code_s, delta_s, dqt_s, dq_s, dk_s, dv_s,
):
    slope = slope_ref[0, 0]
    feat_self = table_ref[2, 0]
    first, last = table_ref[2, 1], table_ref[2, 2]
    slots, rows = qkv_ref.shape[0], dout_ref.shape[1]
    group = 2 * FEATS * rows
    length = nat_s.shape[0]
    blocks = length // BLOCK
    unpack_qkv(qkv_ref, nat_s, feat_self, rows)
    spread_codes(code_ref, code_s)
    for unit in range(slots // 2):
        for feat in range(FEATS):
            for core in range(2):
                piece = dout_ref[(unit * FEATS + feat) * 2 + core]
                for side in range(2):
                    start = place(unit, side, feat, core, rows)
                    do_s[start : start + rows, :] = piece[:, side * HEAD_DIM : (side + 1) * HEAD_DIM]
    zero_half = jnp.zeros((HEAD_DIM, length), bf16)
    qz_s[:HEAD_DIM, :] = zero_half
    dz_s[HEAD_DIM:, :] = zero_half
    dqt_s[...] = jnp.zeros_like(dqt_s)
    for start in range(0, length, 128):
        here = slice(start, start + 128)
        qk_turned = turn(nat_s[here, :128])
        qz_s[HEAD_DIM:, here] = (qk_turned[:HEAD_DIM] * (HEAD_DIM**-0.5)).astype(bf16)
        kt_s[:, here] = qk_turned[HEAD_DIM:].astype(bf16)
        do_turned = turn(do_s[here, :])
        dz_s[:HEAD_DIM, here] = do_turned.astype(bf16)
        delta_s[:, here] = jnp.sum(do_turned * ot_ref[:, here], axis=0, keepdims=True)

    def key_step(j, carry):
        there = span(j)
        qk_part, vx_part = nat_s[there, :128], nat_s[there, 128:]
        code_part, kt_part = code_s[there, :], kt_s[:, there]
        low, pairs = even_range(table_ref[0, j], table_ref[1, j], first, last)

        def query_step(pair, state):
            dk, dv = state
            for i in (low + 2 * pair, low + 2 * pair + 1):
                here = span(i)
                scores = score_tile(
                    qk_part, qz_s[:, here], code_part, seg_ref[:, here],
                    ((i - j) * BLOCK).astype(f32), slope,
                )
                probs = jnp.exp(scores - lse_ref[:, here])
                back_probs = dot(vx_part, dz_s[:, here])
                back_scores = (probs * (back_probs - delta_s[:, here])).astype(bf16)
                dv = dv + dot(probs.astype(bf16), do_s[here, :])
                dk = dk + dot(back_scores, nat_s[here, :HEAD_DIM])
                dqt_s[:, here] += dot(kt_part, back_scores)
            return dk, dv

        zero = jnp.zeros((BLOCK, HEAD_DIM), f32)
        dk, dv = lax.fori_loop(0, pairs, query_step, (zero, zero))
        dk_s[there, :] = dk
        dv_s[there, :] = dv
        return carry

    lax.fori_loop(0, blocks, key_step, 0)
    for start in range(0, length, 128):
        here = slice(start, start + 128)
        dq_s[here, :] = jnp.transpose(dqt_s[:, here])
    for slot in range(slots):
        for k in range(FEATS):
            for side in range(2):
                here = pl.ds(
                    pl.multiple_of(place(slot // 2, side, feat_self ^ k, slot % 2, rows), rows), rows
                )
                start = (2 * k + side) * rows
                both = jnp.concatenate([dq_s[here, :], dk_s[here, :]], axis=1) * (HEAD_DIM**-0.5)
                dqkv_ref[slot, start : start + rows, :] = both.astype(bf16)
                start = group + (2 * (k % 2) + side) * rows
                lanes = slice((k // 2) * HEAD_DIM, (k // 2 + 1) * HEAD_DIM)
                dqkv_ref[slot, start : start + rows, lanes] = dv_s[here, :].astype(bf16)


def attend(table, slope, qkv, seg_row, code_row):
    slots, length = qkv.shape[0], seg_row.shape[1]
    rows = length // (slots * FEATS * 2)
    vmem = pl.BlockSpec(memory_space=pltpu.VMEM)
    smem = pl.BlockSpec(memory_space=pltpu.SMEM)
    return pl.pallas_call(
        attend_kernel,
        out_shape=(
            jax.ShapeDtypeStruct((slots * FEATS, rows, 2 * HEAD_DIM), bf16),
            jax.ShapeDtypeStruct((1, length), f32),
            jax.ShapeDtypeStruct((HEAD_DIM, length), f32),
        ),
        in_specs=[smem, smem, vmem, vmem, vmem],
        out_specs=(vmem, vmem, vmem),
        scratch_shapes=[
            pltpu.VMEM((length, PACK), bf16),
            pltpu.VMEM((2 * HEAD_DIM, length), bf16),
            pltpu.VMEM((HEAD_DIM, length), bf16),
            pltpu.VMEM((length, HEAD_DIM), f32),
            pltpu.VMEM((length, 128), f32),
        ],
        name="attend",
    )(table, slope, qkv, seg_row, code_row)


def attend_back(table, slope, qkv, dout, o_turned, lse, seg_row, code_row):
    slots, length = qkv.shape[0], seg_row.shape[1]
    rows = length // (slots * FEATS * 2)
    vmem = pl.BlockSpec(memory_space=pltpu.VMEM)
    smem = pl.BlockSpec(memory_space=pltpu.SMEM)
    return pl.pallas_call(
        attend_back_kernel,
        out_shape=jax.ShapeDtypeStruct(qkv.shape, bf16),
        in_specs=[smem, smem] + [vmem] * 6,
        out_specs=vmem,
        scratch_shapes=[
            pltpu.VMEM((length, PACK), bf16),
            pltpu.VMEM((2 * HEAD_DIM, length), bf16),
            pltpu.VMEM((HEAD_DIM, length), bf16),
            pltpu.VMEM((length, HEAD_DIM), bf16),
            pltpu.VMEM((2 * HEAD_DIM, length), bf16),
            pltpu.VMEM((length, 128), f32),
            pltpu.VMEM((1, length), f32),
            pltpu.VMEM((HEAD_DIM, length), f32),
            pltpu.VMEM((length, HEAD_DIM), f32),
            pltpu.VMEM((length, HEAD_DIM), f32),
            pltpu.VMEM((length, HEAD_DIM), f32),
        ],
        name="attend_back",
    )(table, slope, qkv, dout, o_turned, lse, seg_row, code_row)


def norm_forward(values, gain, shift):
    centred = values - jnp.mean(values, axis=-1, keepdims=True)
    inverse = lax.rsqrt(jnp.mean(centred * centred, axis=-1, keepdims=True) + norm_epsilon)
    normed = centred * inverse
    return normed * gain + shift, normed, inverse


def norm_backward(upstream, normed, inverse, gain):
    scaled = upstream * gain
    adjusted = (
        scaled
        - jnp.mean(scaled, axis=-1, keepdims=True)
        - normed * jnp.mean(scaled * normed, axis=-1, keepdims=True)
    )
    sums = [jnp.sum(upstream * normed, axis=0, keepdims=True), jnp.sum(upstream, axis=0, keepdims=True)]
    return adjusted * inverse, sums[0], sums[1]


def call(kernel, shapes, name, where, scratch=(), aliases={}):
    spaces = {"s": pltpu.SMEM, "v": pltpu.VMEM}
    return pl.pallas_call(
        kernel,
        out_shape=shapes,
        in_specs=[pl.BlockSpec(memory_space=spaces[key]) for key in where],
        out_specs=tuple(pl.BlockSpec(memory_space=pltpu.VMEM) for _ in shapes),
        scratch_shapes=list(scratch),
        input_output_aliases=aliases,
        name=name,
    )


def pack_kernel(query_ref, key_ref, value_ref, *refs, heads):
    vector_refs, (seg_ref, live_ref, out_ref, vec_s) = refs[:-4], refs[-4:]
    w_rows = query_ref.shape[0]
    sequences, rows = seg_ref.shape
    vec_s[...] = jnp.zeros_like(vec_s)
    for index, ref in enumerate(vector_refs):
        vec_s[index : index + 1, :w_rows] = ref[...].astype(f32)
    columns = jnp.transpose(vec_s[...])[:w_rows, :HEAD_DIM]
    seg = seg_ref[...]
    codes = jnp.where(live_ref[...] == 1, seg, -1)
    lines = jnp.concatenate([seg.astype(f32), codes.astype(f32)], axis=0)
    lines = jnp.concatenate([lines, jnp.zeros((w_rows - 2 * sequences, rows), f32)], axis=0)
    if rows < HEAD_DIM:
        lines = jnp.concatenate([lines, jnp.zeros((w_rows, HEAD_DIM - rows), f32)], axis=1)
    half = heads * 2 * HEAD_DIM
    for feat in range(FEATS):
        pair, single = [], []
        for h in range(heads):
            lanes = slice((feat * heads + h) * HEAD_DIM, (feat * heads + h + 1) * HEAD_DIM)
            pair += [query_ref[:, lanes].astype(f32), key_ref[:, lanes].astype(f32)]
            single.append(value_ref[:, lanes].astype(f32))
        single += [lines, columns, jnp.zeros((w_rows, HEAD_DIM), f32)]
        for core, pieces in ((0, pair), (1, single)):
            wide = jnp.concatenate(pieces, axis=1).astype(bf16)
            out_ref[feat, core] = wide


def pack_late_kernel(place_ref, w_ref, gate_ref, up_ref, kept_ref, sent_ref, *, slots):
    half = w_ref.shape[1] // 2
    cols = gate_ref.shape[1] // (FEATS * slots)

    def write(core, source_ref, target_ref):
        for feat in range(FEATS):
            pieces = [w_ref[:, core * half : (core + 1) * half]]
            for slot in range(slots):
                start = (slot * FEATS + feat) * cols
                pieces.append(source_ref[:, start : start + cols])
            target_ref[feat] = jnp.concatenate([p.astype(f32) for p in pieces], axis=1).astype(bf16)

    @pl.when(place_ref[0] == 0)
    def _():
        write(0, gate_ref, kept_ref)
        write(1, up_ref, sent_ref)

    @pl.when(place_ref[0] == 1)
    def _():
        write(0, gate_ref, sent_ref)
        write(1, up_ref, kept_ref)


def route_kernel(place_ref, kept_ref, got_ref, *out_refs):
    rows = kept_ref.shape[1]
    first, second = pl.ds(0, rows), pl.ds(rows, rows)
    for k in range(FEATS):
        target = place_ref[2] ^ k
        kept, got = kept_ref[target].astype(f32), got_ref[target].astype(f32)
        first_core = place_ref[0] == 0
        both = [jnp.where(first_core, kept, got), jnp.where(first_core, got, kept)]
        out_refs[k][...] = jnp.concatenate(both, axis=0).astype(bf16)


def piece_row(place_ref, index, piece_rows):
    member = (place_ref[3] ^ (index // 2)) * 2 + (place_ref[1] ^ (index % 2))
    return pl.multiple_of(member * piece_rows, 16)


def qkv_kernel(place_ref, *refs, w_rows, rows, heads, pieces):
    mine_refs, other_refs = refs[:pieces], refs[pieces : 2 * pieces]
    token_refs = refs[2 * pieces : 2 * pieces + FEATS]
    sent_ref, w_ref, params_ref, seg_ref, code_ref, wide_s, vec_s = refs[2 * pieces + FEATS :]
    first_core = place_ref[0] == 0
    side, feat = place_ref[1], place_ref[2]
    piece_rows, half = mine_refs[0].shape
    for index in range(pieces):
        here = pl.ds(piece_row(place_ref, index, piece_rows), piece_rows)
        mine, other = mine_refs[index][...], other_refs[index][...]
        w_ref[here, :half] = jnp.where(first_core, mine, other)
        w_ref[here, half:] = jnp.where(first_core, other, mine)
    vec_s[...] = w_ref[:, 2 * half - 128 :].astype(f32)
    wide_s[...] = w_ref[:, 2 * half - 256 : 2 * half - 128].astype(f32)
    head_width = heads * HEAD_DIM
    own = vec_s[pl.ds(pl.multiple_of(feat * head_width, HEAD_DIM), head_width), :]
    own = jnp.concatenate([own, jnp.zeros((256 - head_width, 128), f32)], axis=0)
    own = jnp.concatenate([jnp.transpose(own[:128]), jnp.transpose(own[128:])], axis=1)
    local = token_refs[0].shape[0]
    group = FEATS * local
    rest = jnp.zeros((1, half - head_width), f32)
    value_bias = jnp.concatenate([own[1:2, :head_width], rest], axis=1)
    for k in range(FEATS):
        tokens = token_refs[k][...]
        values = (dot(tokens, w_ref[:, half:]) + value_bias).astype(bf16)
        pairs = dot(tokens, w_ref[:, :half])
        for h in range(heads):
            bias = own[0:1, h * HEAD_DIM : (h + 1) * HEAD_DIM]
            bias = jnp.concatenate([bias, jnp.zeros((1, HEAD_DIM), f32)], axis=1)
            made = (pairs[:, 2 * h * HEAD_DIM : 2 * (h + 1) * HEAD_DIM] + bias).astype(bf16)
            value = values[:, h * HEAD_DIM : (h + 1) * HEAD_DIM]
            start = group + (k % 2) * local
            lanes = slice((k // 2) * HEAD_DIM, (k // 2 + 1) * HEAD_DIM)
            for slot in range(pieces):
                if min(slot % SLOTS, heads - 1) == h:
                    sent_ref[slot, k * local : (k + 1) * local, :] = made
                    sent_ref[slot, start : start + local, lanes] = value
    for start in range(0, w_ref.shape[0], 128):
        turned = jnp.transpose(vec_s[start : start + 128, :])
        params_ref[:, start : start + 128] = turned[:8]
    devices = w_ref.shape[0] // w_rows
    for ref, row in ((seg_ref, 0), (code_ref, 2)):
        for device in range(0, devices, 2):
            lines = []
            for start in (device * w_rows + row, (device + 1) * w_rows + row):
                pair = wide_s[start : start + 2, HEAD_DIM : HEAD_DIM + rows]
                lines.append(jnp.where(side == 0, pair[:1], pair[1:]))
            ref[:, device * rows : (device + 2) * rows] = jnp.concatenate(lines, axis=1)


def split_rows(first_core, values, kept_ref, sent_ref, lanes, rows):
    def write(first, second):
        for block in range(values.shape[0] // (2 * rows)):
            start = 2 * rows * block
            first[block, :, lanes] = values[start : start + rows].astype(bf16)
            second[block, :, lanes] = values[start + rows : start + 2 * rows].astype(bf16)

    @pl.when(first_core)
    def _():
        write(kept_ref, sent_ref)

    @pl.when(jnp.logical_not(first_core))
    def _():
        write(sent_ref, kept_ref)


def grad_qkv_kernel(place_ref, *refs, heads, w_rows):
    token_refs = refs[:FEATS]
    dqkv_ref, sums_ref, back_ref, kept_ref, sent_ref, wide_s, vec_s = refs[FEATS:]
    first_core = place_ref[0] == 0
    head_width = heads * HEAD_DIM
    half = 2 * head_width
    group = back_ref.shape[0]
    quarter = group // 2
    back_ref[:, half + head_width :] = jnp.zeros((group, half - head_width), bf16)
    for h in range(heads):
        back_ref[:, 2 * h * HEAD_DIM : 2 * (h + 1) * HEAD_DIM] = dqkv_ref[h, :group, :]
        lanes = slice(half + h * HEAD_DIM, half + (h + 1) * HEAD_DIM)
        back_ref[:quarter, lanes] = dqkv_ref[h, group:, :HEAD_DIM]
        back_ref[quarter:, lanes] = dqkv_ref[h, group:, HEAD_DIM:]
    width = wide_s.shape[1]
    wide_s[...] = jnp.zeros_like(wide_s)
    wide_s[2 : 2 + sums_ref.shape[0], :] = sums_ref[...]
    for start in range(0, width, 128):
        vec_s[start : start + 128, :] = jnp.transpose(wide_s[:, start : start + 128])
    tokens = jnp.concatenate([ref[...] for ref in token_refs], axis=0)
    back = back_ref[...]
    sums = jnp.sum(back.astype(f32), axis=0, keepdims=True)
    queries = [sums[:, 2 * h * HEAD_DIM : (2 * h + 1) * HEAD_DIM] for h in range(heads)]
    none = jnp.zeros((1, 256 - head_width), f32)
    own = jnp.concatenate(
        [
            jnp.concatenate(queries + [none], axis=1),
            sums[:, half : half + 256],
            jnp.zeros((126, 256), f32),
        ],
        axis=0,
    )
    own = jnp.concatenate([jnp.transpose(own[:, :128]), jnp.transpose(own[:, 128:])], axis=0)
    here = pl.ds(pl.multiple_of(place_ref[2] * head_width, HEAD_DIM), head_width)
    vec_s[here, :] += own[:head_width]
    grad = dot(tokens, back, 0, 0)
    grad = jnp.concatenate([grad[:, : 2 * half - 128], grad[:, 2 * half - 128 :] + vec_s[...]], axis=1)
    split_rows(first_core, grad, kept_ref, sent_ref, slice(None), w_rows)


def place_first_kernel(place_ref, *refs, pieces, down_rows):
    mine_refs, other_refs = refs[:pieces], refs[pieces : 2 * pieces]
    out_ref, down_ref = refs[2 * pieces :]
    out_rows, half = mine_refs[0].shape
    out_rows = out_rows - 2 * down_rows
    feat_rows = out_rows // FEATS

    def fill(cores):
        for index in range(pieces):
            for core in range(2):
                ref = cores[core][index]
                columns = slice(core * half, (core + 1) * half)
                for k in range(FEATS):
                    start = piece_row(place_ref, index, out_rows) + (place_ref[2] ^ k) * feat_rows
                    here = pl.ds(pl.multiple_of(start, 4), feat_rows)
                    out_ref[here, columns] = ref[k * feat_rows : (k + 1) * feat_rows, :]
                start = piece_row(place_ref, index, 2 * down_rows) + core * down_rows
                here = pl.ds(pl.multiple_of(start, 8), down_rows)
                down_ref[here, :half] = ref[out_rows : out_rows + down_rows, :]
                down_ref[here, half:] = ref[out_rows + down_rows :, :]

    @pl.when(place_ref[0] == 0)
    def _():
        fill((mine_refs, other_refs))

    @pl.when(place_ref[0] == 1)
    def _():
        fill((other_refs, mine_refs))


def place_second_kernel(place_ref, *refs, indices):
    pieces = len(indices)
    mine_refs, other_refs = refs[:pieces], refs[pieces : 2 * pieces]
    gate_ref, up_ref = refs[-2:]
    rows = mine_refs[0].shape[0]
    feat_rows = rows // FEATS

    def fill(gate_refs, up_refs):
        for position, index in enumerate(indices):
            for k in range(FEATS):
                start = piece_row(place_ref, index, rows) + (place_ref[2] ^ k) * feat_rows
                here = pl.ds(pl.multiple_of(start, 4), feat_rows)
                source = slice(k * feat_rows, (k + 1) * feat_rows)
                gate_ref[here, :] = gate_refs[position][source, :]
                up_ref[here, :] = up_refs[position][source, :]

    @pl.when(place_ref[0] == 0)
    def _():
        fill(mine_refs, other_refs)

    @pl.when(place_ref[0] == 1)
    def _():
        fill(other_refs, mine_refs)


def join_kernel(
    heads_ref, tokens_ref, w_ref, params_ref,
    attended_ref, norm_ref, low_ref, normed_ref, inverse_ref, *, heads,
):
    sides = []
    for side in range(2):
        lanes = slice(side * HEAD_DIM, (side + 1) * HEAD_DIM)
        pieces = [
            heads_ref[((h // 2) * FEATS + feat) * 2 + h % 2][:, lanes]
            for feat in range(FEATS)
            for h in range(heads)
        ]
        sides.append(jnp.concatenate(pieces, axis=1))
    attended = jnp.concatenate(sides, axis=0)
    attended_ref[...] = attended
    branch = dot(attended, w_ref[...])
    first, normed, inverse = norm_forward(
        tokens_ref[...].astype(f32) + branch + params_ref[2:3, :],
        params_ref[3:4, :],
        params_ref[4:5, :],
    )
    norm_ref[...] = first
    low_ref[...] = first.astype(bf16)
    normed_ref[...] = normed
    inverse_ref[...] = inverse


def part_kernel(
    place_ref, second_ref, own_ref, got_a_ref, got_b_ref, got_c_ref, normed_ref, inverse_ref,
    params_ref, w_ref, attended_ref,
    inner_ref, dout_ref, kept_ref, sent_ref, sums_ref, *, heads, rows,
):
    back_first = second_ref[...] + own_ref[...].astype(f32) + got_a_ref[...].astype(f32)
    back_first = back_first + got_b_ref[...].astype(f32) + got_c_ref[...].astype(f32)
    inner, gain_sum, shift_sum = norm_backward(
        back_first, normed_ref[...], inverse_ref[...], params_ref[3:4, :]
    )
    inner_ref[...] = inner
    branch = inner.astype(bf16)
    sums_ref[...] = jnp.concatenate(
        [jnp.sum(branch.astype(f32), axis=0, keepdims=True), gain_sum, shift_sum], axis=0
    )
    back = dot(branch, w_ref[...], 1, 1).astype(bf16)
    for slot in range(SLOTS):
        for feat in range(FEATS):
            start = (feat * heads + min(slot, heads - 1)) * HEAD_DIM
            piece = back[:, start : start + HEAD_DIM]
            dout_ref[((slot // 2) * FEATS + feat) * 2 + slot % 2] = jnp.concatenate(
                [piece[:rows], piece[rows:]], axis=1
            )
    half = branch.shape[1] // 2
    grad = dot(attended_ref[...], branch, 0, 0).astype(bf16)
    first_core = place_ref[0] == 0
    kept_ref[...] = jnp.where(first_core, grad[:, :half], grad[:, half:])
    sent_ref[...] = jnp.where(first_core, grad[:, half:], grad[:, :half])


def finish_kernel(parts_ref, query_ref, key_ref, value_ref, *refs, heads):
    vector_refs, vec_s = refs[:-1], refs[-1]
    groups = parts_ref.shape[0] // FEATS
    vec_s[...] = jnp.zeros_like(vec_s)
    w_rows = parts_ref.shape[1]
    half = heads * 2 * HEAD_DIM
    head_width = heads * HEAD_DIM
    vectors = jnp.zeros((w_rows, 128), f32)
    for feat in range(FEATS):
        total = parts_ref[feat].astype(f32)
        for group in range(1, groups):
            total = total + parts_ref[group * FEATS + feat].astype(f32)
        lanes = slice(feat * head_width, (feat + 1) * head_width)
        for index, ref in enumerate((query_ref, key_ref)):
            starts = [(2 * h + index) * HEAD_DIM for h in range(heads)]
            ref[:, lanes] = jnp.concatenate([total[:, at : at + HEAD_DIM] for at in starts], axis=1)
        value_ref[:, lanes] = total[:, half : half + head_width]
        vectors = vectors + total[:, 2 * half - 128 :]
    vec_s[:w_rows, :] = vectors
    turned = jnp.transpose(vec_s[...])
    for index, ref in enumerate(vector_refs):
        ref[...] = turned[index : index + 1, :w_rows]


def fold_kernel(
    place_ref, ff_kept_ref, ff_got_ref, down_kept_ref, down_got_ref, out_kept_ref, out_got_ref, *refs,
    units,
):
    ff_refs, down_refs, out_refs = refs[:2], refs[2 : 2 + units], refs[2 + units :]
    rows = ff_kept_ref.shape[0] // (2 * units)
    for k, ref in enumerate(ff_refs):
        for unit in range(units):
            start = (unit * 2 + (place_ref[1] ^ k)) * rows
            here = pl.ds(pl.multiple_of(start, 16), rows)
            value = ff_kept_ref[here, :].astype(f32) + ff_got_ref[here, :].astype(f32)
            ref[unit] = value.astype(bf16)
    for kept_ref, got_ref, moved_refs in (
        (down_kept_ref, down_got_ref, down_refs),
        (out_kept_ref, out_got_ref, out_refs),
    ):
        rows = kept_ref.shape[0] // units
        for k, ref in enumerate(moved_refs):
            here = pl.ds(pl.multiple_of((place_ref[3] ^ k) * rows, 16), rows)
            value = kept_ref[here, :].astype(f32) + got_ref[here, :].astype(f32)
            ref[...] = value.astype(bf16)


def finish_late_kernel(place_ref, *refs, ff_part):
    part_refs, (kept_ref, sent_ref) = refs[:FEATS], refs[FEATS:]
    w_rows = kept_ref.shape[0]
    total = part_refs[0][:, ff_part:].astype(f32)
    for part in part_refs[1:]:
        total = total + part[:, ff_part:].astype(f32)
    for core in range(2):

        @pl.when(place_ref[0] == core)
        def _():
            for ref, rows in (
                (kept_ref, slice(core * w_rows, (core + 1) * w_rows)),
                (sent_ref, slice((1 - core) * w_rows, (2 - core) * w_rows)),
            ):
                ref[:, FEATS * ff_part :] = total[rows].astype(bf16)
                for k in range(FEATS):
                    lanes = pl.ds(pl.multiple_of((place_ref[2] ^ k) * ff_part, 128), ff_part)
                    ref[:, lanes] = part_refs[k][rows, :ff_part]


def finish_wide_kernel(
    place_ref, kept_ref, got_ref, down_kept_ref, down_got_ref,
    gate_ref, up_ref, out_ref, down_ref, *, slots,
):
    total = gate_ref.shape[1]
    cols = total // (FEATS * slots)
    half = out_ref.shape[1] // 2

    def write(first, second, down_first, down_second):
        for source, target in ((first, gate_ref), (second, up_ref)):
            for slot in range(slots):
                pieces = []
                for feat in range(FEATS):
                    start = (feat * slots + slot) * cols
                    pieces.append(source[:, start : start + cols].astype(f32))
                start = slot * FEATS * cols
                target[:, start : start + FEATS * cols] = jnp.concatenate(pieces, axis=1)
        out_ref[:, :half] = first[:, total:].astype(f32)
        out_ref[:, half:] = second[:, total:].astype(f32)
        down_ref[:, :half] = down_first[...].astype(f32)
        down_ref[:, half:] = down_second[...].astype(f32)

    @pl.when(place_ref[0] == 0)
    def _():
        write(kept_ref, got_ref, down_kept_ref, down_got_ref)

    @pl.when(place_ref[0] == 1)
    def _():
        write(got_ref, kept_ref, down_got_ref, down_kept_ref)


def after(values, *others):
    return lax.optimization_barrier((values,) + others)[0]


def tie(*values):
    return lax.optimization_barrier(values)


def on_device(
    layer_input, segment_ids, token_live, w_query, b_query, w_key, w_value, b_value,
    w_output, b_output, first_gain, first_shift, w_gate, w_up, w_down, b_down,
    second_gain, second_shift, output_grad,
):
    units = lax.axis_size("u")
    unit, side, feat, core = (lax.axis_index(name) for name in ("u", "s", "f", "c"))
    devices = units * 2 * FEATS * 2
    sequences, rows, width = layer_input.shape
    length = rows * devices
    w_rows = w_query.shape[0]
    down_rows, ff_part = w_down.shape[0], w_gate.shape[1] // FEATS
    slots = units * 2
    heads = HEADS // FEATS
    head_width = heads * HEAD_DIM
    ranges = slots // SLOTS
    local = 2 * rows
    group = FEATS * local
    here = jnp.stack([core, side, feat, unit]).astype(jnp.int32)
    parts = slots

    def exchange_sides(values):
        kept = jnp.where(side == 0, values[0], values[1])
        got = swap(jnp.where(side == 0, values[1], values[0]), "s")
        return kept, got

    def to_tokens(values):
        kept, got = exchange_sides(values)
        return jnp.concatenate(
            [jnp.where(side == 0, kept, got), jnp.where(side == 0, got, kept)], axis=0
        )

    def from_tokens(values):
        kept, got = exchange_sides(values.reshape(2, rows, width))
        return jnp.stack([jnp.where(side == 0, kept, got), jnp.where(side == 0, got, kept)])

    def to_group(blocks):
        return all_to_all(blocks.reshape(-1, blocks.shape[-1]), ("f", "c"))

    def from_units(own, other_side, pin=None):
        pieces = [own, other_side]
        for k in range(1, units):
            for piece in (own, other_side):
                pieces.append(swap(piece if pin is None else after(piece, pin), "u", k))
        return pieces

    tokens = to_tokens(layer_input)

    vectors = [
        values.reshape(1, w_rows)
        for values in (
            b_query, b_value, b_output, first_gain, first_shift, b_down, second_gain, second_shift
        )
    ]
    half = heads * 2 * HEAD_DIM
    (early,) = call(
        functools.partial(pack_kernel, heads=heads),
        (jax.ShapeDtypeStruct((FEATS, 2, w_rows, half), bf16),),
        "pack_attn",
        "v" * 13,
        [pltpu.VMEM((128, 128), f32)],
    )(w_query, w_key, w_value, *vectors, segment_ids, token_live)
    token_parts = gather_feats(tokens)
    early_own = all_to_all(early.reshape(-1, half), ("f", "c"))
    others = range(1, units)
    early_side = swap(early_own, "s")
    early_near = [swap(early_own, "u", k) for k in others]
    early_far = [swap(early_side, "u", k) for k in others]

    def by_distance(own, other_side, near, far):
        pieces = [own, other_side]
        for index in range(units - 1):
            pieces += [near[index], far[index]]
        return pieces

    early_pieces = by_distance(early_own, early_side, early_near, early_far)
    early_others = [swap(piece, "c") for piece in early_pieces]

    late_cols = width // 2 + ff_part
    late_shape = jax.ShapeDtypeStruct((FEATS, w_rows, late_cols), bf16)
    late_kept, late_sent = call(
        functools.partial(pack_late_kernel, slots=slots), (late_shape, late_shape), "pack_late", "svvv"
    )(here, w_output, w_gate, w_up)
    routed = call(
        route_kernel,
        (jax.ShapeDtypeStruct((2 * w_rows, late_cols), bf16),) * FEATS,
        "route_late",
        "svv",
    )(here, late_kept, swap(after(late_sent, early_own), "c"))
    out_half = width // 2
    routed = [after(piece, token_parts[1]) for piece in routed]
    late_feats = [routed[0]] + [swap(routed[k], "f", k) for k in range(1, FEATS)]
    here_qkv, *late_feats = tie(here, *late_feats)
    first_own = jnp.concatenate(
        [piece[:, :out_half] for piece in late_feats] + [w_down[:, :out_half], w_down[:, out_half:]]
    )
    second_own = jnp.concatenate([piece[:, out_half:] for piece in late_feats])
    others = range(1, units)

    sent, w_attn, params, seg_row, code_row = call(
        functools.partial(qkv_kernel, w_rows=w_rows, rows=rows, heads=heads, pieces=parts),
        (
            jax.ShapeDtypeStruct((slots, group * 3 // 2, 2 * HEAD_DIM), bf16),
            jax.ShapeDtypeStruct((width, 2 * half), bf16),
            jax.ShapeDtypeStruct((8, width), f32),
            jax.ShapeDtypeStruct((1, length), f32),
            jax.ShapeDtypeStruct((1, length), f32),
        ),
        "qkv",
        "s" + "v" * (2 * parts + FEATS),
        [pltpu.VMEM((width, 128), f32)] * 2,
    )(here_qkv, *early_pieces, *early_others, *token_parts)
    qkv = all_to_all(sent.reshape(-1, 2 * HEAD_DIM), ("u", "c"))
    first_side = swap(first_own, "s")
    first_units = [swap(first_own, "u", k) for k in others]
    first_swaps = [swap(piece, "c") for piece in [first_own, first_side] + first_units]
    second_swaps = [swap(second_own, "c")]
    qkv, first_side, second_swaps[0], *moved = tie(
        qkv, first_side, second_swaps[0], *first_units, *first_swaps
    )
    first_units, first_swaps = moved[: units - 1], moved[units - 1 :]
    qkv = qkv.reshape(sent.shape)

    blocks = length // BLOCK
    slot_self = unit * 2 + core
    range_self = slot_self // SLOTS
    head_self = feat * heads + jnp.minimum(slot_self % SLOTS, heads - 1)
    slope = jnp.asarray(alibi_slopes(HEADS))[head_self].reshape(1, 1)
    seg_blocks = seg_row.reshape(blocks, BLOCK)
    seg_low, seg_high = seg_blocks[:, 0], seg_blocks[:, -1]
    key_low = jnp.sum(seg_high[None, :] < seg_low[:, None], axis=1, dtype=jnp.int32)
    key_high = jnp.sum(seg_low[None, :] <= seg_high[:, None], axis=1, dtype=jnp.int32)
    own = jnp.stack(
        [feat, range_self * (blocks // ranges), (range_self + 1) * (blocks // ranges)]
    ).astype(jnp.int32)
    table = jnp.stack([key_low, key_high, jnp.pad(own, (0, blocks - 3))])
    second_side = swap(second_own, "s")
    second_units = [swap(second_own, "u", k) for k in others]
    first_far = [swap(first_side, "u", k) for k in others]
    out_blocks, lse, o_turned = attend(table, slope, qkv, seg_row, code_row)
    out_blocks, second_side, *moved = tie(out_blocks, second_side, *second_units, *first_far)
    second_units, first_far = moved[: units - 1], moved[units - 1 :]
    second_far = [swap(second_side, "u", k) for k in others]
    first_swaps += [swap(piece, "c") for piece in first_far]
    second_swaps += [swap(piece, "c") for piece in [second_side] + second_units]

    first_pieces = by_distance(first_own, first_side, first_units, first_far)
    first_others = by_distance(
        first_swaps[0], first_swaps[1], first_swaps[2 : 1 + units], first_swaps[1 + units :]
    )
    aligned = w_rows % 8 == 0

    def in_rows(pieces, feats):
        cols = pieces[0].shape[1]
        values = jnp.stack(pieces).reshape(units, 2, feats, -1, cols)
        values = jnp.take(values, jnp.arange(units) ^ unit, axis=0)
        values = jnp.take(values, jnp.arange(2) ^ side, axis=1)
        if feats == FEATS:
            values = jnp.take(values, jnp.arange(FEATS) ^ feat, axis=2)
        return values.reshape(-1, cols)

    def by_core(mine, others_):
        mine, others_ = in_rows(mine, FEATS), in_rows(others_, FEATS)
        return jnp.where(core == 0, mine, others_), jnp.where(core == 0, others_, mine)

    if aligned:
        full_output, full_down = call(
            functools.partial(place_first_kernel, pieces=parts, down_rows=down_rows),
            (
                jax.ShapeDtypeStruct((width, width), bf16),
                jax.ShapeDtypeStruct((ff_part, width), bf16),
            ),
            "place_first",
            "s" + "v" * 2 * parts,
        )(here, *first_pieces, *first_others)
    else:
        out_rows = 2 * FEATS * w_rows
        full_output = jnp.concatenate(
            by_core([p[:out_rows] for p in first_pieces], [p[:out_rows] for p in first_others]), axis=1
        )

        def down_of(pieces):
            return in_rows(
                [
                    jnp.concatenate([p[out_rows : out_rows + down_rows], p[out_rows + down_rows :]], axis=1)
                    for p in pieces
                ],
                1,
            ).reshape(slots, down_rows, width)

        down_mine, down_others = down_of(first_pieces), down_of(first_others)
        full_down = jnp.stack(
            [jnp.where(core == 0, down_mine, down_others), jnp.where(core == 0, down_others, down_mine)],
            axis=1,
        ).reshape(ff_part, width)

    heads_in = all_to_all(out_blocks.reshape(-1, 2 * HEAD_DIM), ("u", "f", "c"))
    heads_in, *second_swaps[1:] = tie(heads_in, *second_swaps[1:])
    heads_in = heads_in.reshape(ranges, SLOTS * FEATS, rows, 2 * HEAD_DIM)
    if ranges > 1:
        heads_in = lax.dynamic_index_in_dim(heads_in, unit * 2 // SLOTS, 0, keepdims=False)
    else:
        heads_in = heads_in[0]
    attended, first_norm, first_low_own, normed_one, inverse_one = call(
        functools.partial(join_kernel, heads=heads),
        (
            jax.ShapeDtypeStruct((local, width), bf16),
            jax.ShapeDtypeStruct((local, width), f32),
            jax.ShapeDtypeStruct((local, width), bf16),
            jax.ShapeDtypeStruct((local, width), f32),
            jax.ShapeDtypeStruct((local, 1), f32),
        ),
        "join_heads",
        "vvvv",
    )(heads_in, tokens, full_output, params)

    first_low_own, *second_far = tie(first_low_own, *second_far)
    second_swaps += [swap(piece, "c") for piece in second_far]
    ff_square = jax.ShapeDtypeStruct((width, ff_part), bf16)
    indices = [0, 1] + [2 * k for k in others] + [2 * k + 1 for k in others]
    second_pieces = [second_own, second_side, *second_units, *second_far]
    if aligned:
        full_gate, full_up = call(
            functools.partial(place_second_kernel, indices=indices),
            (ff_square, ff_square),
            "place_second",
            "s" + "v" * 2 * parts,
        )(here, *second_pieces, *second_swaps)
    else:
        order = [indices.index(position) for position in range(parts)]
        full_gate, full_up = by_core(
            [second_pieces[position] for position in order],
            [second_swaps[position] for position in order],
        )
    low_parts = gather_feats(first_low_own)
    full_gate, full_up, *low_parts = tie(full_gate, full_up, *low_parts)
    first_low = jnp.concatenate(low_parts, axis=0)
    gate_rows = dot(first_low, full_gate)
    up_rows = dot(first_low, full_up)
    spread = 0.5 * (1.0 + lax.erf(gate_rows * (0.5**0.5)))
    gelu = gate_rows * spread
    hidden = (gelu * up_rows).astype(bf16)
    partial_mixed = dot(hidden, full_down).astype(bf16).reshape(FEATS, local, width)
    partial_mixed, gate_kept, up_kept = tie(partial_mixed, gate_rows, up_rows)
    mixed_got = [swap(partial_mixed[k], "f", k) for k in range(1, FEATS)]
    spread = 0.5 * (1.0 + lax.erf(gate_kept * (0.5**0.5)))
    density = jnp.exp(-0.5 * gate_kept * gate_kept) * (1.0 / math.sqrt(2.0 * math.pi))
    gate_factor = (up_kept * (spread + gate_kept * density)).astype(bf16)
    up_factor = (gate_kept * spread).astype(bf16)
    bias_down, gate_factor, up_factor = tie(params[5], gate_factor, up_factor)
    mixed = partial_mixed[0].astype(f32) + bias_down
    for piece in mixed_got:
        mixed = mixed + piece.astype(f32)
    gain_two = params[6]
    layer_wide, normed_two, inverse_two = norm_forward(first_norm + mixed, gain_two, params[7])

    upstream = to_tokens(after(output_grad, out_blocks)).astype(f32)
    back_second, grad_gain_two, grad_shift_two = norm_backward(
        upstream, normed_two, inverse_two, gain_two
    )
    back_low = back_second.astype(bf16)
    grad_down_bias = jnp.sum(back_low.astype(f32), axis=0, keepdims=True)
    back_mixed = jnp.concatenate(gather_feats(back_low), axis=0)
    back_hidden = dot(back_mixed, full_down, 1, 1)
    back_gate = (back_hidden * gate_factor.astype(f32)).astype(bf16)
    back_up = (back_hidden * up_factor.astype(f32)).astype(bf16)
    partial_first = (dot(back_gate, full_gate, 1, 1) + dot(back_up, full_up, 1, 1)).astype(bf16)
    partial_first = partial_first.reshape(FEATS, local, width)
    partial_got = [swap(partial_first[k], "f", k) for k in range(1, FEATS)]
    partial_got[0], back_gate, back_up, back_mixed = tie(partial_got[0], back_gate, back_up, back_mixed)
    half_width = width // 2

    def chosen(first, second):
        return jnp.where(core == 0, first, second)

    left, right = back_mixed[:, :half_width], back_mixed[:, half_width:]

    def outer(rows_side, cols_side):
        return dot(cols_side, rows_side, 0, 0).astype(bf16).T

    ff_sent = outer(first_low, chosen(back_up, back_gate))
    down_sent = outer(hidden, chosen(right, left))
    ff_kept = outer(first_low, chosen(back_gate, back_up))
    down_kept = outer(hidden, chosen(left, right))
    here_join, ff_sent, down_sent, ff_kept, down_kept = tie(here, ff_sent, down_sent, ff_kept, down_kept)
    inner_shape = jax.ShapeDtypeStruct((local, width), f32)
    back_inner, dout_blocks, out_kept, out_sent, sums_one = call(
        functools.partial(part_kernel, heads=heads, rows=rows),
        (
            inner_shape,
            jax.ShapeDtypeStruct((SLOTS * FEATS, rows, 2 * HEAD_DIM), bf16),
            jax.ShapeDtypeStruct((width, half_width), bf16),
            jax.ShapeDtypeStruct((width, half_width), bf16),
            jax.ShapeDtypeStruct((3, width), f32),
        ),
        "back_join",
        "s" + "v" * 10,
    )(
        here_join, back_second, partial_first[0], *partial_got, normed_one, inverse_one, params,
        full_output, attended,
    )
    dout_sent = jnp.broadcast_to(dout_blocks[None], (ranges,) + dout_blocks.shape)
    dout = all_to_all(dout_sent.reshape(-1, 2 * HEAD_DIM), ("u", "f", "c"))
    dout = dout.reshape(slots * FEATS, rows, 2 * HEAD_DIM)

    def fold(values, axis):
        return scatter_axis(values, axis).astype(bf16)

    def added(kept, got):
        return (kept.astype(f32) + got.astype(f32)).astype(bf16)

    out_got = swap(out_sent, "c")
    ff_got, down_got = (swap(after(values, *partial_got), "c") for values in (ff_sent, down_sent))

    def parts_of(values, axis):
        size, me = lax.axis_size(axis), lax.axis_index(axis)
        if size == 2:
            return [jnp.where(me == 0, values[0], values[1]), jnp.where(me == 0, values[1], values[0])]
        return [lax.dynamic_index_in_dim(values, me ^ k, 0, keepdims=False) for k in range(size)]

    def send(values, axis):
        own, *rest = parts_of(values, axis)
        return own, [swap(piece, axis, k + 1) for k, piece in enumerate(rest)]

    def total(own, got):
        result = own.astype(f32)
        for piece in got:
            result = result + piece.astype(f32)
        return result

    def sides(values):
        return jnp.moveaxis(values.reshape(units, 2, -1, values.shape[-1]), 1, 0)

    def by_unit(values):
        return values.reshape(units, -1, values.shape[-1])

    def part(values, member):
        return lax.dynamic_index_in_dim(values, member, 0, keepdims=False)

    def send_sum(kept, got, axis):
        me = lax.axis_index(axis)
        moved = [
            swap(added(part(kept, me ^ k), part(got, me ^ k)), axis, k)
            for k in range(1, lax.axis_size(axis))
        ]
        return [part(kept, me), part(got, me)], moved

    ff_own, ff_moved = send_sum(sides(ff_kept), sides(ff_got), "s")
    down_own, down_moved = send_sum(by_unit(down_kept), by_unit(down_got), "u")
    out_own, out_moved = send_sum(by_unit(out_kept), by_unit(out_got), "u")
    dqkv = attend_back(table, slope, qkv, dout, o_turned, lse, seg_row, code_row)
    dqkv, *moved = tie(dqkv, *ff_moved, *down_moved, *out_moved)
    ff_moved, down_moved, out_moved = moved[:1], moved[1:units], moved[units:]
    grad_down = total(down_own[0], down_own[1:] + down_moved).astype(bf16).reshape(2, 2 * down_rows, -1)
    grad_out = total(out_own[0], out_own[1:] + out_moved).astype(bf16).reshape(2, FEATS * 2 * w_rows, -1)
    grad_down, down_moved = send(grad_down, "s")
    dqkv = all_to_all(dqkv.reshape(-1, 2 * HEAD_DIM), ("u", "c"))
    dqkv, down_moved[0] = tie(dqkv, down_moved[0])
    grad_ff = total(ff_own[0], ff_own[1:] + ff_moved).astype(bf16)
    grad_ff, ff_moved = send(after(grad_ff, dqkv), "u")
    grad_out, out_moved = send(after(grad_out, dqkv), "s")
    dqkv = dqkv.reshape(ranges, SLOTS, group * 3 // 2, 2 * HEAD_DIM)
    if ranges > 1:
        dqkv = jnp.sum(dqkv.astype(f32), axis=0).astype(bf16)
    else:
        dqkv = dqkv[0]
    vector_sums = jnp.concatenate([sums_one, grad_down_bias, grad_gain_two, grad_shift_two], axis=0)
    attn_shape = jax.ShapeDtypeStruct((slots * FEATS, w_rows, 2 * half), bf16)
    back_projected, attn_kept, attn_sent = call(
        functools.partial(grad_qkv_kernel, heads=heads, w_rows=w_rows),
        (jax.ShapeDtypeStruct((group, 2 * half), bf16), attn_shape, attn_shape),
        "grad_qkv",
        "s" + "v" * (FEATS + 2),
        [pltpu.VMEM((128, width), f32), pltpu.VMEM((width, 128), f32)],
    )(here, *token_parts, dqkv, vector_sums)
    attn_sent, back_projected = tie(attn_sent, back_projected)
    partial_input = dot(back_projected, w_attn, 1, 1).astype(bf16).reshape(FEATS, local, width)
    grad_attn = added(attn_kept, swap(attn_sent, "c"))
    grad_attn, partial_input = tie(grad_attn, partial_input)
    grad_attn = grad_attn.reshape(-1, 2 * half)
    grad_down = total(grad_down, down_moved).reshape(2, down_rows, half_width)
    layer_wide_low = after(layer_wide.astype(bf16), grad_attn)
    grad_attn = all_to_all(grad_attn, ("u", "s", "f"))
    input_got = [swap(partial_input[k], "f", k) for k in range(1, FEATS)]
    grad_ff = total(grad_ff, ff_moved)
    grad_out = total(grad_out, out_moved)
    grad_late = jnp.concatenate([grad_ff, grad_out], axis=1).astype(bf16)
    grad_late = grad_late.reshape(FEATS, 2 * w_rows, ff_part + half_width)
    late_got = [lax.dynamic_index_in_dim(grad_late, feat ^ k, 0, keepdims=False) for k in range(FEATS)]
    back_inner, *late_got = tie(back_inner, *late_got)
    late_got = late_got[:1] + [swap(late_got[k], "f", k) for k in range(1, FEATS)]
    input_sum = back_inner + partial_input[0].astype(f32)
    for piece in input_got:
        input_sum = input_sum + piece.astype(f32)
    input_grad = from_tokens(input_sum.astype(bf16))
    layer_output = from_tokens(layer_wide_low)

    wide_shape = jax.ShapeDtypeStruct((w_rows, FEATS * ff_part + half_width), bf16)
    wide_kept, wide_sent = call(
        functools.partial(finish_late_kernel, ff_part=ff_part),
        (wide_shape, wide_shape),
        "finish_late",
        "s" + "v" * FEATS,
    )(here, *late_got)
    wide_got = swap(wide_sent, "c")
    down_kept = chosen(grad_down[0], grad_down[1])
    down_got = swap(chosen(grad_down[1], grad_down[0]).astype(bf16), "c")
    ff_out_shape = jax.ShapeDtypeStruct((w_rows, FEATS * ff_part), f32)
    grad_gate, grad_up, grad_output, grad_down = call(
        functools.partial(finish_wide_kernel, slots=slots),
        (
            ff_out_shape,
            ff_out_shape,
            jax.ShapeDtypeStruct((w_rows, width), f32),
            jax.ShapeDtypeStruct((down_rows, width), f32),
        ),
        "finish_wide",
        "svvvv",
    )(here, wide_kept, wide_got, down_kept, down_got)
    matrix_shape = jax.ShapeDtypeStruct((w_rows, width), f32)
    grad_query, grad_key, grad_value, *vectors_out = call(
        functools.partial(finish_kernel, heads=heads),
        (matrix_shape,) * 3 + (jax.ShapeDtypeStruct((1, w_rows), f32),) * 8,
        "finish",
        "v",
        [pltpu.VMEM((128, 128), f32)],
    )(grad_attn.reshape(slots * FEATS, w_rows, 2 * half))
    vectors_out = [values.reshape(w_rows) for values in vectors_out]
    return (
        layer_output, input_grad, grad_query, vectors_out[0], grad_key, grad_value,
        vectors_out[1], grad_output, vectors_out[2], vectors_out[3], vectors_out[4],
        grad_gate, grad_up, grad_down, vectors_out[5], vectors_out[6], vectors_out[7],
    )


def solution(mesh):
    devices = mesh.devices
    names = ("u", "s", "f", "c")
    inner = Mesh(devices.reshape(devices.size // (4 * FEATS), 2, FEATS, 2), names)
    tokens, matrix, vector = P(None, names, None), P(names, None), P(names)
    ids = P(None, names)
    return jax.shard_map(
        on_device,
        mesh=inner,
        in_specs=(
            tokens, ids, ids, matrix, vector, matrix, matrix, vector, matrix, vector, vector,
            vector, matrix, matrix, matrix, vector, vector, vector, tokens,
        ),
        out_specs=(
            tokens, tokens, matrix, vector, matrix, matrix, vector, matrix, vector, vector,
            vector, matrix, matrix, matrix, vector, vector, vector,
        ),
        check_vma=False,
    )
```

```python
import functools
import math

import jax
import jax.numpy as jnp
import numpy as np
from jax import lax
from jax.experimental import pallas as pl
from jax.experimental.pallas import tpu as pltpu
from jax.sharding import Mesh
from jax.sharding import PartitionSpec as P

HEADS = 12
HEAD_DIM = 64
FEATS = 4
SLOTS = 4
PACK = 4 * HEAD_DIM
BLOCK = 256

norm_epsilon = 1e-12
masked_value = -1e30
f32 = jnp.float32
bf16 = jnp.bfloat16


def alibi_slopes(head_total):
    nearest = 2 ** int(math.floor(math.log2(head_total)))
    slopes = [2.0 ** (-8.0 * (index + 1) / nearest) for index in range(nearest)]
    extra = [2.0 ** (-8.0 * (index + 1) / (2 * nearest)) for index in range(2 * nearest)]
    slopes = slopes + extra[0::2][: head_total - nearest]
    return np.array(slopes, dtype=np.float32)


def dot(left, right, left_dim=1, right_dim=0):
    return lax.dot_general(
        left, right, (((left_dim,), (right_dim,)), ((), ())), preferred_element_type=f32
    )


def swap(values, axis, step=1):
    size = lax.axis_size(axis)
    return lax.ppermute(values, axis, [(i, i ^ step) for i in range(size)])


def in_order(parts, me):
    if len(parts) == 2:
        mine, other = parts
        return jnp.stack([jnp.where(me == 0, mine, other), jnp.where(me == 0, other, mine)])
    return jnp.take(jnp.stack(parts), jnp.arange(len(parts)) ^ me, axis=0)


def gather_axis(values, axis):
    size = lax.axis_size(axis)
    parts = [values] + [swap(values, axis, k) for k in range(1, size)]
    return in_order(parts, lax.axis_index(axis))


def scatter_axis(values, axis):
    size = lax.axis_size(axis)
    me = lax.axis_index(axis)

    def pick(k):
        if size == 2:
            return jnp.where((me ^ k) == 0, values[0], values[1])
        return lax.dynamic_index_in_dim(values, me ^ k, 0, keepdims=False)

    total = pick(0)
    for k in range(1, size):
        total = total + swap(pick(k).astype(bf16), axis, k).astype(f32)
    return total


def gather_feats(values):
    return [values] + [swap(values, "f", k) for k in range(1, FEATS)]


def scatter_feats(values):
    rows = values.shape[0] // FEATS
    total = values[:rows]
    for k in range(1, FEATS):
        total = total + swap(values[k * rows : (k + 1) * rows].astype(bf16), "f", k).astype(f32)
    return total


def all_to_all(values, axes):
    return lax.all_to_all(values, axes, split_axis=0, concat_axis=0, tiled=True)


def place(unit, side, feat, core, rows):
    return (((unit * 2 + side) * FEATS + feat) * 2 + core) * rows


def unpack_qkv(qkv_ref, nat_s, feat, rows):
    slots, lines, _ = qkv_ref.shape
    group = 2 * FEATS * rows
    nothing = jnp.zeros((rows, HEAD_DIM), bf16)
    for slot in range(slots):
        for k in range(FEATS):
            for side in range(2):
                here = pl.ds(
                    pl.multiple_of(place(slot // 2, side, feat ^ k, slot % 2, rows), rows), rows
                )
                start = (2 * k + side) * rows
                nat_s[here, :128] = qkv_ref[slot, start : start + rows, :]
                start = group + (2 * (k % 2) + side) * rows
                lanes = slice((k // 2) * HEAD_DIM, (k // 2 + 1) * HEAD_DIM)
                value = qkv_ref[slot, start : start + rows, lanes]
                nat_s[here, 128:] = jnp.concatenate([value, nothing], axis=1)


def turn(values):
    return jnp.transpose(values.astype(f32))


def spread_codes(code_ref, code_s):
    for start in range(0, code_ref.shape[1], 128):
        row = code_ref[:, start : start + 128]
        code_s[start : start + 128, :] = jnp.transpose(jnp.broadcast_to(row, (128, 128)))


def distance_tile():
    rows = lax.broadcasted_iota(jnp.int32, (BLOCK, BLOCK), 0)
    cols = lax.broadcasted_iota(jnp.int32, (BLOCK, BLOCK), 1)
    return (cols - rows).astype(f32)


def span(index):
    return pl.ds(pl.multiple_of(index * BLOCK, BLOCK), BLOCK)


def even_range(low, high, first, last):
    low, high = jnp.maximum(low, first), jnp.minimum(high, last)
    high = jnp.maximum(low, high)
    odd = (high - low) % 2
    up = odd * (high < last).astype(jnp.int32)
    low = low - (odd - up)
    return low, (high + up - low) // 2


def score_tile(qk_part, qz_part, code_part, seg_part, tile, q_block, k_block, slope, diagonal):
    codes = jnp.concatenate([code_part] * (BLOCK // 128), axis=1)
    allowed = codes == seg_part
    if diagonal:
        distance = tile
    else:
        distance = tile + ((q_block - k_block) * BLOCK).astype(f32)
    if diagonal is False:
        fall = distance * jnp.where(q_block > k_block, slope, -slope)
    else:
        fall = jnp.abs(distance) * slope
        allowed = allowed | (distance == 0.0)
    return jnp.where(allowed, dot(qk_part, qz_part) - fall, masked_value)


def pair_plan(index, low, high, blocks):
    odd = (high - low) % 2
    up = odd * (high < blocks).astype(jnp.int32)
    low, high = low - (odd - up), high + up
    at_low = (low == index).astype(jnp.int32)
    partner = low + at_low
    base = low + 1 + at_low

    def member(t):
        here = base + t
        return here + ((here >= index) & (at_low == 0)).astype(jnp.int32)

    return partner, (high - low - 2) // 2, member


def score_tile_plain(qk_part, qz_part, code_part, seg_part, offset, slope):
    distance = distance_tile() + offset
    scores = dot(qk_part, qz_part) - slope * jnp.abs(distance)
    codes = jnp.concatenate([code_part] * (BLOCK // 128), axis=1)
    allowed = (codes == seg_part) | (distance == 0.0)
    return jnp.where(allowed, scores, masked_value)


def attend_kernel(
    table_ref, slope_ref, qkv_ref, seg_ref, code_ref, out_ref, lse_ref, ot_ref,
    nat_s, qz_s, vt_s, o_s, code_s,
):
    slope = slope_ref[0, 0]
    units = qkv_ref.shape[0] // 2
    rows = out_ref.shape[1]
    unpack_qkv(qkv_ref, nat_s, table_ref[2, 0], rows)
    spread_codes(code_ref, code_s)
    length = nat_s.shape[0]
    blocks = length // BLOCK
    qz_s[:HEAD_DIM, :] = jnp.zeros((HEAD_DIM, length), bf16)
    for start in range(0, length, 128):
        here = slice(start, start + 128)
        qk_turned = turn(nat_s[here, :128])
        qz_s[HEAD_DIM:, here] = (qk_turned[:HEAD_DIM] * (HEAD_DIM**-0.5)).astype(bf16)
        vt_s[:, here] = turn(nat_s[here, 128:])[:HEAD_DIM].astype(bf16)
    if qkv_ref.shape[0] > SLOTS:
        o_s[...] = jnp.zeros_like(o_s)
        ot_ref[...] = jnp.zeros_like(ot_ref)
        lse_ref[...] = jnp.zeros_like(lse_ref)


    def query_step(i, carry):
        here = span(i)
        qz_part = qz_s[:, here]
        seg_part = seg_ref[:, here]
        partner, pairs, member = pair_plan(i, table_ref[0, i], table_ref[1, i], blocks)

        def scores_of(j, diagonal):
            return score_tile(
                nat_s[span(j), :128], qz_part, code_s[span(j), :], seg_part, distance_tile(), i, j,
                slope, diagonal,
            )

        def mixed_of(j, probs):
            return dot(vt_s[:, span(j)], probs.astype(bf16))

        def highest(scores):
            return jnp.maximum(*(jnp.max(values, axis=0, keepdims=True) for values in scores))

        def key_step(pair, state):
            top, total, mixed = state
            keys = [member(2 * pair), member(2 * pair + 1)]
            scores = [scores_of(j, False) for j in keys]
            top_new = jnp.maximum(top, highest(scores))
            factor = jnp.exp(top - top_new)
            probs = [jnp.exp(values - top_new) for values in scores]
            total = total * factor + jnp.sum(probs[0] + probs[1], axis=0, keepdims=True)
            mixed = mixed * factor + (mixed_of(keys[0], probs[0]) + mixed_of(keys[1], probs[1]))
            return top_new, total, mixed

        scores = [scores_of(i, True), scores_of(partner, False)]
        top = highest(scores)
        probs = [jnp.exp(values - top) for values in scores]
        total = jnp.sum(probs[0] + probs[1], axis=0, keepdims=True)
        mixed = mixed_of(i, probs[0]) + mixed_of(partner, probs[1])
        top, total, mixed = lax.fori_loop(0, pairs, key_step, (top, total, mixed))
        mixed = mixed / total
        ot_ref[:, here] = mixed
        lse_ref[:, here] = top + jnp.log(total)
        o_s[here, :] = jnp.transpose(mixed)
        return carry

    lax.fori_loop(table_ref[2, 1], table_ref[2, 2], query_step, 0)
    for unit in range(units):
        for feat in range(FEATS):
            for core in range(2):
                starts = [place(unit, side, feat, core, rows) for side in range(2)]
                sides = [o_s[start : start + rows, :] for start in starts]
                out_ref[(unit * FEATS + feat) * 2 + core] = jnp.concatenate(sides, axis=1).astype(bf16)


def attend_back_kernel(
    table_ref, slope_ref, qkv_ref, dout_ref, ot_ref, lse_ref, seg_ref, code_ref, dqkv_ref,
    nat_s, qz_s, kt_s, do_s, dz_s, code_s, delta_s, dqt_s, dq_s, dk_s, dv_s,
):
    slope = slope_ref[0, 0]
    feat_self = table_ref[2, 0]
    first, last = table_ref[2, 1], table_ref[2, 2]
    slots, rows = qkv_ref.shape[0], dout_ref.shape[1]
    group = 2 * FEATS * rows
    length = nat_s.shape[0]
    blocks = length // BLOCK
    unpack_qkv(qkv_ref, nat_s, feat_self, rows)
    spread_codes(code_ref, code_s)
    for unit in range(slots // 2):
        for feat in range(FEATS):
            for core in range(2):
                piece = dout_ref[(unit * FEATS + feat) * 2 + core]
                for side in range(2):
                    start = place(unit, side, feat, core, rows)
                    do_s[start : start + rows, :] = piece[:, side * HEAD_DIM : (side + 1) * HEAD_DIM]
    zero_half = jnp.zeros((HEAD_DIM, length), bf16)
    qz_s[:HEAD_DIM, :] = zero_half
    dz_s[HEAD_DIM:, :] = zero_half
    dqt_s[...] = jnp.zeros_like(dqt_s)
    for start in range(0, length, 128):
        here = slice(start, start + 128)
        qk_turned = turn(nat_s[here, :128])
        qz_s[HEAD_DIM:, here] = (qk_turned[:HEAD_DIM] * (HEAD_DIM**-0.5)).astype(bf16)
        kt_s[:, here] = qk_turned[HEAD_DIM:].astype(bf16)
        do_turned = turn(do_s[here, :])
        dz_s[:HEAD_DIM, here] = do_turned.astype(bf16)
        delta_s[:, here] = jnp.sum(do_turned * ot_ref[:, here], axis=0, keepdims=True)

    def key_step(j, carry):
        there = span(j)
        qk_part, vx_part = nat_s[there, :128], nat_s[there, 128:]
        code_part, kt_part = code_s[there, :], kt_s[:, there]
        low, pairs = even_range(table_ref[0, j], table_ref[1, j], first, last)

        def query_step(pair, state):
            dk, dv = state
            for i in (low + 2 * pair, low + 2 * pair + 1):
                here = span(i)
                scores = score_tile_plain(
                    qk_part, qz_s[:, here], code_part, seg_ref[:, here],
                    ((i - j) * BLOCK).astype(f32), slope,
                )
                probs = jnp.exp(scores - lse_ref[:, here])
                back_probs = dot(vx_part, dz_s[:, here])
                back_scores = (probs * (back_probs - delta_s[:, here])).astype(bf16)
                dv = dv + dot(probs.astype(bf16), do_s[here, :])
                dk = dk + dot(back_scores, nat_s[here, :HEAD_DIM])
                dqt_s[:, here] += dot(kt_part, back_scores)
            return dk, dv

        zero = jnp.zeros((BLOCK, HEAD_DIM), f32)
        dk, dv = lax.fori_loop(0, pairs, query_step, (zero, zero))
        dk_s[there, :] = dk
        dv_s[there, :] = dv
        return carry

    lax.fori_loop(0, blocks, key_step, 0)
    for start in range(0, length, 128):
        here = slice(start, start + 128)
        dq_s[here, :] = jnp.transpose(dqt_s[:, here])
    for slot in range(slots):
        for k in range(FEATS):
            for side in range(2):
                here = pl.ds(
                    pl.multiple_of(place(slot // 2, side, feat_self ^ k, slot % 2, rows), rows), rows
                )
                start = (2 * k + side) * rows
                both = jnp.concatenate([dq_s[here, :], dk_s[here, :]], axis=1) * (HEAD_DIM**-0.5)
                dqkv_ref[slot, start : start + rows, :] = both.astype(bf16)
                start = group + (2 * (k % 2) + side) * rows
                lanes = slice((k // 2) * HEAD_DIM, (k // 2 + 1) * HEAD_DIM)
                dqkv_ref[slot, start : start + rows, lanes] = dv_s[here, :].astype(bf16)


def attend(table, slope, qkv, seg_row, code_row):
    slots, length = qkv.shape[0], seg_row.shape[1]
    rows = length // (slots * FEATS * 2)
    vmem = pl.BlockSpec(memory_space=pltpu.VMEM)
    smem = pl.BlockSpec(memory_space=pltpu.SMEM)
    return pl.pallas_call(
        attend_kernel,
        out_shape=(
            jax.ShapeDtypeStruct((slots * FEATS, rows, 2 * HEAD_DIM), bf16),
            jax.ShapeDtypeStruct((1, length), f32),
            jax.ShapeDtypeStruct((HEAD_DIM, length), f32),
        ),
        in_specs=[smem, smem, vmem, vmem, vmem],
        out_specs=(vmem, vmem, vmem),
        scratch_shapes=[
            pltpu.VMEM((length, PACK), bf16),
            pltpu.VMEM((2 * HEAD_DIM, length), bf16),
            pltpu.VMEM((HEAD_DIM, length), bf16),
            pltpu.VMEM((length, HEAD_DIM), f32),
            pltpu.VMEM((length, 128), f32),
        ],
        name="attend",
    )(table, slope, qkv, seg_row, code_row)


def attend_back(table, slope, qkv, dout, o_turned, lse, seg_row, code_row):
    slots, length = qkv.shape[0], seg_row.shape[1]
    rows = length // (slots * FEATS * 2)
    vmem = pl.BlockSpec(memory_space=pltpu.VMEM)
    smem = pl.BlockSpec(memory_space=pltpu.SMEM)
    return pl.pallas_call(
        attend_back_kernel,
        out_shape=jax.ShapeDtypeStruct(qkv.shape, bf16),
        in_specs=[smem, smem] + [vmem] * 6,
        out_specs=vmem,
        scratch_shapes=[
            pltpu.VMEM((length, PACK), bf16),
            pltpu.VMEM((2 * HEAD_DIM, length), bf16),
            pltpu.VMEM((HEAD_DIM, length), bf16),
            pltpu.VMEM((length, HEAD_DIM), bf16),
            pltpu.VMEM((2 * HEAD_DIM, length), bf16),
            pltpu.VMEM((length, 128), f32),
            pltpu.VMEM((1, length), f32),
            pltpu.VMEM((HEAD_DIM, length), f32),
            pltpu.VMEM((length, HEAD_DIM), f32),
            pltpu.VMEM((length, HEAD_DIM), f32),
            pltpu.VMEM((length, HEAD_DIM), f32),
        ],
        name="attend_back",
    )(table, slope, qkv, dout, o_turned, lse, seg_row, code_row)


def norm_forward(values, gain, shift):
    centred = values - jnp.mean(values, axis=-1, keepdims=True)
    inverse = lax.rsqrt(jnp.mean(centred * centred, axis=-1, keepdims=True) + norm_epsilon)
    normed = centred * inverse
    return normed * gain + shift, normed, inverse


def norm_backward(upstream, normed, inverse, gain):
    scaled = upstream * gain
    adjusted = (
        scaled
        - jnp.mean(scaled, axis=-1, keepdims=True)
        - normed * jnp.mean(scaled * normed, axis=-1, keepdims=True)
    )
    sums = [jnp.sum(upstream * normed, axis=0, keepdims=True), jnp.sum(upstream, axis=0, keepdims=True)]
    return adjusted * inverse, sums[0], sums[1]


def call(kernel, shapes, name, where, scratch=(), aliases={}):
    spaces = {"s": pltpu.SMEM, "v": pltpu.VMEM}
    return pl.pallas_call(
        kernel,
        out_shape=shapes,
        in_specs=[pl.BlockSpec(memory_space=spaces[key]) for key in where],
        out_specs=tuple(pl.BlockSpec(memory_space=pltpu.VMEM) for _ in shapes),
        scratch_shapes=list(scratch),
        input_output_aliases=aliases,
        name=name,
    )


def pack_kernel(query_ref, key_ref, value_ref, *refs, heads):
    vector_refs, (seg_ref, live_ref, out_ref, vec_s) = refs[:-4], refs[-4:]
    w_rows = query_ref.shape[0]
    sequences, rows = seg_ref.shape
    vec_s[...] = jnp.zeros_like(vec_s)
    for index, ref in enumerate(vector_refs):
        vec_s[index : index + 1, :w_rows] = ref[...].astype(f32)
    columns = jnp.transpose(vec_s[...])[:w_rows, :HEAD_DIM]
    seg = seg_ref[...]
    codes = jnp.where(live_ref[...] == 1, seg, -1)
    lines = jnp.concatenate([seg.astype(f32), codes.astype(f32)], axis=0)
    lines = jnp.concatenate([lines, jnp.zeros((w_rows - 2 * sequences, rows), f32)], axis=0)
    if rows < HEAD_DIM:
        lines = jnp.concatenate([lines, jnp.zeros((w_rows, HEAD_DIM - rows), f32)], axis=1)
    half = heads * 2 * HEAD_DIM
    for feat in range(FEATS):
        pair, single = [], []
        for h in range(heads):
            lanes = slice((feat * heads + h) * HEAD_DIM, (feat * heads + h + 1) * HEAD_DIM)
            pair += [query_ref[:, lanes].astype(f32), key_ref[:, lanes].astype(f32)]
            single.append(value_ref[:, lanes].astype(f32))
        single += [lines, columns, jnp.zeros((w_rows, HEAD_DIM), f32)]
        for core, pieces in ((0, pair), (1, single)):
            wide = jnp.concatenate(pieces, axis=1).astype(bf16)
            out_ref[feat, core] = wide


def pack_late_kernel(place_ref, w_ref, gate_ref, up_ref, kept_ref, sent_ref, *, slots):
    half = w_ref.shape[1] // 2
    cols = gate_ref.shape[1] // (FEATS * slots)

    def write(core, source_ref, target_ref):
        for feat in range(FEATS):
            pieces = [w_ref[:, core * half : (core + 1) * half]]
            for slot in range(slots):
                start = (slot * FEATS + feat) * cols
                pieces.append(source_ref[:, start : start + cols])
            target_ref[feat] = jnp.concatenate([p.astype(f32) for p in pieces], axis=1).astype(bf16)

    @pl.when(place_ref[0] == 0)
    def _():
        write(0, gate_ref, kept_ref)
        write(1, up_ref, sent_ref)

    @pl.when(place_ref[0] == 1)
    def _():
        write(0, gate_ref, sent_ref)
        write(1, up_ref, kept_ref)


def route_kernel(place_ref, kept_ref, got_ref, *out_refs):
    rows = kept_ref.shape[1]
    first, second = pl.ds(0, rows), pl.ds(rows, rows)
    for k in range(FEATS):
        target = place_ref[2] ^ k
        kept, got = kept_ref[target].astype(f32), got_ref[target].astype(f32)
        first_core = place_ref[0] == 0
        both = [jnp.where(first_core, kept, got), jnp.where(first_core, got, kept)]
        out_refs[k][...] = jnp.concatenate(both, axis=0).astype(bf16)


def piece_row(place_ref, index, piece_rows):
    member = (place_ref[3] ^ (index // 2)) * 2 + (place_ref[1] ^ (index % 2))
    return pl.multiple_of(member * piece_rows, 16)


def qkv_kernel(place_ref, *refs, w_rows, rows, heads, pieces):
    mine_refs, other_refs = refs[:pieces], refs[pieces : 2 * pieces]
    token_refs = refs[2 * pieces : 2 * pieces + FEATS]
    sent_ref, w_ref, params_ref, seg_ref, code_ref, wide_s, vec_s = refs[2 * pieces + FEATS :]
    first_core = place_ref[0] == 0
    side, feat = place_ref[1], place_ref[2]
    piece_rows, half = mine_refs[0].shape
    for index in range(pieces):
        here = pl.ds(piece_row(place_ref, index, piece_rows), piece_rows)
        mine, other = mine_refs[index][...], other_refs[index][...]
        w_ref[here, :half] = jnp.where(first_core, mine, other)
        w_ref[here, half:] = jnp.where(first_core, other, mine)
    vec_s[...] = w_ref[:, 2 * half - 128 :].astype(f32)
    wide_s[...] = w_ref[:, 2 * half - 256 : 2 * half - 128].astype(f32)
    head_width = heads * HEAD_DIM
    own = vec_s[pl.ds(pl.multiple_of(feat * head_width, HEAD_DIM), head_width), :]
    own = jnp.concatenate([own, jnp.zeros((256 - head_width, 128), f32)], axis=0)
    own = jnp.concatenate([jnp.transpose(own[:128]), jnp.transpose(own[128:])], axis=1)
    local = token_refs[0].shape[0]
    group = FEATS * local
    rest = jnp.zeros((1, half - head_width), f32)
    value_bias = jnp.concatenate([own[1:2, :head_width], rest], axis=1)
    for k in range(FEATS):
        tokens = token_refs[k][...]
        values = (dot(tokens, w_ref[:, half:]) + value_bias).astype(bf16)
        pairs = dot(tokens, w_ref[:, :half])
        for h in range(heads):
            bias = own[0:1, h * HEAD_DIM : (h + 1) * HEAD_DIM]
            bias = jnp.concatenate([bias, jnp.zeros((1, HEAD_DIM), f32)], axis=1)
            made = (pairs[:, 2 * h * HEAD_DIM : 2 * (h + 1) * HEAD_DIM] + bias).astype(bf16)
            value = values[:, h * HEAD_DIM : (h + 1) * HEAD_DIM]
            start = group + (k % 2) * local
            lanes = slice((k // 2) * HEAD_DIM, (k // 2 + 1) * HEAD_DIM)
            for slot in range(pieces):
                if min(slot % SLOTS, heads - 1) == h:
                    sent_ref[slot, k * local : (k + 1) * local, :] = made
                    sent_ref[slot, start : start + local, lanes] = value
    for start in range(0, w_ref.shape[0], 128):
        turned = jnp.transpose(vec_s[start : start + 128, :])
        params_ref[:, start : start + 128] = turned[:8]
    devices = w_ref.shape[0] // w_rows
    for ref, row in ((seg_ref, 0), (code_ref, 2)):
        for device in range(0, devices, 2):
            lines = []
            for start in (device * w_rows + row, (device + 1) * w_rows + row):
                pair = wide_s[start : start + 2, HEAD_DIM : HEAD_DIM + rows]
                lines.append(jnp.where(side == 0, pair[:1], pair[1:]))
            ref[:, device * rows : (device + 2) * rows] = jnp.concatenate(lines, axis=1)


def split_rows(first_core, values, kept_ref, sent_ref, lanes, rows):
    def write(first, second):
        for block in range(values.shape[0] // (2 * rows)):
            start = 2 * rows * block
            first[block, :, lanes] = values[start : start + rows].astype(bf16)
            second[block, :, lanes] = values[start + rows : start + 2 * rows].astype(bf16)

    @pl.when(first_core)
    def _():
        write(kept_ref, sent_ref)

    @pl.when(jnp.logical_not(first_core))
    def _():
        write(sent_ref, kept_ref)


def grad_qkv_kernel(place_ref, *refs, heads, w_rows):
    token_refs = refs[:FEATS]
    dqkv_ref, sums_ref, w_ref, back_ref, input_ref, kept_ref, sent_ref, wide_s, vec_s = refs[FEATS:]
    first_core = place_ref[0] == 0
    head_width = heads * HEAD_DIM
    half = 2 * head_width
    group = back_ref.shape[0]
    quarter = group // 2
    back_ref[:, half + head_width :] = jnp.zeros((group, half - head_width), bf16)
    for h in range(heads):
        back_ref[:, 2 * h * HEAD_DIM : 2 * (h + 1) * HEAD_DIM] = dqkv_ref[h, :group, :]
        lanes = slice(half + h * HEAD_DIM, half + (h + 1) * HEAD_DIM)
        back_ref[:quarter, lanes] = dqkv_ref[h, group:, :HEAD_DIM]
        back_ref[quarter:, lanes] = dqkv_ref[h, group:, HEAD_DIM:]
    width = wide_s.shape[1]
    wide_s[...] = jnp.zeros_like(wide_s)
    wide_s[2 : 2 + sums_ref.shape[0], :] = sums_ref[...]
    for start in range(0, width, 128):
        vec_s[start : start + 128, :] = jnp.transpose(wide_s[:, start : start + 128])
    tokens = jnp.concatenate([ref[...] for ref in token_refs], axis=0)
    back = back_ref[...]
    sums = jnp.sum(back.astype(f32), axis=0, keepdims=True)
    queries = [sums[:, 2 * h * HEAD_DIM : (2 * h + 1) * HEAD_DIM] for h in range(heads)]
    none = jnp.zeros((1, 256 - head_width), f32)
    own = jnp.concatenate(
        [
            jnp.concatenate(queries + [none], axis=1),
            sums[:, half : half + 256],
            jnp.zeros((126, 256), f32),
        ],
        axis=0,
    )
    own = jnp.concatenate([jnp.transpose(own[:, :128]), jnp.transpose(own[:, 128:])], axis=0)
    here = pl.ds(pl.multiple_of(place_ref[2] * head_width, HEAD_DIM), head_width)
    vec_s[here, :] += own[:head_width]
    grad = dot(tokens, back, 0, 0)
    grad = jnp.concatenate([grad[:, : 2 * half - 128], grad[:, 2 * half - 128 :] + vec_s[...]], axis=1)
    split_rows(first_core, grad, kept_ref, sent_ref, slice(None), w_rows)
    input_ref[...] = dot(back, w_ref[...], 1, 1).astype(bf16)


def place_first_kernel(place_ref, *refs, pieces, down_rows):
    mine_refs, other_refs = refs[:pieces], refs[pieces : 2 * pieces]
    out_ref, down_ref = refs[2 * pieces :]
    out_rows, half = mine_refs[0].shape
    out_rows = out_rows - 2 * down_rows
    feat_rows = out_rows // FEATS

    def fill(cores):
        for index in range(pieces):
            for core in range(2):
                ref = cores[core][index]
                columns = slice(core * half, (core + 1) * half)
                for k in range(FEATS):
                    start = piece_row(place_ref, index, out_rows) + (place_ref[2] ^ k) * feat_rows
                    here = pl.ds(pl.multiple_of(start, 4), feat_rows)
                    out_ref[here, columns] = ref[k * feat_rows : (k + 1) * feat_rows, :]
                start = piece_row(place_ref, index, 2 * down_rows) + core * down_rows
                here = pl.ds(pl.multiple_of(start, 8), down_rows)
                down_ref[here, :half] = ref[out_rows : out_rows + down_rows, :]
                down_ref[here, half:] = ref[out_rows + down_rows :, :]

    @pl.when(place_ref[0] == 0)
    def _():
        fill((mine_refs, other_refs))

    @pl.when(place_ref[0] == 1)
    def _():
        fill((other_refs, mine_refs))


def place_second_kernel(place_ref, *refs, indices):
    pieces = len(indices)
    mine_refs, other_refs = refs[:pieces], refs[pieces : 2 * pieces]
    gate_ref, up_ref = refs[-2:]
    rows = mine_refs[0].shape[0]
    feat_rows = rows // FEATS

    def fill(gate_refs, up_refs):
        for position, index in enumerate(indices):
            for k in range(FEATS):
                start = piece_row(place_ref, index, rows) + (place_ref[2] ^ k) * feat_rows
                here = pl.ds(pl.multiple_of(start, 4), feat_rows)
                source = slice(k * feat_rows, (k + 1) * feat_rows)
                gate_ref[here, :] = gate_refs[position][source, :]
                up_ref[here, :] = up_refs[position][source, :]

    @pl.when(place_ref[0] == 0)
    def _():
        fill(mine_refs, other_refs)

    @pl.when(place_ref[0] == 1)
    def _():
        fill(other_refs, mine_refs)


def join_kernel(
    heads_ref, tokens_ref, w_ref, params_ref,
    attended_ref, norm_ref, low_ref, normed_ref, inverse_ref, *, heads,
):
    sides = []
    for side in range(2):
        lanes = slice(side * HEAD_DIM, (side + 1) * HEAD_DIM)
        pieces = [
            heads_ref[((h // 2) * FEATS + feat) * 2 + h % 2][:, lanes]
            for feat in range(FEATS)
            for h in range(heads)
        ]
        sides.append(jnp.concatenate(pieces, axis=1))
    attended = jnp.concatenate(sides, axis=0)
    attended_ref[...] = attended
    branch = dot(attended, w_ref[...])
    first, normed, inverse = norm_forward(
        tokens_ref[...].astype(f32) + branch + params_ref[2:3, :],
        params_ref[3:4, :],
        params_ref[4:5, :],
    )
    norm_ref[...] = first
    low_ref[...] = first.astype(bf16)
    normed_ref[...] = normed
    inverse_ref[...] = inverse


def part_kernel(
    place_ref, second_ref, own_ref, got_a_ref, got_b_ref, got_c_ref, normed_ref, inverse_ref,
    params_ref, w_ref, attended_ref,
    inner_ref, dout_ref, kept_ref, sent_ref, sums_ref, *, heads, rows,
):
    back_first = second_ref[...] + own_ref[...].astype(f32) + got_a_ref[...].astype(f32)
    back_first = back_first + got_b_ref[...].astype(f32) + got_c_ref[...].astype(f32)
    inner, gain_sum, shift_sum = norm_backward(
        back_first, normed_ref[...], inverse_ref[...], params_ref[3:4, :]
    )
    inner_ref[...] = inner
    branch = inner.astype(bf16)
    sums_ref[...] = jnp.concatenate(
        [jnp.sum(branch.astype(f32), axis=0, keepdims=True), gain_sum, shift_sum], axis=0
    )
    back = dot(branch, w_ref[...], 1, 1).astype(bf16)
    for slot in range(SLOTS):
        for feat in range(FEATS):
            start = (feat * heads + min(slot, heads - 1)) * HEAD_DIM
            piece = back[:, start : start + HEAD_DIM]
            dout_ref[((slot // 2) * FEATS + feat) * 2 + slot % 2] = jnp.concatenate(
                [piece[:rows], piece[rows:]], axis=1
            )
    half = branch.shape[1] // 2
    grad = dot(attended_ref[...], branch, 0, 0).astype(bf16)
    first_core = place_ref[0] == 0
    kept_ref[...] = jnp.where(first_core, grad[:, :half], grad[:, half:])
    sent_ref[...] = jnp.where(first_core, grad[:, half:], grad[:, :half])


def finish_kernel(parts_ref, query_ref, key_ref, value_ref, *refs, heads):
    vector_refs, vec_s = refs[:-1], refs[-1]
    groups = parts_ref.shape[0] // FEATS
    vec_s[...] = jnp.zeros_like(vec_s)
    w_rows = parts_ref.shape[1]
    half = heads * 2 * HEAD_DIM
    head_width = heads * HEAD_DIM
    vectors = jnp.zeros((w_rows, 128), f32)
    for feat in range(FEATS):
        total = parts_ref[feat].astype(f32)
        for group in range(1, groups):
            total = total + parts_ref[group * FEATS + feat].astype(f32)
        lanes = slice(feat * head_width, (feat + 1) * head_width)
        for index, ref in enumerate((query_ref, key_ref)):
            starts = [(2 * h + index) * HEAD_DIM for h in range(heads)]
            ref[:, lanes] = jnp.concatenate([total[:, at : at + HEAD_DIM] for at in starts], axis=1)
        value_ref[:, lanes] = total[:, half : half + head_width]
        vectors = vectors + total[:, 2 * half - 128 :]
    vec_s[:w_rows, :] = vectors
    turned = jnp.transpose(vec_s[...])
    for index, ref in enumerate(vector_refs):
        ref[...] = turned[index : index + 1, :w_rows]


def fold_kernel(
    place_ref, ff_kept_ref, ff_got_ref, down_kept_ref, down_got_ref, out_kept_ref, out_got_ref, *refs,
    units,
):
    ff_refs, down_refs, out_refs = refs[:2], refs[2 : 2 + units], refs[2 + units :]
    rows = ff_kept_ref.shape[0] // (2 * units)
    for k, ref in enumerate(ff_refs):
        for unit in range(units):
            start = (unit * 2 + (place_ref[1] ^ k)) * rows
            here = pl.ds(pl.multiple_of(start, 16), rows)
            value = ff_kept_ref[here, :].astype(f32) + ff_got_ref[here, :].astype(f32)
            ref[unit] = value.astype(bf16)
    for kept_ref, got_ref, moved_refs in (
        (down_kept_ref, down_got_ref, down_refs),
        (out_kept_ref, out_got_ref, out_refs),
    ):
        rows = kept_ref.shape[0] // units
        for k, ref in enumerate(moved_refs):
            here = pl.ds(pl.multiple_of((place_ref[3] ^ k) * rows, 16), rows)
            value = kept_ref[here, :].astype(f32) + got_ref[here, :].astype(f32)
            ref[...] = value.astype(bf16)


def finish_late_kernel(place_ref, *refs, ff_part):
    part_refs, (kept_ref, sent_ref) = refs[:FEATS], refs[FEATS:]
    w_rows = kept_ref.shape[0]
    total = part_refs[0][:, ff_part:].astype(f32)
    for part in part_refs[1:]:
        total = total + part[:, ff_part:].astype(f32)
    for core in range(2):

        @pl.when(place_ref[0] == core)
        def _():
            for ref, rows in (
                (kept_ref, slice(core * w_rows, (core + 1) * w_rows)),
                (sent_ref, slice((1 - core) * w_rows, (2 - core) * w_rows)),
            ):
                ref[:, FEATS * ff_part :] = total[rows].astype(bf16)
                for k in range(FEATS):
                    lanes = pl.ds(pl.multiple_of((place_ref[2] ^ k) * ff_part, 128), ff_part)
                    ref[:, lanes] = part_refs[k][rows, :ff_part]


def finish_wide_kernel(
    place_ref, kept_ref, got_ref, down_kept_ref, down_got_ref,
    gate_ref, up_ref, out_ref, down_ref, *, slots,
):
    total = gate_ref.shape[1]
    cols = total // (FEATS * slots)
    half = out_ref.shape[1] // 2

    def write(first, second, down_first, down_second):
        for source, target in ((first, gate_ref), (second, up_ref)):
            for slot in range(slots):
                pieces = []
                for feat in range(FEATS):
                    start = (feat * slots + slot) * cols
                    pieces.append(source[:, start : start + cols].astype(f32))
                start = slot * FEATS * cols
                target[:, start : start + FEATS * cols] = jnp.concatenate(pieces, axis=1)
        out_ref[:, :half] = first[:, total:].astype(f32)
        out_ref[:, half:] = second[:, total:].astype(f32)
        down_ref[:, :half] = down_first[...].astype(f32)
        down_ref[:, half:] = down_second[...].astype(f32)

    @pl.when(place_ref[0] == 0)
    def _():
        write(kept_ref, got_ref, down_kept_ref, down_got_ref)

    @pl.when(place_ref[0] == 1)
    def _():
        write(got_ref, kept_ref, down_got_ref, down_kept_ref)


def after(values, *others):
    return lax.optimization_barrier((values,) + others)[0]


def tie(*values):
    return lax.optimization_barrier(values)


def on_device(
    layer_input, segment_ids, token_live, w_query, b_query, w_key, w_value, b_value,
    w_output, b_output, first_gain, first_shift, w_gate, w_up, w_down, b_down,
    second_gain, second_shift, output_grad,
):
    units = lax.axis_size("u")
    unit, side, feat, core = (lax.axis_index(name) for name in ("u", "s", "f", "c"))
    devices = units * 2 * FEATS * 2
    sequences, rows, width = layer_input.shape
    length = rows * devices
    w_rows = w_query.shape[0]
    down_rows, ff_part = w_down.shape[0], w_gate.shape[1] // FEATS
    slots = units * 2
    heads = HEADS // FEATS
    head_width = heads * HEAD_DIM
    ranges = slots // SLOTS
    local = 2 * rows
    group = FEATS * local
    here = jnp.stack([core, side, feat, unit]).astype(jnp.int32)
    parts = slots

    def exchange_sides(values):
        kept = jnp.where(side == 0, values[0], values[1])
        got = swap(jnp.where(side == 0, values[1], values[0]), "s")
        return kept, got

    def to_tokens(values):
        kept, got = exchange_sides(values)
        return jnp.concatenate(
            [jnp.where(side == 0, kept, got), jnp.where(side == 0, got, kept)], axis=0
        )

    def from_tokens(values):
        kept, got = exchange_sides(values.reshape(2, rows, width))
        return jnp.stack([jnp.where(side == 0, kept, got), jnp.where(side == 0, got, kept)])

    def to_group(blocks):
        return all_to_all(blocks.reshape(-1, blocks.shape[-1]), ("f", "c"))

    def from_units(own, other_side, pin=None):
        pieces = [own, other_side]
        for k in range(1, units):
            for piece in (own, other_side):
                pieces.append(swap(piece if pin is None else after(piece, pin), "u", k))
        return pieces

    tokens = to_tokens(layer_input)

    vectors = [
        values.reshape(1, w_rows)
        for values in (
            b_query, b_value, b_output, first_gain, first_shift, b_down, second_gain, second_shift
        )
    ]
    half = heads * 2 * HEAD_DIM
    (early,) = call(
        functools.partial(pack_kernel, heads=heads),
        (jax.ShapeDtypeStruct((FEATS, 2, w_rows, half), bf16),),
        "pack_attn",
        "v" * 13,
        [pltpu.VMEM((128, 128), f32)],
    )(w_query, w_key, w_value, *vectors, segment_ids, token_live)
    token_parts = gather_feats(tokens)
    early_own = all_to_all(early.reshape(-1, half), ("f", "c"))
    others = range(1, units)
    early_side = swap(early_own, "s")
    early_near = [swap(early_own, "u", k) for k in others]
    early_far = [swap(early_side, "u", k) for k in others]

    def by_distance(own, other_side, near, far):
        pieces = [own, other_side]
        for index in range(units - 1):
            pieces += [near[index], far[index]]
        return pieces

    early_pieces = by_distance(early_own, early_side, early_near, early_far)
    early_others = [swap(piece, "c") for piece in early_pieces]

    late_cols = width // 2 + ff_part
    late_shape = jax.ShapeDtypeStruct((FEATS, w_rows, late_cols), bf16)
    late_kept, late_sent = call(
        functools.partial(pack_late_kernel, slots=slots), (late_shape, late_shape), "pack_late", "svvv"
    )(here, w_output, w_gate, w_up)
    routed = call(
        route_kernel,
        (jax.ShapeDtypeStruct((2 * w_rows, late_cols), bf16),) * FEATS,
        "route_late",
        "svv",
    )(here, late_kept, swap(after(late_sent, early_own), "c"))
    out_half = width // 2
    routed = [after(piece, token_parts[1]) for piece in routed]
    late_feats = [routed[0]] + [swap(routed[k], "f", k) for k in range(1, FEATS)]
    here_qkv, *late_feats = tie(here, *late_feats)
    first_own = jnp.concatenate(
        [piece[:, :out_half] for piece in late_feats] + [w_down[:, :out_half], w_down[:, out_half:]]
    )
    second_own = jnp.concatenate([piece[:, out_half:] for piece in late_feats])
    others = range(1, units)

    sent, w_attn, params, seg_row, code_row = call(
        functools.partial(qkv_kernel, w_rows=w_rows, rows=rows, heads=heads, pieces=parts),
        (
            jax.ShapeDtypeStruct((slots, group * 3 // 2, 2 * HEAD_DIM), bf16),
            jax.ShapeDtypeStruct((width, 2 * half), bf16),
            jax.ShapeDtypeStruct((8, width), f32),
            jax.ShapeDtypeStruct((1, length), f32),
            jax.ShapeDtypeStruct((1, length), f32),
        ),
        "qkv",
        "s" + "v" * (2 * parts + FEATS),
        [pltpu.VMEM((width, 128), f32)] * 2,
    )(here_qkv, *early_pieces, *early_others, *token_parts)
    qkv = all_to_all(sent.reshape(-1, 2 * HEAD_DIM), ("u", "c"))
    first_side = swap(first_own, "s")
    first_units = [swap(first_own, "u", k) for k in others]
    first_swaps = [swap(piece, "c") for piece in [first_own, first_side] + first_units]
    second_swaps = [swap(second_own, "c")]
    qkv, first_side, second_swaps[0], *moved = tie(
        qkv, first_side, second_swaps[0], *first_units, *first_swaps
    )
    first_units, first_swaps = moved[: units - 1], moved[units - 1 :]
    qkv = qkv.reshape(sent.shape)

    blocks = length // BLOCK
    slot_self = unit * 2 + core
    range_self = slot_self // SLOTS
    head_self = feat * heads + jnp.minimum(slot_self % SLOTS, heads - 1)
    slope = jnp.asarray(alibi_slopes(HEADS))[head_self].reshape(1, 1)
    seg_blocks = seg_row.reshape(blocks, BLOCK)
    seg_low, seg_high = seg_blocks[:, 0], seg_blocks[:, -1]
    key_low = jnp.sum(seg_high[None, :] < seg_low[:, None], axis=1, dtype=jnp.int32)
    key_high = jnp.sum(seg_low[None, :] <= seg_high[:, None], axis=1, dtype=jnp.int32)
    own = jnp.stack(
        [feat, range_self * (blocks // ranges), (range_self + 1) * (blocks // ranges)]
    ).astype(jnp.int32)
    table = jnp.stack([key_low, key_high, jnp.pad(own, (0, blocks - 3))])
    second_side = swap(second_own, "s")
    second_units = [swap(second_own, "u", k) for k in others]
    first_far = [swap(first_side, "u", k) for k in others]
    out_blocks, lse, o_turned = attend(table, slope, qkv, seg_row, code_row)
    out_blocks, second_side, *moved = tie(out_blocks, second_side, *second_units, *first_far)
    second_units, first_far = moved[: units - 1], moved[units - 1 :]
    second_far = [swap(second_side, "u", k) for k in others]
    first_swaps += [swap(piece, "c") for piece in first_far]
    second_swaps += [swap(piece, "c") for piece in [second_side] + second_units]

    first_pieces = by_distance(first_own, first_side, first_units, first_far)
    first_others = by_distance(
        first_swaps[0], first_swaps[1], first_swaps[2 : 1 + units], first_swaps[1 + units :]
    )
    aligned = w_rows % 8 == 0

    def in_rows(pieces, feats):
        cols = pieces[0].shape[1]
        values = jnp.stack(pieces).reshape(units, 2, feats, -1, cols)
        values = jnp.take(values, jnp.arange(units) ^ unit, axis=0)
        values = jnp.take(values, jnp.arange(2) ^ side, axis=1)
        if feats == FEATS:
            values = jnp.take(values, jnp.arange(FEATS) ^ feat, axis=2)
        return values.reshape(-1, cols)

    def by_core(mine, others_):
        mine, others_ = in_rows(mine, FEATS), in_rows(others_, FEATS)
        return jnp.where(core == 0, mine, others_), jnp.where(core == 0, others_, mine)

    if aligned:
        full_output, full_down = call(
            functools.partial(place_first_kernel, pieces=parts, down_rows=down_rows),
            (
                jax.ShapeDtypeStruct((width, width), bf16),
                jax.ShapeDtypeStruct((ff_part, width), bf16),
            ),
            "place_first",
            "s" + "v" * 2 * parts,
        )(here, *first_pieces, *first_others)
    else:
        out_rows = 2 * FEATS * w_rows
        full_output = jnp.concatenate(
            by_core([p[:out_rows] for p in first_pieces], [p[:out_rows] for p in first_others]), axis=1
        )

        def down_of(pieces):
            return in_rows(
                [
                    jnp.concatenate([p[out_rows : out_rows + down_rows], p[out_rows + down_rows :]], axis=1)
                    for p in pieces
                ],
                1,
            ).reshape(slots, down_rows, width)

        down_mine, down_others = down_of(first_pieces), down_of(first_others)
        full_down = jnp.stack(
            [jnp.where(core == 0, down_mine, down_others), jnp.where(core == 0, down_others, down_mine)],
            axis=1,
        ).reshape(ff_part, width)

    heads_in = all_to_all(out_blocks.reshape(-1, 2 * HEAD_DIM), ("u", "f", "c"))
    heads_in, *second_swaps[1:] = tie(heads_in, *second_swaps[1:])
    heads_in = heads_in.reshape(ranges, SLOTS * FEATS, rows, 2 * HEAD_DIM)
    if ranges > 1:
        heads_in = lax.dynamic_index_in_dim(heads_in, unit * 2 // SLOTS, 0, keepdims=False)
    else:
        heads_in = heads_in[0]
    attended, first_norm, first_low_own, normed_one, inverse_one = call(
        functools.partial(join_kernel, heads=heads),
        (
            jax.ShapeDtypeStruct((local, width), bf16),
            jax.ShapeDtypeStruct((local, width), f32),
            jax.ShapeDtypeStruct((local, width), bf16),
            jax.ShapeDtypeStruct((local, width), f32),
            jax.ShapeDtypeStruct((local, 1), f32),
        ),
        "join_heads",
        "vvvv",
    )(heads_in, tokens, full_output, params)

    first_low_own, *second_far = tie(first_low_own, *second_far)
    second_swaps += [swap(piece, "c") for piece in second_far]
    ff_square = jax.ShapeDtypeStruct((width, ff_part), bf16)
    indices = [0, 1] + [2 * k for k in others] + [2 * k + 1 for k in others]
    second_pieces = [second_own, second_side, *second_units, *second_far]
    if aligned:
        full_gate, full_up = call(
            functools.partial(place_second_kernel, indices=indices),
            (ff_square, ff_square),
            "place_second",
            "s" + "v" * 2 * parts,
        )(here, *second_pieces, *second_swaps)
    else:
        order = [indices.index(position) for position in range(parts)]
        full_gate, full_up = by_core(
            [second_pieces[position] for position in order],
            [second_swaps[position] for position in order],
        )
    low_parts = gather_feats(first_low_own)
    full_gate, full_up, *low_parts = tie(full_gate, full_up, *low_parts)
    first_low = jnp.concatenate(low_parts, axis=0)
    gate_rows = dot(first_low, full_gate)
    up_rows = dot(first_low, full_up)
    spread = 0.5 * (1.0 + lax.erf(gate_rows * (0.5**0.5)))
    gelu = gate_rows * spread
    hidden = (gelu * up_rows).astype(bf16)
    partial_mixed = dot(hidden, full_down).astype(bf16).reshape(FEATS, local, width)
    partial_mixed, gate_kept, up_kept = tie(partial_mixed, gate_rows, up_rows)
    mixed_got = [swap(partial_mixed[k], "f", k) for k in range(1, FEATS)]
    spread = 0.5 * (1.0 + lax.erf(gate_kept * (0.5**0.5)))
    density = jnp.exp(-0.5 * gate_kept * gate_kept) * (1.0 / math.sqrt(2.0 * math.pi))
    gate_factor = (up_kept * (spread + gate_kept * density)).astype(bf16)
    up_factor = (gate_kept * spread).astype(bf16)
    bias_down, gate_factor, up_factor = tie(params[5], gate_factor, up_factor)
    mixed = partial_mixed[0].astype(f32) + bias_down
    for piece in mixed_got:
        mixed = mixed + piece.astype(f32)
    gain_two = params[6]
    layer_wide, normed_two, inverse_two = norm_forward(first_norm + mixed, gain_two, params[7])

    upstream = to_tokens(after(output_grad, out_blocks)).astype(f32)
    back_second, grad_gain_two, grad_shift_two = norm_backward(
        upstream, normed_two, inverse_two, gain_two
    )
    back_low = back_second.astype(bf16)
    grad_down_bias = jnp.sum(back_low.astype(f32), axis=0, keepdims=True)
    back_mixed = jnp.concatenate(gather_feats(back_low), axis=0)
    back_hidden = dot(back_mixed, full_down, 1, 1)
    back_gate = (back_hidden * gate_factor.astype(f32)).astype(bf16)
    back_up = (back_hidden * up_factor.astype(f32)).astype(bf16)
    partial_first = (dot(back_gate, full_gate, 1, 1) + dot(back_up, full_up, 1, 1)).astype(bf16)
    partial_first = partial_first.reshape(FEATS, local, width)
    partial_got = [swap(partial_first[k], "f", k) for k in range(1, FEATS)]
    small = swap(partial_first[0, :16, :128], "c")
    small, back_gate, back_up, back_mixed = tie(small, back_gate, back_up, back_mixed)
    half_width = width // 2

    def chosen(first, second):
        return jnp.where(core == 0, first, second)

    left, right = back_mixed[:, :half_width], back_mixed[:, half_width:]

    def outer(rows_side, cols_side):
        return dot(cols_side, rows_side, 0, 0).astype(bf16).T

    ff_sent = outer(first_low, chosen(back_up, back_gate))
    down_sent = outer(hidden, chosen(right, left))
    ff_kept = outer(first_low, chosen(back_gate, back_up))
    down_kept = outer(hidden, chosen(left, right))
    here_join, ff_sent, down_sent, ff_kept, down_kept = tie(here, ff_sent, down_sent, ff_kept, down_kept)
    inner_shape = jax.ShapeDtypeStruct((local, width), f32)
    back_inner, dout_blocks, out_kept, out_sent, sums_one = call(
        functools.partial(part_kernel, heads=heads, rows=rows),
        (
            inner_shape,
            jax.ShapeDtypeStruct((SLOTS * FEATS, rows, 2 * HEAD_DIM), bf16),
            jax.ShapeDtypeStruct((width, half_width), bf16),
            jax.ShapeDtypeStruct((width, half_width), bf16),
            jax.ShapeDtypeStruct((3, width), f32),
        ),
        "back_join",
        "s" + "v" * 10,
    )(
        here_join, back_second, partial_first[0], *partial_got, normed_one, inverse_one, params,
        full_output, attended,
    )
    dout_sent = jnp.broadcast_to(dout_blocks[None], (ranges,) + dout_blocks.shape)
    dout = all_to_all(dout_sent.reshape(-1, 2 * HEAD_DIM), ("u", "f", "c"))
    dout = dout.reshape(slots * FEATS, rows, 2 * HEAD_DIM)

    def fold(values, axis):
        return scatter_axis(values, axis).astype(bf16)

    def added(kept, got):
        return (kept.astype(f32) + got.astype(f32)).astype(bf16)

    out_got = swap(out_sent, "c")
    ff_got, down_got = (swap(after(values, *partial_got), "c") for values in (ff_sent, down_sent))

    def parts_of(values, axis):
        size, me = lax.axis_size(axis), lax.axis_index(axis)
        if size == 2:
            return [jnp.where(me == 0, values[0], values[1]), jnp.where(me == 0, values[1], values[0])]
        return [lax.dynamic_index_in_dim(values, me ^ k, 0, keepdims=False) for k in range(size)]

    def send(values, axis):
        own, *rest = parts_of(values, axis)
        return own, [swap(piece, axis, k + 1) for k, piece in enumerate(rest)]

    def total(own, got):
        result = own.astype(f32)
        for piece in got:
            result = result + piece.astype(f32)
        return result

    def sides(values):
        return jnp.moveaxis(values.reshape(units, 2, -1, values.shape[-1]), 1, 0)

    def by_unit(values):
        return values.reshape(units, -1, values.shape[-1])

    def part(values, member):
        return lax.dynamic_index_in_dim(values, member, 0, keepdims=False)

    def send_sum(kept, got, axis):
        me = lax.axis_index(axis)
        moved = [
            swap(added(part(kept, me ^ k), part(got, me ^ k)), axis, k)
            for k in range(1, lax.axis_size(axis))
        ]
        return [part(kept, me), part(got, me)], moved

    ff_own, ff_moved = send_sum(sides(ff_kept), sides(ff_got), "s")
    down_own, down_moved = send_sum(by_unit(down_kept), by_unit(down_got), "u")
    out_own, out_moved = send_sum(by_unit(out_kept), by_unit(out_got), "u")
    dqkv = attend_back(table, slope, qkv, dout, o_turned, lse, seg_row, code_row)
    dqkv, *moved = tie(dqkv, *ff_moved, *down_moved, *out_moved)
    ff_moved, down_moved, out_moved = moved[:1], moved[1:units], moved[units:]
    grad_down = total(down_own[0], down_own[1:] + down_moved).astype(bf16).reshape(2, 2 * down_rows, -1)
    grad_out = total(out_own[0], out_own[1:] + out_moved).astype(bf16).reshape(2, FEATS * 2 * w_rows, -1)
    grad_down, down_moved = send(grad_down, "s")
    dqkv = all_to_all(dqkv.reshape(-1, 2 * HEAD_DIM), ("u", "c"))
    dqkv, down_moved[0] = tie(dqkv, down_moved[0])
    grad_ff = total(ff_own[0], ff_own[1:] + ff_moved).astype(bf16)
    grad_ff, ff_moved = send(after(grad_ff, dqkv), "u")
    grad_out, out_moved = send(after(grad_out, dqkv), "s")
    dqkv = dqkv.reshape(ranges, SLOTS, group * 3 // 2, 2 * HEAD_DIM)
    if ranges > 1:
        dqkv = jnp.sum(dqkv.astype(f32), axis=0).astype(bf16)
    else:
        dqkv = dqkv[0]
    vector_sums = jnp.concatenate([sums_one, grad_down_bias, grad_gain_two, grad_shift_two], axis=0)
    attn_shape = jax.ShapeDtypeStruct((slots * FEATS, w_rows, 2 * half), bf16)
    ignored, partial_input, attn_kept, attn_sent = call(
        functools.partial(grad_qkv_kernel, heads=heads, w_rows=w_rows),
        (
            jax.ShapeDtypeStruct((group, 2 * half), bf16),
            jax.ShapeDtypeStruct((group, width), bf16),
            attn_shape,
            attn_shape,
        ),
        "grad_qkv",
        "s" + "v" * (FEATS + 3),
        [pltpu.VMEM((128, width), f32), pltpu.VMEM((width, 128), f32)],
    )(here, *token_parts, dqkv, vector_sums, w_attn)
    partial_input = partial_input.reshape(FEATS, local, width)
    grad_attn = added(after(attn_kept, partial_input), swap(attn_sent, "c"))
    grad_attn = grad_attn.reshape(-1, 2 * half)
    grad_down = total(grad_down, down_moved).reshape(2, down_rows, half_width)
    layer_wide_low = after(layer_wide.astype(bf16), grad_attn)
    grad_attn = all_to_all(grad_attn, ("u", "s", "f"))
    input_got = [swap(partial_input[k], "f", k) for k in range(1, FEATS)]
    grad_ff = total(grad_ff, ff_moved)
    grad_out = total(grad_out, out_moved)
    grad_late = jnp.concatenate([grad_ff, grad_out], axis=1).astype(bf16)
    grad_late = grad_late.reshape(FEATS, 2 * w_rows, ff_part + half_width)
    late_got = [lax.dynamic_index_in_dim(grad_late, feat ^ k, 0, keepdims=False) for k in range(FEATS)]
    back_inner, *late_got = tie(back_inner, *late_got)
    late_got = late_got[:1] + [swap(late_got[k], "f", k) for k in range(1, FEATS)]
    input_sum = back_inner + partial_input[0].astype(f32)
    for piece in input_got:
        input_sum = input_sum + piece.astype(f32)
    input_grad = from_tokens(input_sum.astype(bf16))
    layer_output = from_tokens(layer_wide_low)

    wide_shape = jax.ShapeDtypeStruct((w_rows, FEATS * ff_part + half_width), bf16)
    wide_kept, wide_sent = call(
        functools.partial(finish_late_kernel, ff_part=ff_part),
        (wide_shape, wide_shape),
        "finish_late",
        "s" + "v" * FEATS,
    )(here, *late_got)
    wide_got = swap(wide_sent, "c")
    down_kept = chosen(grad_down[0], grad_down[1])
    down_got = swap(chosen(grad_down[1], grad_down[0]).astype(bf16), "c")
    ff_out_shape = jax.ShapeDtypeStruct((w_rows, FEATS * ff_part), f32)
    grad_gate, grad_up, grad_output, grad_down = call(
        functools.partial(finish_wide_kernel, slots=slots),
        (
            ff_out_shape,
            ff_out_shape,
            jax.ShapeDtypeStruct((w_rows, width), f32),
            jax.ShapeDtypeStruct((down_rows, width), f32),
        ),
        "finish_wide",
        "svvvv",
    )(here, wide_kept, wide_got, down_kept, down_got)
    matrix_shape = jax.ShapeDtypeStruct((w_rows, width), f32)
    grad_query, grad_key, grad_value, *vectors_out = call(
        functools.partial(finish_kernel, heads=heads),
        (matrix_shape,) * 3 + (jax.ShapeDtypeStruct((1, w_rows), f32),) * 8,
        "finish",
        "v",
        [pltpu.VMEM((128, 128), f32)],
    )(grad_attn.reshape(slots * FEATS, w_rows, 2 * half))
    vectors_out = [values.reshape(w_rows) for values in vectors_out]
    return (
        layer_output, input_grad, grad_query, vectors_out[0], grad_key, grad_value,
        vectors_out[1], grad_output, vectors_out[2], vectors_out[3], vectors_out[4],
        grad_gate, grad_up, grad_down, vectors_out[5], vectors_out[6], vectors_out[7],
    )


def solution(mesh):
    devices = mesh.devices
    names = ("u", "s", "f", "c")
    inner = Mesh(devices.reshape(devices.size // (4 * FEATS), 2, FEATS, 2), names)
    tokens, matrix, vector = P(None, names, None), P(names, None), P(names)
    ids = P(None, names)
    return jax.shard_map(
        on_device,
        mesh=inner,
        in_specs=(
            tokens, ids, ids, matrix, vector, matrix, matrix, vector, matrix, vector, vector,
            vector, matrix, matrix, matrix, vector, vector, vector, tokens,
        ),
        out_specs=(
            tokens, tokens, matrix, vector, matrix, matrix, vector, matrix, vector, vector,
            vector, matrix, matrix, matrix, vector, vector, vector,
        ),
        check_vma=False,
    )
```

```python
import functools
import math

import jax
import jax.numpy as jnp
import numpy as np
from jax import lax
from jax.experimental import pallas as pl
from jax.experimental.pallas import tpu as pltpu
from jax.sharding import Mesh
from jax.sharding import PartitionSpec as P

HEADS = 12
HEAD_DIM = 64
FEATS = 4
SLOTS = 4
PACK = 4 * HEAD_DIM
BLOCK = 256

norm_epsilon = 1e-12
masked_value = -1e30
f32 = jnp.float32
bf16 = jnp.bfloat16


def alibi_slopes(head_total):
    nearest = 2 ** int(math.floor(math.log2(head_total)))
    slopes = [2.0 ** (-8.0 * (index + 1) / nearest) for index in range(nearest)]
    extra = [2.0 ** (-8.0 * (index + 1) / (2 * nearest)) for index in range(2 * nearest)]
    slopes = slopes + extra[0::2][: head_total - nearest]
    return np.array(slopes, dtype=np.float32)


def dot(left, right, left_dim=1, right_dim=0):
    return lax.dot_general(
        left, right, (((left_dim,), (right_dim,)), ((), ())), preferred_element_type=f32
    )


def swap(values, axis, step=1):
    size = lax.axis_size(axis)
    return lax.ppermute(values, axis, [(i, i ^ step) for i in range(size)])


def in_order(parts, me):
    if len(parts) == 2:
        mine, other = parts
        return jnp.stack([jnp.where(me == 0, mine, other), jnp.where(me == 0, other, mine)])
    return jnp.take(jnp.stack(parts), jnp.arange(len(parts)) ^ me, axis=0)


def gather_axis(values, axis):
    size = lax.axis_size(axis)
    parts = [values] + [swap(values, axis, k) for k in range(1, size)]
    return in_order(parts, lax.axis_index(axis))


def scatter_axis(values, axis):
    size = lax.axis_size(axis)
    me = lax.axis_index(axis)

    def pick(k):
        if size == 2:
            return jnp.where((me ^ k) == 0, values[0], values[1])
        return lax.dynamic_index_in_dim(values, me ^ k, 0, keepdims=False)

    total = pick(0)
    for k in range(1, size):
        total = total + swap(pick(k).astype(bf16), axis, k).astype(f32)
    return total


def gather_feats(values):
    return [values] + [swap(values, "f", k) for k in range(1, FEATS)]


def scatter_feats(values):
    rows = values.shape[0] // FEATS
    total = values[:rows]
    for k in range(1, FEATS):
        total = total + swap(values[k * rows : (k + 1) * rows].astype(bf16), "f", k).astype(f32)
    return total


def all_to_all(values, axes):
    return lax.all_to_all(values, axes, split_axis=0, concat_axis=0, tiled=True)


def place(unit, side, feat, core, rows):
    return (((unit * 2 + side) * FEATS + feat) * 2 + core) * rows


def unpack_qkv(qkv_ref, nat_s, feat, rows):
    slots, lines, _ = qkv_ref.shape
    group = 2 * FEATS * rows
    nothing = jnp.zeros((rows, HEAD_DIM), bf16)
    for slot in range(slots):
        for k in range(FEATS):
            for side in range(2):
                here = pl.ds(
                    pl.multiple_of(place(slot // 2, side, feat ^ k, slot % 2, rows), rows), rows
                )
                start = (2 * k + side) * rows
                nat_s[here, :128] = qkv_ref[slot, start : start + rows, :]
                start = group + (2 * (k % 2) + side) * rows
                lanes = slice((k // 2) * HEAD_DIM, (k // 2 + 1) * HEAD_DIM)
                value = qkv_ref[slot, start : start + rows, lanes]
                nat_s[here, 128:] = jnp.concatenate([value, nothing], axis=1)


def turn(values):
    return jnp.transpose(values.astype(f32))


def spread_codes(code_ref, code_s):
    for start in range(0, code_ref.shape[1], 128):
        row = code_ref[:, start : start + 128]
        code_s[start : start + 128, :] = jnp.transpose(jnp.broadcast_to(row, (128, 128)))


def distance_tile():
    rows = lax.broadcasted_iota(jnp.int32, (BLOCK, BLOCK), 0)
    cols = lax.broadcasted_iota(jnp.int32, (BLOCK, BLOCK), 1)
    return (cols - rows).astype(f32)


def span(index):
    return pl.ds(pl.multiple_of(index * BLOCK, BLOCK), BLOCK)


def even_range(low, high, first, last):
    low, high = jnp.maximum(low, first), jnp.minimum(high, last)
    high = jnp.maximum(low, high)
    odd = (high - low) % 2
    up = odd * (high < last).astype(jnp.int32)
    low = low - (odd - up)
    return low, (high + up - low) // 2


def score_tile(qk_part, qz_part, code_part, seg_part, tile, q_block, k_block, slope, diagonal):
    codes = jnp.concatenate([code_part] * (BLOCK // 128), axis=1)
    allowed = codes == seg_part
    if diagonal:
        distance = tile
    else:
        distance = tile + ((q_block - k_block) * BLOCK).astype(f32)
    if diagonal is False:
        fall = distance * jnp.where(q_block > k_block, slope, -slope)
    else:
        fall = jnp.abs(distance) * slope
        allowed = allowed | (distance == 0.0)
    return jnp.where(allowed, dot(qk_part, qz_part) - fall, masked_value)


def pair_plan(index, low, high, blocks):
    odd = (high - low) % 2
    up = odd * (high < blocks).astype(jnp.int32)
    low, high = low - (odd - up), high + up
    at_low = (low == index).astype(jnp.int32)
    partner = low + at_low
    base = low + 1 + at_low

    def member(t):
        here = base + t
        return here + ((here >= index) & (at_low == 0)).astype(jnp.int32)

    return partner, (high - low - 2) // 2, member


def score_tile_plain(qk_part, qz_part, code_part, seg_part, offset, slope):
    distance = distance_tile() + offset
    scores = dot(qk_part, qz_part) - slope * jnp.abs(distance)
    codes = jnp.concatenate([code_part] * (BLOCK // 128), axis=1)
    allowed = (codes == seg_part) | (distance == 0.0)
    return jnp.where(allowed, scores, masked_value)


def attend_kernel(
    table_ref, slope_ref, qkv_ref, seg_ref, code_ref, out_ref, lse_ref, ot_ref,
    nat_s, qz_s, vt_s, o_s, code_s,
):
    slope = slope_ref[0, 0]
    units = qkv_ref.shape[0] // 2
    rows = out_ref.shape[1]
    unpack_qkv(qkv_ref, nat_s, table_ref[2, 0], rows)
    spread_codes(code_ref, code_s)
    length = nat_s.shape[0]
    blocks = length // BLOCK
    qz_s[:HEAD_DIM, :] = jnp.zeros((HEAD_DIM, length), bf16)
    for start in range(0, length, 128):
        here = slice(start, start + 128)
        qk_turned = turn(nat_s[here, :128])
        qz_s[HEAD_DIM:, here] = (qk_turned[:HEAD_DIM] * (HEAD_DIM**-0.5)).astype(bf16)
        vt_s[:, here] = turn(nat_s[here, 128:])[:HEAD_DIM].astype(bf16)
    if qkv_ref.shape[0] > SLOTS:
        o_s[...] = jnp.zeros_like(o_s)
        ot_ref[...] = jnp.zeros_like(ot_ref)
        lse_ref[...] = jnp.zeros_like(lse_ref)


    def query_step(i, carry):
        here = span(i)
        qz_part = qz_s[:, here]
        seg_part = seg_ref[:, here]
        partner, pairs, member = pair_plan(i, table_ref[0, i], table_ref[1, i], blocks)

        def scores_of(j, diagonal):
            return score_tile(
                nat_s[span(j), :128], qz_part, code_s[span(j), :], seg_part, distance_tile(), i, j,
                slope, diagonal,
            )

        def mixed_of(j, probs):
            return dot(vt_s[:, span(j)], probs.astype(bf16))

        def highest(scores):
            return jnp.maximum(*(jnp.max(values, axis=0, keepdims=True) for values in scores))

        def key_step(pair, state):
            top, total, mixed = state
            keys = [member(2 * pair), member(2 * pair + 1)]
            scores = [scores_of(j, False) for j in keys]
            top_new = jnp.maximum(top, highest(scores))
            factor = jnp.exp(top - top_new)
            probs = [jnp.exp(values - top_new) for values in scores]
            total = total * factor + jnp.sum(probs[0] + probs[1], axis=0, keepdims=True)
            mixed = mixed * factor + (mixed_of(keys[0], probs[0]) + mixed_of(keys[1], probs[1]))
            return top_new, total, mixed

        scores = [scores_of(i, True), scores_of(partner, False)]
        top = highest(scores)
        probs = [jnp.exp(values - top) for values in scores]
        total = jnp.sum(probs[0] + probs[1], axis=0, keepdims=True)
        mixed = mixed_of(i, probs[0]) + mixed_of(partner, probs[1])
        top, total, mixed = lax.fori_loop(0, pairs, key_step, (top, total, mixed))
        mixed = mixed / total
        ot_ref[:, here] = mixed
        lse_ref[:, here] = top + jnp.log(total)
        o_s[here, :] = jnp.transpose(mixed)
        return carry

    lax.fori_loop(table_ref[2, 1], table_ref[2, 2], query_step, 0)
    for unit in range(units):
        for feat in range(FEATS):
            for core in range(2):
                starts = [place(unit, side, feat, core, rows) for side in range(2)]
                sides = [o_s[start : start + rows, :] for start in starts]
                out_ref[(unit * FEATS + feat) * 2 + core] = jnp.concatenate(sides, axis=1).astype(bf16)


def attend_back_kernel(
    table_ref, slope_ref, qkv_ref, dout_ref, ot_ref, lse_ref, seg_ref, code_ref, dqkv_ref,
    nat_s, qz_s, kt_s, do_s, dz_s, code_s, delta_s, dqt_s, dq_s, dk_s, dv_s,
):
    slope = slope_ref[0, 0]
    feat_self = table_ref[2, 0]
    first, last = table_ref[2, 1], table_ref[2, 2]
    slots, rows = qkv_ref.shape[0], dout_ref.shape[1]
    group = 2 * FEATS * rows
    length = nat_s.shape[0]
    blocks = length // BLOCK
    unpack_qkv(qkv_ref, nat_s, feat_self, rows)
    spread_codes(code_ref, code_s)
    for unit in range(slots // 2):
        for feat in range(FEATS):
            for core in range(2):
                piece = dout_ref[(unit * FEATS + feat) * 2 + core]
                for side in range(2):
                    start = place(unit, side, feat, core, rows)
                    do_s[start : start + rows, :] = piece[:, side * HEAD_DIM : (side + 1) * HEAD_DIM]
    zero_half = jnp.zeros((HEAD_DIM, length), bf16)
    qz_s[:HEAD_DIM, :] = zero_half
    dz_s[HEAD_DIM:, :] = zero_half
    dqt_s[...] = jnp.zeros_like(dqt_s)
    for start in range(0, length, 128):
        here = slice(start, start + 128)
        qk_turned = turn(nat_s[here, :128])
        qz_s[HEAD_DIM:, here] = (qk_turned[:HEAD_DIM] * (HEAD_DIM**-0.5)).astype(bf16)
        kt_s[:, here] = qk_turned[HEAD_DIM:].astype(bf16)
        do_turned = turn(do_s[here, :])
        dz_s[:HEAD_DIM, here] = do_turned.astype(bf16)
        delta_s[:, here] = jnp.sum(do_turned * ot_ref[:, here], axis=0, keepdims=True)

    def key_step(j, carry):
        there = span(j)
        qk_part, vx_part = nat_s[there, :128], nat_s[there, 128:]
        code_part, kt_part = code_s[there, :], kt_s[:, there]
        low, pairs = even_range(table_ref[0, j], table_ref[1, j], first, last)

        def query_step(pair, state):
            dk, dv = state
            for i in (low + 2 * pair, low + 2 * pair + 1):
                here = span(i)
                scores = score_tile_plain(
                    qk_part, qz_s[:, here], code_part, seg_ref[:, here],
                    ((i - j) * BLOCK).astype(f32), slope,
                )
                probs = jnp.exp(scores - lse_ref[:, here])
                back_probs = dot(vx_part, dz_s[:, here])
                back_scores = (probs * (back_probs - delta_s[:, here])).astype(bf16)
                dv = dv + dot(probs.astype(bf16), do_s[here, :])
                dk = dk + dot(back_scores, nat_s[here, :HEAD_DIM])
                dqt_s[:, here] += dot(kt_part, back_scores)
            return dk, dv

        zero = jnp.zeros((BLOCK, HEAD_DIM), f32)
        dk, dv = lax.fori_loop(0, pairs, query_step, (zero, zero))
        dk_s[there, :] = dk
        dv_s[there, :] = dv
        return carry

    lax.fori_loop(0, blocks, key_step, 0)
    for start in range(0, length, 128):
        here = slice(start, start + 128)
        dq_s[here, :] = jnp.transpose(dqt_s[:, here])
    for slot in range(slots):
        for k in range(FEATS):
            for side in range(2):
                here = pl.ds(
                    pl.multiple_of(place(slot // 2, side, feat_self ^ k, slot % 2, rows), rows), rows
                )
                start = (2 * k + side) * rows
                both = jnp.concatenate([dq_s[here, :], dk_s[here, :]], axis=1) * (HEAD_DIM**-0.5)
                dqkv_ref[slot, start : start + rows, :] = both.astype(bf16)
                start = group + (2 * (k % 2) + side) * rows
                lanes = slice((k // 2) * HEAD_DIM, (k // 2 + 1) * HEAD_DIM)
                dqkv_ref[slot, start : start + rows, lanes] = dv_s[here, :].astype(bf16)


def attend(table, slope, qkv, seg_row, code_row):
    slots, length = qkv.shape[0], seg_row.shape[1]
    rows = length // (slots * FEATS * 2)
    vmem = pl.BlockSpec(memory_space=pltpu.VMEM)
    smem = pl.BlockSpec(memory_space=pltpu.SMEM)
    return pl.pallas_call(
        attend_kernel,
        out_shape=(
            jax.ShapeDtypeStruct((slots * FEATS, rows, 2 * HEAD_DIM), bf16),
            jax.ShapeDtypeStruct((1, length), f32),
            jax.ShapeDtypeStruct((HEAD_DIM, length), f32),
        ),
        in_specs=[smem, smem, vmem, vmem, vmem],
        out_specs=(vmem, vmem, vmem),
        scratch_shapes=[
            pltpu.VMEM((length, PACK), bf16),
            pltpu.VMEM((2 * HEAD_DIM, length), bf16),
            pltpu.VMEM((HEAD_DIM, length), bf16),
            pltpu.VMEM((length, HEAD_DIM), f32),
            pltpu.VMEM((length, 128), f32),
        ],
        name="attend",
    )(table, slope, qkv, seg_row, code_row)


def attend_back(table, slope, qkv, dout, o_turned, lse, seg_row, code_row):
    slots, length = qkv.shape[0], seg_row.shape[1]
    rows = length // (slots * FEATS * 2)
    vmem = pl.BlockSpec(memory_space=pltpu.VMEM)
    smem = pl.BlockSpec(memory_space=pltpu.SMEM)
    return pl.pallas_call(
        attend_back_kernel,
        out_shape=jax.ShapeDtypeStruct(qkv.shape, bf16),
        in_specs=[smem, smem] + [vmem] * 6,
        out_specs=vmem,
        scratch_shapes=[
            pltpu.VMEM((length, PACK), bf16),
            pltpu.VMEM((2 * HEAD_DIM, length), bf16),
            pltpu.VMEM((HEAD_DIM, length), bf16),
            pltpu.VMEM((length, HEAD_DIM), bf16),
            pltpu.VMEM((2 * HEAD_DIM, length), bf16),
            pltpu.VMEM((length, 128), f32),
            pltpu.VMEM((1, length), f32),
            pltpu.VMEM((HEAD_DIM, length), f32),
            pltpu.VMEM((length, HEAD_DIM), f32),
            pltpu.VMEM((length, HEAD_DIM), f32),
            pltpu.VMEM((length, HEAD_DIM), f32),
        ],
        name="attend_back",
    )(table, slope, qkv, dout, o_turned, lse, seg_row, code_row)


def norm_forward(values, gain, shift):
    centred = values - jnp.mean(values, axis=-1, keepdims=True)
    inverse = lax.rsqrt(jnp.mean(centred * centred, axis=-1, keepdims=True) + norm_epsilon)
    normed = centred * inverse
    return normed * gain + shift, normed, inverse


def norm_backward(upstream, normed, inverse, gain):
    scaled = upstream * gain
    adjusted = (
        scaled
        - jnp.mean(scaled, axis=-1, keepdims=True)
        - normed * jnp.mean(scaled * normed, axis=-1, keepdims=True)
    )
    sums = [jnp.sum(upstream * normed, axis=0, keepdims=True), jnp.sum(upstream, axis=0, keepdims=True)]
    return adjusted * inverse, sums[0], sums[1]


def call(kernel, shapes, name, where, scratch=(), aliases={}):
    spaces = {"s": pltpu.SMEM, "v": pltpu.VMEM}
    return pl.pallas_call(
        kernel,
        out_shape=shapes,
        in_specs=[pl.BlockSpec(memory_space=spaces[key]) for key in where],
        out_specs=tuple(pl.BlockSpec(memory_space=pltpu.VMEM) for _ in shapes),
        scratch_shapes=list(scratch),
        input_output_aliases=aliases,
        name=name,
    )


def pack_kernel(query_ref, key_ref, value_ref, *refs, heads):
    vector_refs, (seg_ref, live_ref, out_ref, vec_s) = refs[:-4], refs[-4:]
    w_rows = query_ref.shape[0]
    sequences, rows = seg_ref.shape
    vec_s[...] = jnp.zeros_like(vec_s)
    for index, ref in enumerate(vector_refs):
        vec_s[index : index + 1, :w_rows] = ref[...].astype(f32)
    columns = jnp.transpose(vec_s[...])[:w_rows, :HEAD_DIM]
    seg = seg_ref[...]
    codes = jnp.where(live_ref[...] == 1, seg, -1)
    lines = jnp.concatenate([seg.astype(f32), codes.astype(f32)], axis=0)
    lines = jnp.concatenate([lines, jnp.zeros((w_rows - 2 * sequences, rows), f32)], axis=0)
    if rows < HEAD_DIM:
        lines = jnp.concatenate([lines, jnp.zeros((w_rows, HEAD_DIM - rows), f32)], axis=1)
    half = heads * 2 * HEAD_DIM
    for feat in range(FEATS):
        pair, single = [], []
        for h in range(heads):
            lanes = slice((feat * heads + h) * HEAD_DIM, (feat * heads + h + 1) * HEAD_DIM)
            pair += [query_ref[:, lanes].astype(f32), key_ref[:, lanes].astype(f32)]
            single.append(value_ref[:, lanes].astype(f32))
        single += [lines, columns, jnp.zeros((w_rows, HEAD_DIM), f32)]
        for core, pieces in ((0, pair), (1, single)):
            wide = jnp.concatenate(pieces, axis=1).astype(bf16)
            out_ref[feat, core] = wide


def pack_late_kernel(place_ref, w_ref, gate_ref, up_ref, kept_ref, sent_ref, *, slots):
    half = w_ref.shape[1] // 2
    cols = gate_ref.shape[1] // (FEATS * slots)

    def write(core, source_ref, target_ref):
        for feat in range(FEATS):
            pieces = [w_ref[:, core * half : (core + 1) * half]]
            for slot in range(slots):
                start = (slot * FEATS + feat) * cols
                pieces.append(source_ref[:, start : start + cols])
            target_ref[feat] = jnp.concatenate([p.astype(f32) for p in pieces], axis=1).astype(bf16)

    @pl.when(place_ref[0] == 0)
    def _():
        write(0, gate_ref, kept_ref)
        write(1, up_ref, sent_ref)

    @pl.when(place_ref[0] == 1)
    def _():
        write(0, gate_ref, sent_ref)
        write(1, up_ref, kept_ref)


def route_kernel(place_ref, kept_ref, got_ref, *out_refs):
    rows = kept_ref.shape[1]
    first, second = pl.ds(0, rows), pl.ds(rows, rows)
    for k in range(FEATS):
        target = place_ref[2] ^ k
        kept, got = kept_ref[target].astype(f32), got_ref[target].astype(f32)
        first_core = place_ref[0] == 0
        both = [jnp.where(first_core, kept, got), jnp.where(first_core, got, kept)]
        out_refs[k][...] = jnp.concatenate(both, axis=0).astype(bf16)


def piece_row(place_ref, index, piece_rows):
    member = (place_ref[3] ^ (index // 2)) * 2 + (place_ref[1] ^ (index % 2))
    return pl.multiple_of(member * piece_rows, 16)


def qkv_kernel(place_ref, *refs, w_rows, rows, heads, pieces):
    mine_refs, other_refs = refs[:pieces], refs[pieces : 2 * pieces]
    token_refs = refs[2 * pieces : 2 * pieces + FEATS]
    sent_ref, w_ref, params_ref, seg_ref, code_ref, wide_s, vec_s = refs[2 * pieces + FEATS :]
    first_core = place_ref[0] == 0
    side, feat = place_ref[1], place_ref[2]
    piece_rows, half = mine_refs[0].shape
    for index in range(pieces):
        here = pl.ds(piece_row(place_ref, index, piece_rows), piece_rows)
        mine, other = mine_refs[index][...], other_refs[index][...]
        w_ref[here, :half] = jnp.where(first_core, mine, other)
        w_ref[here, half:] = jnp.where(first_core, other, mine)
    vec_s[...] = w_ref[:, 2 * half - 128 :].astype(f32)
    wide_s[...] = w_ref[:, 2 * half - 256 : 2 * half - 128].astype(f32)
    head_width = heads * HEAD_DIM
    own = vec_s[pl.ds(pl.multiple_of(feat * head_width, HEAD_DIM), head_width), :]
    own = jnp.concatenate([own, jnp.zeros((256 - head_width, 128), f32)], axis=0)
    own = jnp.concatenate([jnp.transpose(own[:128]), jnp.transpose(own[128:])], axis=1)
    local = token_refs[0].shape[0]
    group = FEATS * local
    rest = jnp.zeros((1, half - head_width), f32)
    value_bias = jnp.concatenate([own[1:2, :head_width], rest], axis=1)
    for k in range(FEATS):
        tokens = token_refs[k][...]
        values = (dot(tokens, w_ref[:, half:]) + value_bias).astype(bf16)
        pairs = dot(tokens, w_ref[:, :half])
        for h in range(heads):
            bias = own[0:1, h * HEAD_DIM : (h + 1) * HEAD_DIM]
            bias = jnp.concatenate([bias, jnp.zeros((1, HEAD_DIM), f32)], axis=1)
            made = (pairs[:, 2 * h * HEAD_DIM : 2 * (h + 1) * HEAD_DIM] + bias).astype(bf16)
            value = values[:, h * HEAD_DIM : (h + 1) * HEAD_DIM]
            start = group + (k % 2) * local
            lanes = slice((k // 2) * HEAD_DIM, (k // 2 + 1) * HEAD_DIM)
            for slot in range(pieces):
                if min(slot % SLOTS, heads - 1) == h:
                    sent_ref[slot, k * local : (k + 1) * local, :] = made
                    sent_ref[slot, start : start + local, lanes] = value
    for start in range(0, w_ref.shape[0], 128):
        turned = jnp.transpose(vec_s[start : start + 128, :])
        params_ref[:, start : start + 128] = turned[:8]
    devices = w_ref.shape[0] // w_rows
    for ref, row in ((seg_ref, 0), (code_ref, 2)):
        for device in range(0, devices, 2):
            lines = []
            for start in (device * w_rows + row, (device + 1) * w_rows + row):
                pair = wide_s[start : start + 2, HEAD_DIM : HEAD_DIM + rows]
                lines.append(jnp.where(side == 0, pair[:1], pair[1:]))
            ref[:, device * rows : (device + 2) * rows] = jnp.concatenate(lines, axis=1)


def split_rows(first_core, values, kept_ref, sent_ref, lanes, rows):
    def write(first, second):
        for block in range(values.shape[0] // (2 * rows)):
            start = 2 * rows * block
            first[block, :, lanes] = values[start : start + rows].astype(bf16)
            second[block, :, lanes] = values[start + rows : start + 2 * rows].astype(bf16)

    @pl.when(first_core)
    def _():
        write(kept_ref, sent_ref)

    @pl.when(jnp.logical_not(first_core))
    def _():
        write(sent_ref, kept_ref)


def grad_qkv_kernel(place_ref, *refs, heads, w_rows):
    token_refs = refs[:FEATS]
    dqkv_ref, sums_ref, w_ref, back_ref, input_ref, kept_ref, sent_ref, wide_s, vec_s = refs[FEATS:]
    first_core = place_ref[0] == 0
    head_width = heads * HEAD_DIM
    half = 2 * head_width
    group = back_ref.shape[0]
    quarter = group // 2
    back_ref[:, half + head_width :] = jnp.zeros((group, half - head_width), bf16)
    for h in range(heads):
        back_ref[:, 2 * h * HEAD_DIM : 2 * (h + 1) * HEAD_DIM] = dqkv_ref[h, :group, :]
        lanes = slice(half + h * HEAD_DIM, half + (h + 1) * HEAD_DIM)
        back_ref[:quarter, lanes] = dqkv_ref[h, group:, :HEAD_DIM]
        back_ref[quarter:, lanes] = dqkv_ref[h, group:, HEAD_DIM:]
    width = wide_s.shape[1]
    wide_s[...] = jnp.zeros_like(wide_s)
    wide_s[2 : 2 + sums_ref.shape[0], :] = sums_ref[...]
    for start in range(0, width, 128):
        vec_s[start : start + 128, :] = jnp.transpose(wide_s[:, start : start + 128])
    tokens = jnp.concatenate([ref[...] for ref in token_refs], axis=0)
    back = back_ref[...]
    sums = jnp.sum(back.astype(f32), axis=0, keepdims=True)
    queries = [sums[:, 2 * h * HEAD_DIM : (2 * h + 1) * HEAD_DIM] for h in range(heads)]
    none = jnp.zeros((1, 256 - head_width), f32)
    own = jnp.concatenate(
        [
            jnp.concatenate(queries + [none], axis=1),
            sums[:, half : half + 256],
            jnp.zeros((126, 256), f32),
        ],
        axis=0,
    )
    own = jnp.concatenate([jnp.transpose(own[:, :128]), jnp.transpose(own[:, 128:])], axis=0)
    here = pl.ds(pl.multiple_of(place_ref[2] * head_width, HEAD_DIM), head_width)
    vec_s[here, :] += own[:head_width]
    grad = dot(tokens, back, 0, 0)
    grad = jnp.concatenate([grad[:, : 2 * half - 128], grad[:, 2 * half - 128 :] + vec_s[...]], axis=1)
    split_rows(first_core, grad, kept_ref, sent_ref, slice(None), w_rows)
    input_ref[...] = dot(back, w_ref[...], 1, 1).astype(bf16)


def place_first_kernel(place_ref, *refs, pieces, down_rows):
    mine_refs, other_refs = refs[:pieces], refs[pieces : 2 * pieces]
    out_ref, down_ref = refs[2 * pieces :]
    out_rows, half = mine_refs[0].shape
    out_rows = out_rows - 2 * down_rows
    feat_rows = out_rows // FEATS

    def fill(cores):
        for index in range(pieces):
            for core in range(2):
                ref = cores[core][index]
                columns = slice(core * half, (core + 1) * half)
                for k in range(FEATS):
                    start = piece_row(place_ref, index, out_rows) + (place_ref[2] ^ k) * feat_rows
                    here = pl.ds(pl.multiple_of(start, 4), feat_rows)
                    out_ref[here, columns] = ref[k * feat_rows : (k + 1) * feat_rows, :]
                start = piece_row(place_ref, index, 2 * down_rows) + core * down_rows
                here = pl.ds(pl.multiple_of(start, 8), down_rows)
                down_ref[here, :half] = ref[out_rows : out_rows + down_rows, :]
                down_ref[here, half:] = ref[out_rows + down_rows :, :]

    @pl.when(place_ref[0] == 0)
    def _():
        fill((mine_refs, other_refs))

    @pl.when(place_ref[0] == 1)
    def _():
        fill((other_refs, mine_refs))


def place_second_kernel(place_ref, *refs, indices):
    pieces = len(indices)
    mine_refs, other_refs = refs[:pieces], refs[pieces : 2 * pieces]
    gate_ref, up_ref = refs[-2:]
    rows = mine_refs[0].shape[0]
    feat_rows = rows // FEATS

    def fill(gate_refs, up_refs):
        for position, index in enumerate(indices):
            for k in range(FEATS):
                start = piece_row(place_ref, index, rows) + (place_ref[2] ^ k) * feat_rows
                here = pl.ds(pl.multiple_of(start, 4), feat_rows)
                source = slice(k * feat_rows, (k + 1) * feat_rows)
                gate_ref[here, :] = gate_refs[position][source, :]
                up_ref[here, :] = up_refs[position][source, :]

    @pl.when(place_ref[0] == 0)
    def _():
        fill(mine_refs, other_refs)

    @pl.when(place_ref[0] == 1)
    def _():
        fill(other_refs, mine_refs)


def join_kernel(
    heads_ref, tokens_ref, w_ref, params_ref,
    attended_ref, norm_ref, low_ref, normed_ref, inverse_ref, *, heads,
):
    sides = []
    for side in range(2):
        lanes = slice(side * HEAD_DIM, (side + 1) * HEAD_DIM)
        pieces = [
            heads_ref[((h // 2) * FEATS + feat) * 2 + h % 2][:, lanes]
            for feat in range(FEATS)
            for h in range(heads)
        ]
        sides.append(jnp.concatenate(pieces, axis=1))
    attended = jnp.concatenate(sides, axis=0)
    attended_ref[...] = attended
    branch = dot(attended, w_ref[...])
    first, normed, inverse = norm_forward(
        tokens_ref[...].astype(f32) + branch + params_ref[2:3, :],
        params_ref[3:4, :],
        params_ref[4:5, :],
    )
    norm_ref[...] = first
    low_ref[...] = first.astype(bf16)
    normed_ref[...] = normed
    inverse_ref[...] = inverse


def part_kernel(
    place_ref, second_ref, own_ref, got_a_ref, got_b_ref, got_c_ref, normed_ref, inverse_ref,
    params_ref, w_ref, attended_ref,
    inner_ref, dout_ref, kept_ref, sent_ref, sums_ref, *, heads, rows,
):
    back_first = second_ref[...] + own_ref[...].astype(f32) + got_a_ref[...].astype(f32)
    back_first = back_first + got_b_ref[...].astype(f32) + got_c_ref[...].astype(f32)
    inner, gain_sum, shift_sum = norm_backward(
        back_first, normed_ref[...], inverse_ref[...], params_ref[3:4, :]
    )
    inner_ref[...] = inner
    branch = inner.astype(bf16)
    sums_ref[...] = jnp.concatenate(
        [jnp.sum(branch.astype(f32), axis=0, keepdims=True), gain_sum, shift_sum], axis=0
    )
    back = dot(branch, w_ref[...], 1, 1).astype(bf16)
    for slot in range(SLOTS):
        for feat in range(FEATS):
            start = (feat * heads + min(slot, heads - 1)) * HEAD_DIM
            piece = back[:, start : start + HEAD_DIM]
            dout_ref[((slot // 2) * FEATS + feat) * 2 + slot % 2] = jnp.concatenate(
                [piece[:rows], piece[rows:]], axis=1
            )
    half = branch.shape[1] // 2
    grad = dot(attended_ref[...], branch, 0, 0).astype(bf16)
    first_core = place_ref[0] == 0
    kept_ref[...] = jnp.where(first_core, grad[:, :half], grad[:, half:])
    sent_ref[...] = jnp.where(first_core, grad[:, half:], grad[:, :half])


def finish_kernel(parts_ref, query_ref, key_ref, value_ref, *refs, heads):
    vector_refs, vec_s = refs[:-1], refs[-1]
    groups = parts_ref.shape[0] // FEATS
    vec_s[...] = jnp.zeros_like(vec_s)
    w_rows = parts_ref.shape[1]
    half = heads * 2 * HEAD_DIM
    head_width = heads * HEAD_DIM
    vectors = jnp.zeros((w_rows, 128), f32)
    for feat in range(FEATS):
        total = parts_ref[feat].astype(f32)
        for group in range(1, groups):
            total = total + parts_ref[group * FEATS + feat].astype(f32)
        lanes = slice(feat * head_width, (feat + 1) * head_width)
        for index, ref in enumerate((query_ref, key_ref)):
            starts = [(2 * h + index) * HEAD_DIM for h in range(heads)]
            ref[:, lanes] = jnp.concatenate([total[:, at : at + HEAD_DIM] for at in starts], axis=1)
        value_ref[:, lanes] = total[:, half : half + head_width]
        vectors = vectors + total[:, 2 * half - 128 :]
    vec_s[:w_rows, :] = vectors
    turned = jnp.transpose(vec_s[...])
    for index, ref in enumerate(vector_refs):
        ref[...] = turned[index : index + 1, :w_rows]


def fold_kernel(
    place_ref, ff_kept_ref, ff_got_ref, down_kept_ref, down_got_ref, out_kept_ref, out_got_ref, *refs,
    units,
):
    ff_refs, down_refs, out_refs = refs[:2], refs[2 : 2 + units], refs[2 + units :]
    rows = ff_kept_ref.shape[0] // (2 * units)
    for k, ref in enumerate(ff_refs):
        for unit in range(units):
            start = (unit * 2 + (place_ref[1] ^ k)) * rows
            here = pl.ds(pl.multiple_of(start, 16), rows)
            value = ff_kept_ref[here, :].astype(f32) + ff_got_ref[here, :].astype(f32)
            ref[unit] = value.astype(bf16)
    for kept_ref, got_ref, moved_refs in (
        (down_kept_ref, down_got_ref, down_refs),
        (out_kept_ref, out_got_ref, out_refs),
    ):
        rows = kept_ref.shape[0] // units
        for k, ref in enumerate(moved_refs):
            here = pl.ds(pl.multiple_of((place_ref[3] ^ k) * rows, 16), rows)
            value = kept_ref[here, :].astype(f32) + got_ref[here, :].astype(f32)
            ref[...] = value.astype(bf16)


def finish_late_kernel(place_ref, *refs, ff_part):
    part_refs, (kept_ref, sent_ref) = refs[:FEATS], refs[FEATS:]
    w_rows = kept_ref.shape[0]
    total = part_refs[0][:, ff_part:].astype(f32)
    for part in part_refs[1:]:
        total = total + part[:, ff_part:].astype(f32)
    for core in range(2):

        @pl.when(place_ref[0] == core)
        def _():
            for ref, rows in (
                (kept_ref, slice(core * w_rows, (core + 1) * w_rows)),
                (sent_ref, slice((1 - core) * w_rows, (2 - core) * w_rows)),
            ):
                ref[:, FEATS * ff_part :] = total[rows].astype(bf16)
                for k in range(FEATS):
                    lanes = pl.ds(pl.multiple_of((place_ref[2] ^ k) * ff_part, 128), ff_part)
                    ref[:, lanes] = part_refs[k][rows, :ff_part]


def finish_wide_kernel(
    place_ref, kept_ref, got_ref, down_kept_ref, down_got_ref,
    gate_ref, up_ref, out_ref, down_ref, *, slots,
):
    total = gate_ref.shape[1]
    cols = total // (FEATS * slots)
    half = out_ref.shape[1] // 2

    def write(first, second, down_first, down_second):
        for source, target in ((first, gate_ref), (second, up_ref)):
            for slot in range(slots):
                pieces = []
                for feat in range(FEATS):
                    start = (feat * slots + slot) * cols
                    pieces.append(source[:, start : start + cols].astype(f32))
                start = slot * FEATS * cols
                target[:, start : start + FEATS * cols] = jnp.concatenate(pieces, axis=1)
        out_ref[:, :half] = first[:, total:].astype(f32)
        out_ref[:, half:] = second[:, total:].astype(f32)
        down_ref[:, :half] = down_first[...].astype(f32)
        down_ref[:, half:] = down_second[...].astype(f32)

    @pl.when(place_ref[0] == 0)
    def _():
        write(kept_ref, got_ref, down_kept_ref, down_got_ref)

    @pl.when(place_ref[0] == 1)
    def _():
        write(got_ref, kept_ref, down_got_ref, down_kept_ref)


def after(values, *others):
    return lax.optimization_barrier((values,) + others)[0]


def tie(*values):
    return lax.optimization_barrier(values)


def on_device(
    layer_input, segment_ids, token_live, w_query, b_query, w_key, w_value, b_value,
    w_output, b_output, first_gain, first_shift, w_gate, w_up, w_down, b_down,
    second_gain, second_shift, output_grad,
):
    units = lax.axis_size("u")
    unit, side, feat, core = (lax.axis_index(name) for name in ("u", "s", "f", "c"))
    devices = units * 2 * FEATS * 2
    sequences, rows, width = layer_input.shape
    length = rows * devices
    w_rows = w_query.shape[0]
    down_rows, ff_part = w_down.shape[0], w_gate.shape[1] // FEATS
    slots = units * 2
    heads = HEADS // FEATS
    head_width = heads * HEAD_DIM
    ranges = slots // SLOTS
    local = 2 * rows
    group = FEATS * local
    here = jnp.stack([core, side, feat, unit]).astype(jnp.int32)
    parts = slots

    def exchange_sides(values):
        kept = jnp.where(side == 0, values[0], values[1])
        got = swap(jnp.where(side == 0, values[1], values[0]), "s")
        return kept, got

    def to_tokens(values):
        kept, got = exchange_sides(values)
        return jnp.concatenate(
            [jnp.where(side == 0, kept, got), jnp.where(side == 0, got, kept)], axis=0
        )

    def from_tokens(values):
        kept, got = exchange_sides(values.reshape(2, rows, width))
        return jnp.stack([jnp.where(side == 0, kept, got), jnp.where(side == 0, got, kept)])

    def to_group(blocks):
        return all_to_all(blocks.reshape(-1, blocks.shape[-1]), ("f", "c"))

    def from_units(own, other_side, pin=None):
        pieces = [own, other_side]
        for k in range(1, units):
            for piece in (own, other_side):
                pieces.append(swap(piece if pin is None else after(piece, pin), "u", k))
        return pieces

    tokens = to_tokens(layer_input)

    vectors = [
        values.reshape(1, w_rows)
        for values in (
            b_query, b_value, b_output, first_gain, first_shift, b_down, second_gain, second_shift
        )
    ]
    half = heads * 2 * HEAD_DIM
    (early,) = call(
        functools.partial(pack_kernel, heads=heads),
        (jax.ShapeDtypeStruct((FEATS, 2, w_rows, half), bf16),),
        "pack_attn",
        "v" * 13,
        [pltpu.VMEM((128, 128), f32)],
    )(w_query, w_key, w_value, *vectors, segment_ids, token_live)
    token_parts = gather_feats(tokens)
    early_own = all_to_all(early.reshape(-1, half), ("f", "c"))
    others = range(1, units)
    early_side = swap(early_own, "s")
    early_near = [swap(early_own, "u", k) for k in others]
    early_far = [swap(early_side, "u", k) for k in others]

    def by_distance(own, other_side, near, far):
        pieces = [own, other_side]
        for index in range(units - 1):
            pieces += [near[index], far[index]]
        return pieces

    early_pieces = by_distance(early_own, early_side, early_near, early_far)
    early_others = [swap(piece, "c") for piece in early_pieces]

    late_cols = width // 2 + ff_part
    late_shape = jax.ShapeDtypeStruct((FEATS, w_rows, late_cols), bf16)
    late_kept, late_sent = call(
        functools.partial(pack_late_kernel, slots=slots), (late_shape, late_shape), "pack_late", "svvv"
    )(here, w_output, w_gate, w_up)
    routed = call(
        route_kernel,
        (jax.ShapeDtypeStruct((2 * w_rows, late_cols), bf16),) * FEATS,
        "route_late",
        "svv",
    )(here, late_kept, swap(after(late_sent, early_own), "c"))
    out_half = width // 2
    routed = [after(piece, token_parts[1]) for piece in routed]
    late_feats = [routed[0]] + [swap(routed[k], "f", k) for k in range(1, FEATS)]
    here_qkv, *late_feats = tie(here, *late_feats)
    first_own = jnp.concatenate(
        [piece[:, :out_half] for piece in late_feats] + [w_down[:, :out_half], w_down[:, out_half:]]
    )
    second_own = jnp.concatenate([piece[:, out_half:] for piece in late_feats])
    others = range(1, units)

    sent, w_attn, params, seg_row, code_row = call(
        functools.partial(qkv_kernel, w_rows=w_rows, rows=rows, heads=heads, pieces=parts),
        (
            jax.ShapeDtypeStruct((slots, group * 3 // 2, 2 * HEAD_DIM), bf16),
            jax.ShapeDtypeStruct((width, 2 * half), bf16),
            jax.ShapeDtypeStruct((8, width), f32),
            jax.ShapeDtypeStruct((1, length), f32),
            jax.ShapeDtypeStruct((1, length), f32),
        ),
        "qkv",
        "s" + "v" * (2 * parts + FEATS),
        [pltpu.VMEM((width, 128), f32)] * 2,
    )(here_qkv, *early_pieces, *early_others, *token_parts)
    qkv = all_to_all(sent.reshape(-1, 2 * HEAD_DIM), ("u", "c"))
    first_side = swap(first_own, "s")
    first_units = [swap(first_own, "u", k) for k in others]
    first_swaps = [swap(piece, "c") for piece in [first_own, first_side] + first_units]
    second_swaps = [swap(second_own, "c")]
    qkv, first_side, second_swaps[0], *moved = tie(
        qkv, first_side, second_swaps[0], *first_units, *first_swaps
    )
    first_units, first_swaps = moved[: units - 1], moved[units - 1 :]
    qkv = qkv.reshape(sent.shape)

    blocks = length // BLOCK
    slot_self = unit * 2 + core
    range_self = slot_self // SLOTS
    head_self = feat * heads + jnp.minimum(slot_self % SLOTS, heads - 1)
    slope = jnp.asarray(alibi_slopes(HEADS))[head_self].reshape(1, 1)
    seg_blocks = seg_row.reshape(blocks, BLOCK)
    seg_low, seg_high = seg_blocks[:, 0], seg_blocks[:, -1]
    key_low = jnp.sum(seg_high[None, :] < seg_low[:, None], axis=1, dtype=jnp.int32)
    key_high = jnp.sum(seg_low[None, :] <= seg_high[:, None], axis=1, dtype=jnp.int32)
    own = jnp.stack(
        [feat, range_self * (blocks // ranges), (range_self + 1) * (blocks // ranges)]
    ).astype(jnp.int32)
    table = jnp.stack([key_low, key_high, jnp.pad(own, (0, blocks - 3))])
    second_side = swap(second_own, "s")
    second_units = [swap(second_own, "u", k) for k in others]
    first_far = [swap(first_side, "u", k) for k in others]
    out_blocks, lse, o_turned = attend(table, slope, qkv, seg_row, code_row)
    out_blocks, second_side, *moved = tie(out_blocks, second_side, *second_units, *first_far)
    second_units, first_far = moved[: units - 1], moved[units - 1 :]
    second_far = [swap(second_side, "u", k) for k in others]
    first_swaps += [swap(piece, "c") for piece in first_far]
    second_swaps += [swap(piece, "c") for piece in [second_side] + second_units]

    first_pieces = by_distance(first_own, first_side, first_units, first_far)
    first_others = by_distance(
        first_swaps[0], first_swaps[1], first_swaps[2 : 1 + units], first_swaps[1 + units :]
    )
    aligned = w_rows % 8 == 0

    def in_rows(pieces, feats):
        cols = pieces[0].shape[1]
        values = jnp.stack(pieces).reshape(units, 2, feats, -1, cols)
        values = jnp.take(values, jnp.arange(units) ^ unit, axis=0)
        values = jnp.take(values, jnp.arange(2) ^ side, axis=1)
        if feats == FEATS:
            values = jnp.take(values, jnp.arange(FEATS) ^ feat, axis=2)
        return values.reshape(-1, cols)

    def by_core(mine, others_):
        mine, others_ = in_rows(mine, FEATS), in_rows(others_, FEATS)
        return jnp.where(core == 0, mine, others_), jnp.where(core == 0, others_, mine)

    if aligned:
        full_output, full_down = call(
            functools.partial(place_first_kernel, pieces=parts, down_rows=down_rows),
            (
                jax.ShapeDtypeStruct((width, width), bf16),
                jax.ShapeDtypeStruct((ff_part, width), bf16),
            ),
            "place_first",
            "s" + "v" * 2 * parts,
        )(here, *first_pieces, *first_others)
    else:
        out_rows = 2 * FEATS * w_rows
        full_output = jnp.concatenate(
            by_core([p[:out_rows] for p in first_pieces], [p[:out_rows] for p in first_others]), axis=1
        )

        def down_of(pieces):
            return in_rows(
                [
                    jnp.concatenate([p[out_rows : out_rows + down_rows], p[out_rows + down_rows :]], axis=1)
                    for p in pieces
                ],
                1,
            ).reshape(slots, down_rows, width)

        down_mine, down_others = down_of(first_pieces), down_of(first_others)
        full_down = jnp.stack(
            [jnp.where(core == 0, down_mine, down_others), jnp.where(core == 0, down_others, down_mine)],
            axis=1,
        ).reshape(ff_part, width)

    heads_in = all_to_all(out_blocks.reshape(-1, 2 * HEAD_DIM), ("u", "f", "c"))
    heads_in, *second_swaps[1:] = tie(heads_in, *second_swaps[1:])
    heads_in = heads_in.reshape(ranges, SLOTS * FEATS, rows, 2 * HEAD_DIM)
    if ranges > 1:
        heads_in = lax.dynamic_index_in_dim(heads_in, unit * 2 // SLOTS, 0, keepdims=False)
    else:
        heads_in = heads_in[0]
    attended, first_norm, first_low_own, normed_one, inverse_one = call(
        functools.partial(join_kernel, heads=heads),
        (
            jax.ShapeDtypeStruct((local, width), bf16),
            jax.ShapeDtypeStruct((local, width), f32),
            jax.ShapeDtypeStruct((local, width), bf16),
            jax.ShapeDtypeStruct((local, width), f32),
            jax.ShapeDtypeStruct((local, 1), f32),
        ),
        "join_heads",
        "vvvv",
    )(heads_in, tokens, full_output, params)

    first_low_own, *second_far = tie(first_low_own, *second_far)
    second_swaps += [swap(piece, "c") for piece in second_far]
    ff_square = jax.ShapeDtypeStruct((width, ff_part), bf16)
    indices = [0, 1] + [2 * k for k in others] + [2 * k + 1 for k in others]
    second_pieces = [second_own, second_side, *second_units, *second_far]
    if aligned:
        full_gate, full_up = call(
            functools.partial(place_second_kernel, indices=indices),
            (ff_square, ff_square),
            "place_second",
            "s" + "v" * 2 * parts,
        )(here, *second_pieces, *second_swaps)
    else:
        order = [indices.index(position) for position in range(parts)]
        full_gate, full_up = by_core(
            [second_pieces[position] for position in order],
            [second_swaps[position] for position in order],
        )
    low_parts = gather_feats(first_low_own)
    full_gate, full_up, *low_parts = tie(full_gate, full_up, *low_parts)
    first_low = jnp.concatenate(low_parts, axis=0)
    gate_rows = dot(first_low, full_gate)
    up_rows = dot(first_low, full_up)
    spread = 0.5 * (1.0 + lax.erf(gate_rows * (0.5**0.5)))
    gelu = gate_rows * spread
    hidden = (gelu * up_rows).astype(bf16)
    partial_mixed = dot(hidden, full_down).astype(bf16).reshape(FEATS, local, width)
    partial_mixed, gate_kept, up_kept = tie(partial_mixed, gate_rows, up_rows)
    mixed_got = [swap(partial_mixed[k], "f", k) for k in range(1, FEATS)]
    spread = 0.5 * (1.0 + lax.erf(gate_kept * (0.5**0.5)))
    density = jnp.exp(-0.5 * gate_kept * gate_kept) * (1.0 / math.sqrt(2.0 * math.pi))
    gate_factor = (up_kept * (spread + gate_kept * density)).astype(bf16)
    up_factor = (gate_kept * spread).astype(bf16)
    bias_down, gate_factor, up_factor = tie(params[5], gate_factor, up_factor)
    mixed = partial_mixed[0].astype(f32) + bias_down
    for piece in mixed_got:
        mixed = mixed + piece.astype(f32)
    gain_two = params[6]
    layer_wide, normed_two, inverse_two = norm_forward(first_norm + mixed, gain_two, params[7])

    upstream = to_tokens(after(output_grad, out_blocks)).astype(f32)
    back_second, grad_gain_two, grad_shift_two = norm_backward(
        upstream, normed_two, inverse_two, gain_two
    )
    back_low = back_second.astype(bf16)
    grad_down_bias = jnp.sum(back_low.astype(f32), axis=0, keepdims=True)
    back_mixed = jnp.concatenate(gather_feats(back_low), axis=0)
    back_hidden = dot(back_mixed, full_down, 1, 1)
    back_gate = (back_hidden * gate_factor.astype(f32)).astype(bf16)
    back_up = (back_hidden * up_factor.astype(f32)).astype(bf16)
    partial_first = (dot(back_gate, full_gate, 1, 1) + dot(back_up, full_up, 1, 1)).astype(bf16)
    partial_first = partial_first.reshape(FEATS, local, width)
    partial_got = [swap(partial_first[k], "f", k) for k in range(1, FEATS)]
    small = swap(partial_first[0, :16, :128], "c")
    small, back_gate, back_up, back_mixed = tie(small, back_gate, back_up, back_mixed)
    half_width = width // 2

    def chosen(first, second):
        return jnp.where(core == 0, first, second)

    left, right = back_mixed[:, :half_width], back_mixed[:, half_width:]

    def outer(rows_side, cols_side):
        return dot(cols_side, rows_side, 0, 0).astype(bf16).T

    ff_sent = outer(first_low, chosen(back_up, back_gate))
    down_sent = outer(hidden, chosen(right, left))
    ff_kept = outer(first_low, chosen(back_gate, back_up))
    down_kept = outer(hidden, chosen(left, right))
    here_join, ff_sent, down_sent, ff_kept, down_kept = tie(here, ff_sent, down_sent, ff_kept, down_kept)
    inner_shape = jax.ShapeDtypeStruct((local, width), f32)
    back_inner, dout_blocks, out_kept, out_sent, sums_one = call(
        functools.partial(part_kernel, heads=heads, rows=rows),
        (
            inner_shape,
            jax.ShapeDtypeStruct((SLOTS * FEATS, rows, 2 * HEAD_DIM), bf16),
            jax.ShapeDtypeStruct((width, half_width), bf16),
            jax.ShapeDtypeStruct((width, half_width), bf16),
            jax.ShapeDtypeStruct((3, width), f32),
        ),
        "back_join",
        "s" + "v" * 10,
    )(
        here_join, back_second, partial_first[0], *partial_got, normed_one, inverse_one, params,
        full_output, attended,
    )
    dout_sent = jnp.broadcast_to(dout_blocks[None], (ranges,) + dout_blocks.shape)
    dout = all_to_all(dout_sent.reshape(-1, 2 * HEAD_DIM), ("u", "f", "c"))
    dout = dout.reshape(slots * FEATS, rows, 2 * HEAD_DIM)

    def fold(values, axis):
        return scatter_axis(values, axis).astype(bf16)

    def added(kept, got):
        return (kept.astype(f32) + got.astype(f32)).astype(bf16)

    out_got = swap(out_sent, "c")
    ff_got, down_got = (swap(after(values, *partial_got), "c") for values in (ff_sent, down_sent))

    def parts_of(values, axis):
        size, me = lax.axis_size(axis), lax.axis_index(axis)
        if size == 2:
            return [jnp.where(me == 0, values[0], values[1]), jnp.where(me == 0, values[1], values[0])]
        return [lax.dynamic_index_in_dim(values, me ^ k, 0, keepdims=False) for k in range(size)]

    def send(values, axis):
        own, *rest = parts_of(values, axis)
        return own, [swap(piece, axis, k + 1) for k, piece in enumerate(rest)]

    def total(own, got):
        result = own.astype(f32)
        for piece in got:
            result = result + piece.astype(f32)
        return result

    def sides(values):
        return jnp.moveaxis(values.reshape(units, 2, -1, values.shape[-1]), 1, 0)

    def by_unit(values):
        return values.reshape(units, -1, values.shape[-1])

    def part(values, member):
        return lax.dynamic_index_in_dim(values, member, 0, keepdims=False)

    def send_sum(kept, got, axis):
        me = lax.axis_index(axis)
        moved = [
            swap(added(part(kept, me ^ k), part(got, me ^ k)), axis, k)
            for k in range(1, lax.axis_size(axis))
        ]
        return [part(kept, me), part(got, me)], moved

    ff_own, ff_moved = send_sum(sides(ff_kept), sides(ff_got), "s")
    down_own, down_moved = send_sum(by_unit(down_kept), by_unit(down_got), "u")
    out_own, out_moved = send_sum(by_unit(out_kept), by_unit(out_got), "u")
    dqkv = attend_back(table, slope, qkv, dout, o_turned, lse, seg_row, code_row)
    dqkv, *moved = tie(dqkv, *ff_moved, *down_moved, *out_moved)
    ff_moved, down_moved, out_moved = moved[:1], moved[1:units], moved[units:]
    grad_down = total(down_own[0], down_own[1:] + down_moved).astype(bf16).reshape(2, 2 * down_rows, -1)
    grad_out = total(out_own[0], out_own[1:] + out_moved).astype(bf16).reshape(2, FEATS * 2 * w_rows, -1)
    grad_down, down_moved = send(grad_down, "s")
    dqkv = all_to_all(dqkv.reshape(-1, 2 * HEAD_DIM), ("u", "c"))
    grad_ff = total(ff_own[0], ff_own[1:] + ff_moved).astype(bf16)
    grad_ff, ff_moved = send(after(grad_ff, dqkv), "u")
    grad_out, out_moved = send(after(grad_out, dqkv), "s")
    dqkv = dqkv.reshape(ranges, SLOTS, group * 3 // 2, 2 * HEAD_DIM)
    if ranges > 1:
        dqkv = jnp.sum(dqkv.astype(f32), axis=0).astype(bf16)
    else:
        dqkv = dqkv[0]
    vector_sums = jnp.concatenate([sums_one, grad_down_bias, grad_gain_two, grad_shift_two], axis=0)
    attn_shape = jax.ShapeDtypeStruct((slots * FEATS, w_rows, 2 * half), bf16)
    ignored, partial_input, attn_kept, attn_sent = call(
        functools.partial(grad_qkv_kernel, heads=heads, w_rows=w_rows),
        (
            jax.ShapeDtypeStruct((group, 2 * half), bf16),
            jax.ShapeDtypeStruct((group, width), bf16),
            attn_shape,
            attn_shape,
        ),
        "grad_qkv",
        "s" + "v" * (FEATS + 3),
        [pltpu.VMEM((128, width), f32), pltpu.VMEM((width, 128), f32)],
    )(here, *token_parts, dqkv, vector_sums, w_attn)
    partial_input = partial_input.reshape(FEATS, local, width)
    grad_attn = added(after(attn_kept, partial_input), swap(attn_sent, "c"))
    grad_attn = grad_attn.reshape(-1, 2 * half)
    grad_down = total(grad_down, down_moved).reshape(2, down_rows, half_width)
    layer_wide_low = after(layer_wide.astype(bf16), grad_attn)
    grad_attn = all_to_all(grad_attn, ("u", "s", "f"))
    input_got = [swap(partial_input[k], "f", k) for k in range(1, FEATS)]
    grad_ff = total(grad_ff, ff_moved)
    grad_out = total(grad_out, out_moved)
    grad_late = jnp.concatenate([grad_ff, grad_out], axis=1).astype(bf16)
    grad_late = grad_late.reshape(FEATS, 2 * w_rows, ff_part + half_width)
    late_got = [lax.dynamic_index_in_dim(grad_late, feat ^ k, 0, keepdims=False) for k in range(FEATS)]
    back_inner, *late_got = tie(back_inner, *late_got)
    late_got = late_got[:1] + [swap(late_got[k], "f", k) for k in range(1, FEATS)]
    input_sum = back_inner + partial_input[0].astype(f32)
    for piece in input_got:
        input_sum = input_sum + piece.astype(f32)
    input_grad = from_tokens(input_sum.astype(bf16))
    layer_output = from_tokens(layer_wide_low)

    wide_shape = jax.ShapeDtypeStruct((w_rows, FEATS * ff_part + half_width), bf16)
    wide_kept, wide_sent = call(
        functools.partial(finish_late_kernel, ff_part=ff_part),
        (wide_shape, wide_shape),
        "finish_late",
        "s" + "v" * FEATS,
    )(here, *late_got)
    wide_got = swap(wide_sent, "c")
    down_kept = chosen(grad_down[0], grad_down[1])
    down_got = swap(chosen(grad_down[1], grad_down[0]).astype(bf16), "c")
    ff_out_shape = jax.ShapeDtypeStruct((w_rows, FEATS * ff_part), f32)
    grad_gate, grad_up, grad_output, grad_down = call(
        functools.partial(finish_wide_kernel, slots=slots),
        (
            ff_out_shape,
            ff_out_shape,
            jax.ShapeDtypeStruct((w_rows, width), f32),
            jax.ShapeDtypeStruct((down_rows, width), f32),
        ),
        "finish_wide",
        "svvvv",
    )(here, wide_kept, wide_got, down_kept, down_got)
    matrix_shape = jax.ShapeDtypeStruct((w_rows, width), f32)
    grad_query, grad_key, grad_value, *vectors_out = call(
        functools.partial(finish_kernel, heads=heads),
        (matrix_shape,) * 3 + (jax.ShapeDtypeStruct((1, w_rows), f32),) * 8,
        "finish",
        "v",
        [pltpu.VMEM((128, 128), f32)],
    )(grad_attn.reshape(slots * FEATS, w_rows, 2 * half))
    vectors_out = [values.reshape(w_rows) for values in vectors_out]
    return (
        layer_output, input_grad, grad_query, vectors_out[0], grad_key, grad_value,
        vectors_out[1], grad_output, vectors_out[2], vectors_out[3], vectors_out[4],
        grad_gate, grad_up, grad_down, vectors_out[5], vectors_out[6], vectors_out[7],
    )


def solution(mesh):
    devices = mesh.devices
    names = ("u", "s", "f", "c")
    inner = Mesh(devices.reshape(devices.size // (4 * FEATS), 2, FEATS, 2), names)
    tokens, matrix, vector = P(None, names, None), P(names, None), P(names)
    ids = P(None, names)
    return jax.shard_map(
        on_device,
        mesh=inner,
        in_specs=(
            tokens, ids, ids, matrix, vector, matrix, matrix, vector, matrix, vector, vector,
            vector, matrix, matrix, matrix, vector, vector, vector, tokens,
        ),
        out_specs=(
            tokens, tokens, matrix, vector, matrix, matrix, vector, matrix, vector, vector,
            vector, matrix, matrix, matrix, vector, vector, vector,
        ),
        check_vma=False,
    )
```
